32 devices in a mesh: lon: 16 (over z, x, core), lat: 2 (over y).
Axes of the slice: x: 2, y: 2, z: 4, core: 2. Of those that a mesh axis runs over, the one named last changes fastest.
Arguments:
- thermal_anomaly_array: float32 [16, 256, 256], P(None, 'lon', 'lat'), may hold values from -6 to 6
- saltiness_anomaly_array: float32 [16, 256, 256], P(None, 'lon', 'lat'), may hold values from -6 to 6
- zonal_volume_passage: float32 [16, 256, 256], P(None, 'lon', 'lat'), may hold values from -0.15 to 0.15
- meridional_volume_passage: float32 [16, 256, 256], P(None, 'lon', 'lat'), may hold values from -0.15 to 0.15
- rising_volume_passage: float32 [15, 256, 256], P(None, 'lon', 'lat'), may hold values from -0.15 to 0.15
- diffusive_coupling_number: float32 [15, 256, 256], P(None, 'lon', 'lat'), may hold values from 0.05 to 2
- sea_column_flag: int32 [256, 256], P('lon', 'lat'), may hold values 0 or 1
- seabed_layer_index: int32 [256, 256], P('lon', 'lat'), may hold values from 1 to 16
Outputs:
- new_temperature: float32 [16, 256, 256], P(None, 'lon', 'lat')
- new_salinity: float32 [16, 256, 256], P(None, 'lon', 'lat')
The draws below stay inside these ranges and needn't reach their ends.
All inputs are finite; a program needn't handle non-finite values. No bound on the sum of `sea_column_flag` on one device may be relied on, other than what follows from the above.
Results may differ from the reference program's by a relative error of at most 0.0003.
Values sent between devices are 32-bit elements; how exact they have to be, the bound alone decides.
No kernel may reach another device: no remote copies, remote signals or barrier semaphores. Data moves between devices by JAX's collectives and lax.ppermute only.
A program may use at most 64 MiB of HBM per device.

```python
import math
import jax
import jax.numpy as jnp
from jax import lax

LAYER_TOTAL = 16
MERIDIAN_TOTAL = 256
PARALLEL_TOTAL = 256


def with_ends(entries, rng, smallest, top_value):
    shape = entries.shape
    index_at = [jax.random.randint(jax.random.fold_in(rng, axis), (), 0, shape[axis]) for axis in range(len(shape))]
    entries = entries.at[tuple(index_at)].set(smallest)
    longest = shape.index(max(shape))
    index_at[longest] = (index_at[longest] + 1) % shape[longest]
    return entries.at[tuple(index_at)].set(top_value)


def steps_of(stream_key, extent, pieces, least, top_value):
    level, own = 1.0, jax.random.fold_in(stream_key, 6)
    for dim, parts in pieces:
        steps = jnp.exp(jax.random.uniform(jax.random.fold_in(own, dim), (parts,), jnp.float32, least / len(pieces), top_value / len(pieces)))
        level = level * jnp.repeat(steps, extent[dim] // parts).reshape([-1 if axis == dim else 1 for axis in range(len(extent))])
    return level


def normal_values(own_key, shape, width, limit, split=(), kind=jnp.bfloat16):
    result = jax.random.normal(own_key, shape, jnp.float32) * width
    if len(split) > 0:
        result = steps_of(own_key, shape, split, -0.22, 0.18) * result
    return jnp.clip(result, min=-limit, max=limit).astype(kind)


def setup_inputs(seed: int = 0) -> dict:
    seeds = jax.random.split(jax.random.key(seed), 9)
    thermal_anomaly_array = normal_values(seeds[0], (LAYER_TOTAL, MERIDIAN_TOTAL, PARALLEL_TOTAL), 1.0, 6.0, ((1, 16), (2, 2)), jnp.float32)
    saltiness_anomaly_array = normal_values(seeds[1], (LAYER_TOTAL, MERIDIAN_TOTAL, PARALLEL_TOTAL), 1.0, 6.0, ((1, 16), (2, 2)), jnp.float32)
    zonal_volume_passage = jnp.clip(jax.random.uniform(seeds[2], (LAYER_TOTAL, MERIDIAN_TOTAL, PARALLEL_TOTAL), jnp.float32, -0.15, 0.15) * steps_of(seeds[2], (LAYER_TOTAL, MERIDIAN_TOTAL, PARALLEL_TOTAL), ((1, 16), (2, 2)), -0.4, 0.0), -0.15, 0.15)
    meridional_volume_passage = jnp.clip(jax.random.uniform(seeds[3], (LAYER_TOTAL, MERIDIAN_TOTAL, PARALLEL_TOTAL), jnp.float32, -0.15, 0.15) * steps_of(seeds[3], (LAYER_TOTAL, MERIDIAN_TOTAL, PARALLEL_TOTAL), ((1, 16), (2, 2)), -0.4, 0.0), -0.15, 0.15)
    rising_volume_passage = jnp.clip(jax.random.uniform(seeds[4], (LAYER_TOTAL - 1, MERIDIAN_TOTAL, PARALLEL_TOTAL), jnp.float32, -0.15, 0.15) * steps_of(seeds[4], (LAYER_TOTAL - 1, MERIDIAN_TOTAL, PARALLEL_TOTAL), ((1, 16), (2, 2)), -0.4, 0.0), -0.15, 0.15)
    diffusive_coupling_number = jnp.clip(jnp.exp(math.log(2.0) - 3.6888794 * jax.random.uniform(seeds[5], (LAYER_TOTAL - 1, MERIDIAN_TOTAL, PARALLEL_TOTAL), jnp.float32) ** steps_of(seeds[5], (LAYER_TOTAL - 1, MERIDIAN_TOTAL, PARALLEL_TOTAL), ((1, 16), (2, 2)), -0.2, 0.2)), 0.05, 2.0)
    sea_column_flag = with_ends((jax.random.randint(seeds[6], (MERIDIAN_TOTAL, PARALLEL_TOTAL), 0, 5) < 4).astype(jnp.int32), jax.random.fold_in(seeds[6], 1), 0, 1)
    seabed_layer_index = with_ends(jax.random.randint(seeds[7], (MERIDIAN_TOTAL, PARALLEL_TOTAL), 1, LAYER_TOTAL + 1), jax.random.fold_in(seeds[7], 1), 1, LAYER_TOTAL).astype(jnp.int32)
    return dict(thermal_anomaly_array=thermal_anomaly_array, saltiness_anomaly_array=saltiness_anomaly_array, zonal_volume_passage=zonal_volume_passage, meridional_volume_passage=meridional_volume_passage, rising_volume_passage=rising_volume_passage, diffusive_coupling_number=diffusive_coupling_number, sea_column_flag=sea_column_flag, seabed_layer_index=seabed_layer_index)


flux_floor = 0.01


def face_fluxes(cells, sea_grid_indicator, eastward, northward, upward):
    behind = cells[:, :-1, 1:-1]
    beyond = cells[:, 1:, 1:-1]
    speed = eastward[:, :-1, 1:-1]
    open_face = sea_grid_indicator[:, :-1, 1:-1] * sea_grid_indicator[:, 1:, 1:-1]
    low_east = open_face * (jnp.maximum(speed, 0.0) * behind + jnp.minimum(speed, 0.0) * beyond)
    anti_east = open_face * speed * 0.5 * (behind + beyond) - low_east
    behind = cells[:, 1:-1, :-1]
    beyond = cells[:, 1:-1, 1:]
    speed = northward[:, 1:-1, :-1]
    open_face = sea_grid_indicator[:, 1:-1, :-1] * sea_grid_indicator[:, 1:-1, 1:]
    low_north = open_face * (jnp.maximum(speed, 0.0) * behind + jnp.minimum(speed, 0.0) * beyond)
    anti_north = open_face * speed * 0.5 * (behind + beyond) - low_north
    middle = cells[:, 1:-1, 1:-1]
    middle_wet = sea_grid_indicator[:, 1:-1, 1:-1]
    deeper = middle[1:]
    higher = middle[:-1]
    speed = upward[1:, 1:-1, 1:-1]
    open_face = middle_wet[1:] * middle_wet[:-1]
    low_up = open_face * (jnp.maximum(speed, 0.0) * deeper + jnp.minimum(speed, 0.0) * higher)
    anti_up = open_face * speed * 0.5 * (deeper + higher) - low_up
    border = jnp.zeros_like(low_up[:1])
    low_up = jnp.concatenate([border, low_up, border], axis=0)
    anti_up = jnp.concatenate([border, anti_up, border], axis=0)
    return (low_east, low_north, low_up), (anti_east, anti_north, anti_up)


def divergence(flux_east, flux_north, flux_up):
    return (flux_east[:, 1:] - flux_east[:, :-1] + flux_north[:, :, 1:] - flux_north[:, :, :-1]
            + flux_up[:-1] - flux_up[1:])


def limits(cells, lowered, sea_grid_indicator, anti):
    highs = jnp.maximum(cells, lowered)
    lowest = jnp.minimum(cells, lowered)
    middle_wet = sea_grid_indicator[:, 1:-1, 1:-1]
    self_high = highs[:, 1:-1, 1:-1]
    self_low = lowest[:, 1:-1, 1:-1]
    upper_bound = self_high
    lower_bound = self_low
    windows = ((slice(None), slice(None, -2), slice(1, -1)), (slice(None), slice(2, None), slice(1, -1)),
               (slice(None), slice(1, -1), slice(None, -2)), (slice(None), slice(1, -1), slice(2, None)))
    for window in windows:
        joined = middle_wet * sea_grid_indicator[window] > 0.0
        upper_bound = jnp.maximum(upper_bound, jnp.where(joined, highs[window], self_high))
        lower_bound = jnp.minimum(lower_bound, jnp.where(joined, lowest[window], self_low))
    joined = middle_wet[1:] * middle_wet[:-1] > 0.0
    above_high = jnp.concatenate([self_high[:1], jnp.where(joined, self_high[:-1], self_high[1:])], axis=0)
    below_high = jnp.concatenate([jnp.where(joined, self_high[1:], self_high[:-1]), self_high[-1:]], axis=0)
    above_low = jnp.concatenate([self_low[:1], jnp.where(joined, self_low[:-1], self_low[1:])], axis=0)
    below_low = jnp.concatenate([jnp.where(joined, self_low[1:], self_low[:-1]), self_low[-1:]], axis=0)
    upper_bound = jnp.maximum(upper_bound, jnp.maximum(above_high, below_high))
    lower_bound = jnp.minimum(lower_bound, jnp.minimum(above_low, below_low))
    anti_east, anti_north, anti_up = anti
    gain = (jnp.maximum(anti_east[:, :-1], 0.0) + jnp.maximum(-anti_east[:, 1:], 0.0)
            + jnp.maximum(anti_north[:, :, :-1], 0.0) + jnp.maximum(-anti_north[:, :, 1:], 0.0)
            + jnp.maximum(anti_up[1:], 0.0) + jnp.maximum(-anti_up[:-1], 0.0))
    loss = (jnp.maximum(anti_east[:, 1:], 0.0) + jnp.maximum(-anti_east[:, :-1], 0.0)
            + jnp.maximum(anti_north[:, :, 1:], 0.0) + jnp.maximum(-anti_north[:, :, :-1], 0.0)
            + jnp.maximum(anti_up[:-1], 0.0) + jnp.maximum(-anti_up[1:], 0.0))
    lowered_mid = lowered[:, 1:-1, 1:-1]
    raise_ratio = jnp.minimum(1.0, (upper_bound - lowered_mid) / jnp.maximum(gain, flux_floor))
    drop_ratio = jnp.minimum(1.0, (lowered_mid - lower_bound) / jnp.maximum(loss, flux_floor))
    return raise_ratio, drop_ratio


def limited(anti, raise_pad, drop_pad):
    anti_east, anti_north, anti_up = anti
    factor_east = jnp.where(anti_east >= 0.0,
                            jnp.minimum(raise_pad[:, 1:, 1:-1], drop_pad[:, :-1, 1:-1]),
                            jnp.minimum(raise_pad[:, :-1, 1:-1], drop_pad[:, 1:, 1:-1]))
    factor_north = jnp.where(anti_north >= 0.0,
                             jnp.minimum(raise_pad[:, 1:-1, 1:], drop_pad[:, 1:-1, :-1]),
                             jnp.minimum(raise_pad[:, 1:-1, :-1], drop_pad[:, 1:-1, 1:]))
    raise_mid = raise_pad[:, 1:-1, 1:-1]
    drop_mid = drop_pad[:, 1:-1, 1:-1]
    factor_up = jnp.where(anti_up[1:-1] >= 0.0,
                          jnp.minimum(raise_mid[:-1], drop_mid[1:]),
                          jnp.minimum(raise_mid[1:], drop_mid[:-1]))
    border = jnp.ones_like(factor_up[:1])
    factor_up = jnp.concatenate([border, factor_up, border], axis=0)
    return factor_east * anti_east, factor_north * anti_north, factor_up * anti_up


def first_round(padded):
    results = []
    for tracer in range(2):
        low, anti = face_fluxes(padded[tracer], padded[2], padded[3], padded[4], padded[5])
        results.append(padded[tracer, :, 1:-1, 1:-1] - divergence(*low))
    return jnp.stack(results)


def second_round(padded, lowered_pad):
    results = []
    for tracer in range(2):
        low, anti = face_fluxes(padded[tracer], padded[2], padded[3], padded[4], padded[5])
        raise_ratio, drop_ratio = limits(padded[tracer], lowered_pad[tracer], padded[2], anti)
        results.append(raise_ratio)
        results.append(drop_ratio)
    return jnp.stack(results)


def third_round(padded, ratios_pad, lowered):
    results = []
    for tracer in range(2):
        low, anti = face_fluxes(padded[tracer], padded[2], padded[3], padded[4], padded[5])
        fluxes = limited(anti, ratios_pad[2 * tracer], ratios_pad[2 * tracer + 1])
        results.append(lowered[tracer] - divergence(*fluxes))
    return jnp.stack(results)


def vertical_mix(scalar_property_arrays, diffusive_coupling_number, sea_grid_indicator):
    vertical_layer_grid = sea_grid_indicator.shape[0]
    zeros_row = jnp.zeros_like(sea_grid_indicator[0])
    inner = diffusive_coupling_number * sea_grid_indicator[1:] * sea_grid_indicator[:-1]
    numbers = [zeros_row] + [inner[level] for level in range(vertical_layer_grid - 1)] + [zeros_row]
    ratios = []
    values = []
    prior_ratio = zeros_row
    prior_value = jnp.zeros_like(scalar_property_arrays[:, 0])
    for level in range(vertical_layer_grid):
        denom = 1.0 + numbers[level] + numbers[level + 1] + numbers[level] * prior_ratio
        prior_ratio = -numbers[level + 1] / denom
        prior_value = (scalar_property_arrays[:, level] + numbers[level] * prior_value) / denom
        ratios.append(prior_ratio)
        values.append(prior_value)
    solved = [None] * vertical_layer_grid
    solved[vertical_layer_grid - 1] = values[vertical_layer_grid - 1]
    for level in range(vertical_layer_grid - 2, -1, -1):
        solved[level] = values[level] - ratios[level] * solved[level + 1]
    return jnp.stack(solved, axis=1)


def pad_global(scalar_property_arrays):
    scalar_property_arrays = jnp.concatenate([scalar_property_arrays[:, :, -1:], scalar_property_arrays, scalar_property_arrays[:, :, :1]], axis=2)
    southern = jnp.zeros_like(scalar_property_arrays[..., :1])
    northern = jnp.flip(scalar_property_arrays[..., -1:], axis=2)
    return jnp.concatenate([southern, scalar_property_arrays, northern], axis=3)


def reference(thermal_anomaly_array, saltiness_anomaly_array, zonal_volume_passage, meridional_volume_passage, rising_volume_passage, diffusive_coupling_number, sea_column_flag, seabed_layer_index):
    vertical_layer_grid = lax.broadcasted_iota(jnp.int32, thermal_anomaly_array.shape, 0)
    sea_grid_indicator = jnp.where((vertical_layer_grid < seabed_layer_index[None]) & (sea_column_flag[None] > 0), 1.0, 0.0).astype(jnp.float32)
    rising_passage_finished = jnp.concatenate([jnp.zeros_like(rising_volume_passage[:1]), rising_volume_passage], axis=0)
    scalar_property_arrays = jnp.stack([thermal_anomaly_array, saltiness_anomaly_array, sea_grid_indicator, zonal_volume_passage, meridional_volume_passage, rising_passage_finished])
    padded = pad_global(scalar_property_arrays)
    northward = padded[4]
    folded = 0.5 * (northward[..., -2] - northward[..., -1])
    padded = padded.at[4, :, :, -2].set(folded)
    lowered = first_round(padded)
    ratios = second_round(padded, pad_global(lowered))
    updated = third_round(padded, pad_global(ratios), lowered)
    mixed = vertical_mix(updated, diffusive_coupling_number, sea_grid_indicator)
    return mixed[0], mixed[1]
```

```python
import jax
import jax.numpy as jnp
from jax import lax
from jax.experimental import pallas as pl
from jax.experimental.pallas import tpu as pltpu
from jax.sharding import PartitionSpec as P

FLUX_FLOOR = 0.01
BIG = 1e30
AXES = ("lon", "lat")
F32 = jnp.float32


SPOTS = (("t", 0, 0, 3), ("s", 0, 3, 3), ("u", 0, 6, 2), ("v", 1, 0, 3), ("w", 1, 3, 2), ("m", 1, 5, 3))


def roll(x, shift, axis):
    shift = shift % x.shape[axis]
    return x if shift == 0 else pltpu.roll(x, shift, axis)


def place():
    return lax.axis_index("lon"), lax.axis_index("lat")


def wet_of(flag, depth, level):
    return jnp.where((level < depth) & (flag > 0), 1.0, 0.0).astype(F32)


def pack(t, s, u, v, w, flag, depth, core, chip, chip1, lat1, top, bottom):
    levels, rows, lanes = t.shape
    i, j = place()
    even = lax.rem(i, 2) == 0
    lane = lax.broadcasted_iota(jnp.int32, (rows, lanes), 1)
    group, spot = lane >> 3, lane & 7
    flags, depths = flag[...], depth[...]
    zero = jnp.zeros((rows, lanes), F32)
    tops, bottoms = [zero, zero], [zero, zero]
    wets = []
    for k in range(levels):
        wet = wet_of(flags, depths, k)
        wets.append(wet)
        here = dict(t=t[k], s=s[k], u=u[k], v=v[k], w=w[k] if k < levels - 1 else zero, m=wet)
        for name, slab, start, count in SPOTS:
            mine = (group == k) & (spot >= start) & (spot < start + count)
            tops[slab] = jnp.where(mine, roll(here[name], 8 * k + start - (lanes - count), 1), tops[slab])
            bottoms[slab] = jnp.where(mine, roll(here[name], 8 * k + start, 1), bottoms[slab])
    for slab in range(2):
        top[slab] = tops[slab]
        bottom[slab] = bottoms[slab]
        lat1[slab] = jnp.where(j == 0, tops[slab], bottoms[slab])

    def sides(out, east, tail):
        a, b, c = (rows - 3, rows - 3, rows - 2) if east else (0, 0, 0)
        for k in range(levels):
            out[k, 0:3] = t[k, a : a + 3]
            out[k, 3:6] = s[k, a : a + 3]
            out[k, 6:9] = u[k, a : a + 3]
            out[k, 9:11] = v[k, c : c + 2]
            if k < levels - 1:
                out[k, 11:13] = w[k, c : c + 2]
            else:
                out[k, 11:13] = jnp.zeros((2, lanes), F32)
            out[k, 13:16] = wets[k][b : b + 3]
        edges(out.at[levels], east)
        if tail is not None:
            edges(tail, east)

    def edges(out, east):
        a = rows - 3 if east else 0
        for n, x in enumerate(tops + (bottoms if out.shape[0] > 8 else [])):
            out[3 * n : 3 * n + 3] = x[a : a + 3]

    core[levels] = zero
    chip[levels] = zero
    chip1[...] = jnp.zeros(chip1.shape, F32)

    @pl.when(even)
    def _():
        sides(core, True, None)
        sides(chip, False, chip1)

    @pl.when(jnp.logical_not(even))
    def _():
        sides(core, False, None)
        sides(chip, True, chip1)


def repack(top, core, chip1, lat1, chip_in, chip, core2, fold):
    i, j = place()
    even = lax.rem(i, 2) == 0
    levels = core.shape[0] - 1
    rows, lanes = top.shape[1:]
    for slab in range(2):
        fold[slab, 0:rows] = top[slab]
        fold[slab, rows : rows + 8] = jnp.zeros((8, lanes), F32)
    chip[0] = jnp.zeros((rows, lanes), F32)
    core2[...] = jnp.zeros(core2.shape, F32)

    def fill(even):
        for slab in range(2):
            near, far = core[levels, 3 * slab : 3 * slab + 3], chip1[3 * slab : 3 * slab + 3]
            east, west = (near, far) if even else (far, near)
            fold[slab, rows : rows + 3] = east
            fold[slab, rows + 5 : rows + 8] = west
            a, b = (rows - 3, 0) if even else (0, rows - 3)
            core2[3 * slab : 3 * slab + 3] = lat1[slab, a : a + 3]
            chip[0, 3 * slab : 3 * slab + 3] = lat1[slab, b : b + 3]

    @pl.when(even)
    def _():
        fill(True)

    @pl.when(jnp.logical_not(even))
    def _():
        fill(False)

    for slab in range(2):
        for part in range(3):
            piece = fold[slab, 8 * part : 8 * part + 8]
            at = slab * 24 + 8 * part
            chip[1 + at // 16, at % 16 : at % 16 + 8] = piece


def coefficients(dc, flag, depth, number, inverse):
    levels = inverse.shape[0]
    flags, depths = flag[...], depth[...]
    zero = jnp.zeros(flags.shape, F32)
    q = [zero]
    for k in range(1, levels):
        q.append(dc[k - 1] * wet_of(flags, depths, k))
    q.append(zero)
    ratio = zero
    for k in range(levels):
        denom = 1.0 + q[k] + q[k + 1] - q[k] * ratio
        inv = 1.0 / denom
        ratio = q[k + 1] * inv
        number[k] = q[k]
        inverse[k] = inv


def step(
    t, s, u, v, w, flag, depth, number, inverse, core, chip, chip2, core2, fold, lat1, top, bottom,
    new_t, new_s,
    ct, cs, cu, cv, cw, cm, mirror, edge,
    low_t, low_s, ae_t, ae_s, an_t, an_s, au_t, au_s, hi_t, hi_s, lo_t, lo_s, up_t, up_s, dn_t, dn_s,
):
    i, j = place()
    n_lon, n_lat = lax.axis_size("lon"), lax.axis_size("lat")
    even = lax.rem(i, 2) == 0
    first, last, is_top, is_low = i == 0, i == n_lon - 1, j == n_lat - 1, j == 0
    levels, rows, lanes = t.shape
    wide = rows + 8
    lane = lax.broadcasted_iota(jnp.int32, (wide, lanes), 1)
    spot = lane & 7
    flags, depths = flag[...], depth[...]
    cells = (ct, cs, cu, cv, cw, cm)
    north, south = levels, levels + 1

    for ref in cells:
        for k in range(levels):
            ref[k, rows : rows + 8] = jnp.zeros((8, lanes), F32)
    for k in range(levels):
        ct[k, 0:rows] = t[k]
        cs[k, 0:rows] = s[k]
        cu[k, 0:rows] = u[k]
        cv[k, 0:rows] = v[k]
        cw[k, 0:rows] = w[k] if k < levels - 1 else jnp.zeros((rows, lanes), F32)
        cm[k, 0:rows] = wet_of(flags, depths, k)

    for slab in range(2):
        edge[slab, 0:rows] = top[slab]
        edge[2 + slab, 0:rows] = bottom[slab]
        edge[4 + slab, 0:rows] = lat1[slab]
        for n in range(3):
            edge[2 * n + slab, rows : rows + 8] = jnp.zeros((8, lanes), F32)
        for part in range(3):
            at = slab * 24 + 8 * part
            wrapped = chip2[1 + at // 16, at % 16 : at % 16 + 8]
            edge[6 + slab, 8 * part : 8 * part + 8] = jnp.where(
                first | last, wrapped, fold[slab, 8 * part : 8 * part + 8]
            )

    def fill(even):
        for src, src2, east in ((core, core2, even), (chip, chip2.at[0], not even)):
            a = rows if east else rows + 5
            b = rows if east else rows + 6
            for k in range(levels):
                ct[k, a : a + 3] = src[k, 0:3]
                cs[k, a : a + 3] = src[k, 3:6]
                cu[k, a : a + 3] = src[k, 6:9]
                cv[k, b : b + 2] = src[k, 9:11]
                cw[k, b : b + 2] = src[k, 11:13]
                cm[k, a : a + 3] = src[k, 13:16]
            for n in range(4):
                edge[n, a : a + 3] = src[levels, 3 * n : 3 * n + 3]
            for n in range(2):
                edge[4 + n, a : a + 3] = src2[3 * n : 3 * n + 3]

    @pl.when(even)
    def _():
        fill(True)

    @pl.when(jnp.logical_not(even))
    def _():
        fill(False)

    @pl.when(first)
    def _():
        for slab in range(2):
            edge[6 + slab, rows : rows + 3] = top[slab, 0:3]

    @pl.when(last)
    def _():
        for slab in range(2):
            edge[6 + slab, rows + 5 : rows + 8] = top[slab, rows - 3 : rows]

    for slab in range(2):
        for r in range(wide):
            q = (rows - 1 - r) % wide
            mirror[slab, r : r + 1] = edge[6 + slab, q : q + 1]

    own_n = (edge[0], edge[1])
    own_s = (edge[2], edge[3])
    other = (edge[4], edge[5])
    mir = (mirror[0], mirror[1])

    def pick(pairs):
        out = jnp.zeros((wide, lanes), F32)
        for at, value in pairs:
            out = jnp.where(spot == at, value, out)
        return out

    def mirrored(name):
        _, slab, start, count = next(x for x in SPOTS if x[0] == name)
        x = mir[slab]
        if name == "u":
            x = -roll(x, -1, 0)
            return pick([(3 + d, roll(x, 3 + d - (start + 1 - d), 1)) for d in range(2)])
        if name == "v":
            return pick([(3 + d, -roll(x, 3 + d - (start + 1 - d), 1)) for d in range(2)])
        last_one = start + count - 1
        return pick([(3 + d, roll(x, 3 + d - (last_one - d), 1)) for d in range(count)])

    for ref, (name, slab, start, count) in zip(cells, SPOTS):
        lead = 3 - count
        head = roll(own_n[slab], lead - start, 1)
        if name == "v":
            folded = 0.5 * (head - mir[slab])
            head = jnp.where((spot == 2) & is_top, folded, head)
        beyond = jnp.where(is_top, mirrored(name), roll(other[slab], 3 - start, 1))
        ref[north] = jnp.where(spot < 3, head, beyond)
        before = roll(other[slab], lead - start, 1)
        tail = roll(own_s[slab], 3 - start, 1)
        if name == "m":
            before = jnp.where(is_low, 0.0, before)
        ref[south] = jnp.where(spot < 3, before, tail)

    cut = spot > 5
    for strip in (north, south):
        cm[strip] = jnp.where(cut, 0.0, cm[strip])

    def at_n(ref, k):
        if k >= levels:
            return roll(ref[k], -1, 1)
        return jnp.where(lane == lanes - 1, roll(ref[north], lanes - 1 - (8 * k + 3), 1), roll(ref[k], -1, 1))

    def at_s(ref, k, value=None):
        value = ref[k] if value is None else value
        if k >= levels:
            return roll(value, 1, 1)
        return jnp.where(lane == 0, roll(ref[south], -(8 * k + 2), 1), roll(value, 1, 1))

    def east(x):
        return roll(x, -1, 0)

    def west(x):
        return roll(x, 1, 0)

    lowest = lane >= 8 * (levels - 1)
    highest = lane < 8

    def below(ref, k, edge_value):
        if k >= levels:
            x = roll(ref[k], -8, 1)
            return x if edge_value is None else jnp.where(lowest, edge_value, x)
        return ref[k + 1] if k < levels - 1 else None

    def above(ref, k, edge_value):
        if k >= levels:
            x = roll(ref[k], 8, 1)
            return x if edge_value is None else jnp.where(highest, edge_value, x)
        return ref[k - 1] if k > 0 else None

    order = (north, south) + tuple(range(levels))
    tracers = (
        (ct, low_t, ae_t, an_t, au_t, hi_t, lo_t, up_t, dn_t),
        (cs, low_s, ae_s, an_s, au_s, hi_s, lo_s, up_s, dn_s),
    )

    for k in range(levels):
        cv[k] = jnp.where(lane == lanes - 1, roll(cv[north], lanes - 1 - (8 * k + 2), 1), cv[k])

    above_low = [None, None]
    for k in order:
        wet = cm[k]
        ue = cu[k] * (wet * east(wet))
        un = cv[k] * (wet * at_n(cm, k))
        wet_below = below(cm, k, 0.0)
        uu = None if wet_below is None else cw[k] * (wet * wet_below)
        for n, (c, low, ae, an, au, hi, lo, face, _) in enumerate(tracers):
            x = c[k]

            def fluxes(speed, a, b):
                flux = jnp.maximum(speed, 0.0) * a + jnp.minimum(speed, 0.0) * b
                return flux, 0.5 * jnp.abs(speed) * (b - a)

            fe, anti_e = fluxes(ue, x, east(x))
            fn, anti_n = fluxes(un, x, at_n(c, k))
            ae[k] = anti_e
            an[k] = anti_n
            if k >= levels:
                face[k] = fn
            out = (fe - west(fe)) + (fn - at_s(face, k, fn))
            if uu is not None:
                fu, anti_u = fluxes(uu, below(c, k, None), x)
                au[k] = anti_u
                out = out - fu
            if k >= levels:
                out = out + jnp.where(highest, 0.0, roll(fu, 8, 1))
            else:
                if k > 0:
                    out = out + above_low[n]
                above_low[n] = fu if uu is not None else None
            lowered = x - out
            low[k] = lowered
            dry = wet == 0.0
            hi[k] = jnp.where(dry, -BIG, jnp.maximum(x, lowered))
            lo[k] = jnp.where(dry, BIG, jnp.minimum(x, lowered))

    for k in order:
        for c, low, ae, an, au, hi, lo, rise, drop in tracers:
            top_value = hi[k]
            around = [east(top_value), west(top_value), at_n(hi, k), at_s(hi, k), below(hi, k, -BIG), above(hi, k, -BIG)]
            for x in around:
                if x is not None:
                    top_value = jnp.maximum(top_value, x)
            low_value = lo[k]
            around = [east(low_value), west(low_value), at_n(lo, k), at_s(lo, k), below(lo, k, BIG), above(lo, k, BIG)]
            for x in around:
                if x is not None:
                    low_value = jnp.minimum(low_value, x)
            anti_e, anti_n = ae[k], an[k]
            outward = [anti_e, anti_n]
            inward = [west(anti_e), at_s(an, k)]
            if k >= levels or k < levels - 1:
                inward.append(au[k])
            over = above(au, k, 0.0)
            if over is not None:
                outward.append(over)
            gain = sum(jnp.maximum(x, 0.0) for x in inward) - sum(jnp.minimum(x, 0.0) for x in outward)
            loss = sum(jnp.maximum(x, 0.0) for x in outward) - sum(jnp.minimum(x, 0.0) for x in inward)
            lowered = low[k]
            rise[k] = jnp.minimum(1.0, (top_value - lowered) / jnp.maximum(gain, FLUX_FLOOR))
            drop[k] = jnp.minimum(1.0, (lowered - low_value) / jnp.maximum(loss, FLUX_FLOOR))

    def limited(anti, rise_a, drop_a, rise_b, drop_b):
        return anti * jnp.where(anti >= 0.0, jnp.minimum(rise_b, drop_a), jnp.minimum(rise_a, drop_b))

    for c, low, ae, an, au, hi, lo, rise, drop in tracers:
        k = south
        hi[k] = limited(an[k], rise[k], drop[k], at_n(rise, k), at_n(drop, k))
    values = [None, None]
    above_up = [None, None]
    for k in range(levels):
        q, inv = number[k], inverse[k]
        for n, (c, low, ae, an, au, hi, lo, rise, drop) in enumerate(tracers):
            r, d = rise[k], drop[k]
            fe = limited(ae[k], r, d, east(r), east(d))
            fn = limited(an[k], r, d, at_n(rise, k), at_n(drop, k))
            out = (fe - west(fe)) + (fn - at_s(hi, k, fn))
            if k < levels - 1:
                fu = limited(au[k], rise[k + 1], drop[k + 1], r, d)
                out = out - fu
            if k > 0:
                out = out + above_up[n]
            above_up[n] = fu
            x = (low[k] - out)[0:rows]
            if k > 0:
                x = x + q * values[n]
            values[n] = x * inv
            lo[k, 0:rows] = values[n]
    for n, (tracer, out) in enumerate(zip(tracers, (new_t, new_s))):
        x = values[n]
        out[levels - 1] = x
        for k in range(levels - 2, -1, -1):
            x = tracer[6][k, 0:rows] + (number[k + 1] * inverse[k]) * x
            out[k] = x


def call(body, outs, args, scratch=(), aliases=None, cost=(2_000_000, 2_000_000)):
    vmem = pl.BlockSpec(memory_space=pltpu.VMEM)
    return pl.pallas_call(
        body,
        out_shape=tuple(jax.ShapeDtypeStruct(x, F32) for x in outs),
        in_specs=[vmem] * len(args),
        out_specs=tuple(vmem for _ in outs),
        scratch_shapes=[pltpu.VMEM(x, F32) for x in scratch],
        cost_estimate=pl.CostEstimate(flops=cost[0], bytes_accessed=cost[1], transcendentals=0),
    )(*args)


def local(n_lon, n_lat, t, s, u, v, w, dc, flag, depth):
    levels, rows, lanes = t.shape
    wide = rows + 8

    def number(i, j):
        return (i % n_lon) * n_lat + j

    grid = [(i, j) for i in range(n_lon) for j in range(n_lat)]

    def beside(i):
        return i - 1 if i % 2 == 0 else i + 1

    cores = [(number(i, j), number(i ^ 1, j)) for i, j in grid]
    chips = [(number(i, j), number(beside(i), j)) for i, j in grid]
    inner = [(number(i, j), number(beside(i), j)) for i, j in grid if 0 <= beside(i) < n_lon]
    lats = [(number(i, j), number(i, n_lat - 1 - j)) for i, j in grid]
    folds = [(number(i, n_lat - 1), number(n_lon - 1 - i, n_lat - 1)) for i in range(1, n_lon - 1)]

    core, chip, chip1, lat1, top, bottom = call(
        pack,
        [(levels + 1, rows, lanes), (levels + 1, rows, lanes), (8, lanes)] + [(2, rows, lanes)] * 3,
        (t, s, u, v, w, flag, depth),
    )
    chip1_in = lax.ppermute(chip1, AXES, inner)
    lat1_in = lax.ppermute(lat1, AXES, lats)
    core_in = lax.ppermute(core, AXES, cores)
    numbers, inverse = call(coefficients, [(levels, rows, lanes)] * 2, (dc, flag, depth))
    chip2, core2, fold = call(
        repack, [(4, rows, lanes), (8, lanes), (2, wide, lanes)], (top, core_in, chip1_in, lat1_in, chip)
    )
    chip_in = lax.ppermute(jnp.concatenate([chip, chip2], axis=0), AXES, chips)
    fold_in = lax.ppermute(fold, AXES, folds)
    core2_in = lax.ppermute(core2, AXES, cores)
    slab = (wide, lanes)
    scratch = [(levels + 2, *slab)] * 6 + [(2, *slab), (8, *slab)] + [(levels + 2, *slab)] * 16
    return call(
        step,
        [(levels, rows, lanes)] * 2,
        (t, s, u, v, w, flag, depth, numbers, inverse, core_in, chip_in[: levels + 1], chip_in[levels + 1 :],
         core2_in, fold_in, lat1_in, top, bottom),
        scratch,
    )


def solution(mesh):
    n_lon, n_lat = mesh.shape["lon"], mesh.shape["lat"]
    cube = P(None, "lon", "lat")
    plane = P("lon", "lat")
    return jax.shard_map(
        lambda *args: tuple(local(n_lon, n_lat, *args)),
        mesh=mesh,
        in_specs=(cube,) * 6 + (plane,) * 2,
        out_specs=(cube, cube),
        check_vma=False,
    )
```

```python
import jax
import jax.numpy as jnp
from jax import lax
from jax.experimental import pallas as pl
from jax.experimental.pallas import tpu as pltpu
from jax.sharding import PartitionSpec as P

FLUX_FLOOR = 0.01
BIG = 1e30
AXES = ("lon", "lat")
F32 = jnp.float32


SPOTS = (("t", 0, 0, 3), ("s", 0, 3, 3), ("u", 0, 6, 2), ("v", 1, 0, 3), ("w", 1, 3, 2), ("m", 1, 5, 3))


def roll(x, shift, axis):
    shift = shift % x.shape[axis]
    return x if shift == 0 else pltpu.roll(x, shift, axis)


def place():
    return lax.axis_index("lon"), lax.axis_index("lat")


def wet_of(flag, depth, level):
    return jnp.where((level < depth) & (flag > 0), 1.0, 0.0).astype(F32)


def pack(t, s, u, v, w, flag, depth, core, chip, chip1, lat1, top, bottom):
    levels, rows, lanes = t.shape
    i, j = place()
    even = lax.rem(i, 2) == 0
    lane = lax.broadcasted_iota(jnp.int32, (rows, lanes), 1)
    group, spot = lane >> 3, lane & 7
    flags, depths = flag[...], depth[...]
    zero = jnp.zeros((rows, lanes), F32)
    tops, bottoms = [zero, zero], [zero, zero]
    wets = []
    for k in range(levels):
        wet = wet_of(flags, depths, k)
        wets.append(wet)
        here = dict(t=t[k], s=s[k], u=u[k], v=v[k], w=w[k] if k < levels - 1 else zero, m=wet)
        for name, slab, start, count in SPOTS:
            mine = (group == k) & (spot >= start) & (spot < start + count)
            tops[slab] = jnp.where(mine, roll(here[name], 8 * k + start - (lanes - count), 1), tops[slab])
            bottoms[slab] = jnp.where(mine, roll(here[name], 8 * k + start, 1), bottoms[slab])
    for slab in range(2):
        top[slab] = tops[slab]
        bottom[slab] = bottoms[slab]
        lat1[slab] = jnp.where(j == 0, tops[slab], bottoms[slab])

    def sides(out, east, tail):
        a, b, c = (rows - 3, rows - 3, rows - 2) if east else (0, 0, 0)
        for k in range(levels):
            out[k, 0:3] = t[k, a : a + 3]
            out[k, 3:6] = s[k, a : a + 3]
            out[k, 6:9] = u[k, a : a + 3]
            out[k, 9:11] = v[k, c : c + 2]
            if k < levels - 1:
                out[k, 11:13] = w[k, c : c + 2]
            else:
                out[k, 11:13] = jnp.zeros((2, lanes), F32)
            out[k, 13:16] = wets[k][b : b + 3]
        edges(out.at[levels], east)
        if tail is not None:
            edges(tail, east)

    def edges(out, east):
        a = rows - 3 if east else 0
        for n, x in enumerate(tops + (bottoms if out.shape[0] > 8 else [])):
            out[3 * n : 3 * n + 3] = x[a : a + 3]

    core[levels] = zero
    chip[levels] = zero
    chip1[...] = jnp.zeros(chip1.shape, F32)

    @pl.when(even)
    def _():
        sides(core, True, None)
        sides(chip, False, chip1)

    @pl.when(jnp.logical_not(even))
    def _():
        sides(core, False, None)
        sides(chip, True, chip1)


def repack(top, core, chip1, lat1, packed, chip, core2, fold):
    i, j = place()
    even = lax.rem(i, 2) == 0
    levels = core.shape[0] - 1
    base = levels + 1
    rows, lanes = top.shape[1:]
    for slab in range(2):
        fold[slab, 0:rows] = top[slab]
        fold[slab, rows : rows + 8] = jnp.zeros((8, lanes), F32)
    chip[base] = jnp.zeros((rows, lanes), F32)
    core2[...] = jnp.zeros(core2.shape, F32)

    def fill(even):
        for slab in range(2):
            near, far = core[levels, 3 * slab : 3 * slab + 3], chip1[3 * slab : 3 * slab + 3]
            east, west = (near, far) if even else (far, near)
            fold[slab, rows : rows + 3] = east
            fold[slab, rows + 5 : rows + 8] = west
            a, b = (rows - 3, 0) if even else (0, rows - 3)
            core2[3 * slab : 3 * slab + 3] = lat1[slab, a : a + 3]
            chip[base, 3 * slab : 3 * slab + 3] = lat1[slab, b : b + 3]

    @pl.when(even)
    def _():
        fill(True)

    @pl.when(jnp.logical_not(even))
    def _():
        fill(False)

    for slab in range(2):
        for part in range(3):
            piece = fold[slab, 8 * part : 8 * part + 8]
            at = slab * 24 + 8 * part
            chip[base + 1 + at // 16, at % 16 : at % 16 + 8] = piece


def coefficients(dc, flag, depth, number, inverse):
    levels = inverse.shape[0]
    flags, depths = flag[...], depth[...]
    zero = jnp.zeros(flags.shape, F32)
    q = [zero]
    for k in range(1, levels):
        q.append(dc[k - 1] * wet_of(flags, depths, k))
    q.append(zero)
    ratio = zero
    for k in range(levels):
        denom = 1.0 + q[k] + q[k + 1] - q[k] * ratio
        inv = 1.0 / denom
        ratio = q[k + 1] * inv
        number[k] = q[k]
        inverse[k] = inv


def step(
    t, s, u, v, w, flag, depth, number, inverse, core, chip, core2, fold, lat1, top, bottom,
    new_t, new_s,
    ct, cs, cu, cv, cw, cm, mirror, edge,
    low_t, low_s, ae_t, ae_s, an_t, an_s, au_t, au_s, hi_t, hi_s, lo_t, lo_s, up_t, up_s, dn_t, dn_s,
):
    i, j = place()
    n_lon, n_lat = lax.axis_size("lon"), lax.axis_size("lat")
    even = lax.rem(i, 2) == 0
    first, last, is_top, is_low = i == 0, i == n_lon - 1, j == n_lat - 1, j == 0
    levels, rows, lanes = t.shape
    wide = rows + 8
    lane = lax.broadcasted_iota(jnp.int32, (wide, lanes), 1)
    spot = lane & 7
    flags, depths = flag[...], depth[...]
    cells = (ct, cs, cu, cv, cw, cm)
    north, south = levels, levels + 1

    for ref in cells:
        for k in range(levels):
            ref[k, rows : rows + 8] = jnp.zeros((8, lanes), F32)
    for k in range(levels):
        ct[k, 0:rows] = t[k]
        cs[k, 0:rows] = s[k]
        cu[k, 0:rows] = u[k]
        cv[k, 0:rows] = v[k]
        cw[k, 0:rows] = w[k] if k < levels - 1 else jnp.zeros((rows, lanes), F32)
        cm[k, 0:rows] = wet_of(flags, depths, k)

    for slab in range(2):
        edge[slab, 0:rows] = top[slab]
        edge[2 + slab, 0:rows] = bottom[slab]
        edge[4 + slab, 0:rows] = lat1[slab]
        for n in range(3):
            edge[2 * n + slab, rows : rows + 8] = jnp.zeros((8, lanes), F32)
        for part in range(3):
            at = slab * 24 + 8 * part
            wrapped = chip[levels + 2 + at // 16, at % 16 : at % 16 + 8]
            edge[6 + slab, 8 * part : 8 * part + 8] = jnp.where(
                first | last, wrapped, fold[slab, 8 * part : 8 * part + 8]
            )

    def fill(even):
        for src, src2, east in ((core, core2, even), (chip, chip.at[levels + 1], not even)):
            a = rows if east else rows + 5
            b = rows if east else rows + 6
            for k in range(levels):
                ct[k, a : a + 3] = src[k, 0:3]
                cs[k, a : a + 3] = src[k, 3:6]
                cu[k, a : a + 3] = src[k, 6:9]
                cv[k, b : b + 2] = src[k, 9:11]
                cw[k, b : b + 2] = src[k, 11:13]
                cm[k, a : a + 3] = src[k, 13:16]
            for n in range(4):
                edge[n, a : a + 3] = src[levels, 3 * n : 3 * n + 3]
            for n in range(2):
                edge[4 + n, a : a + 3] = src2[3 * n : 3 * n + 3]

    @pl.when(even)
    def _():
        fill(True)

    @pl.when(jnp.logical_not(even))
    def _():
        fill(False)

    @pl.when(first)
    def _():
        for slab in range(2):
            edge[6 + slab, rows : rows + 3] = top[slab, 0:3]

    @pl.when(last)
    def _():
        for slab in range(2):
            edge[6 + slab, rows + 5 : rows + 8] = top[slab, rows - 3 : rows]

    for slab in range(2):
        for r in range(wide):
            q = (rows - 1 - r) % wide
            mirror[slab, r : r + 1] = edge[6 + slab, q : q + 1]

    own_n = (edge[0], edge[1])
    own_s = (edge[2], edge[3])
    other = (edge[4], edge[5])
    mir = (mirror[0], mirror[1])

    def pick(pairs):
        out = jnp.zeros((wide, lanes), F32)
        for at, value in pairs:
            out = jnp.where(spot == at, value, out)
        return out

    def mirrored(name):
        _, slab, start, count = next(x for x in SPOTS if x[0] == name)
        x = mir[slab]
        if name == "u":
            x = -roll(x, -1, 0)
            return pick([(3 + d, roll(x, 3 + d - (start + 1 - d), 1)) for d in range(2)])
        if name == "v":
            return pick([(3 + d, -roll(x, 3 + d - (start + 1 - d), 1)) for d in range(2)])
        last_one = start + count - 1
        return pick([(3 + d, roll(x, 3 + d - (last_one - d), 1)) for d in range(count)])

    for ref, (name, slab, start, count) in zip(cells, SPOTS):
        lead = 3 - count
        head = roll(own_n[slab], lead - start, 1)
        if name == "v":
            folded = 0.5 * (head - mir[slab])
            head = jnp.where((spot == 2) & is_top, folded, head)
        beyond = jnp.where(is_top, mirrored(name), roll(other[slab], 3 - start, 1))
        ref[north] = jnp.where(spot < 3, head, beyond)
        before = roll(other[slab], lead - start, 1)
        tail = roll(own_s[slab], 3 - start, 1)
        if name == "m":
            before = jnp.where(is_low, 0.0, before)
        ref[south] = jnp.where(spot < 3, before, tail)

    cut = spot > 5
    for strip in (north, south):
        cm[strip] = jnp.where(cut, 0.0, cm[strip])

    def at_n(ref, k):
        if k >= levels:
            return roll(ref[k], -1, 1)
        return jnp.where(lane == lanes - 1, roll(ref[north], lanes - 1 - (8 * k + 3), 1), roll(ref[k], -1, 1))

    def at_s(ref, k, value=None):
        value = ref[k] if value is None else value
        if k >= levels:
            return roll(value, 1, 1)
        return jnp.where(lane == 0, roll(ref[south], -(8 * k + 2), 1), roll(value, 1, 1))

    def east(x):
        return roll(x, -1, 0)

    def west(x):
        return roll(x, 1, 0)

    lowest = lane >= 8 * (levels - 1)
    highest = lane < 8

    def below(ref, k, edge_value):
        if k >= levels:
            x = roll(ref[k], -8, 1)
            return x if edge_value is None else jnp.where(lowest, edge_value, x)
        return ref[k + 1] if k < levels - 1 else None

    def above(ref, k, edge_value):
        if k >= levels:
            x = roll(ref[k], 8, 1)
            return x if edge_value is None else jnp.where(highest, edge_value, x)
        return ref[k - 1] if k > 0 else None

    order = (north, south) + tuple(range(levels))
    tracers = (
        (ct, low_t, ae_t, an_t, au_t, hi_t, lo_t, up_t, dn_t),
        (cs, low_s, ae_s, an_s, au_s, hi_s, lo_s, up_s, dn_s),
    )

    for k in range(levels):
        cv[k] = jnp.where(lane == lanes - 1, roll(cv[north], lanes - 1 - (8 * k + 2), 1), cv[k])

    above_low = [None, None]
    for k in order:
        wet = cm[k]
        ue = cu[k] * (wet * east(wet))
        un = cv[k] * (wet * at_n(cm, k))
        wet_below = below(cm, k, 0.0)
        uu = None if wet_below is None else cw[k] * (wet * wet_below)
        for n, (c, low, ae, an, au, hi, lo, face, _) in enumerate(tracers):
            x = c[k]

            def fluxes(speed, a, b):
                flux = jnp.maximum(speed, 0.0) * a + jnp.minimum(speed, 0.0) * b
                return flux, 0.5 * jnp.abs(speed) * (b - a)

            fe, anti_e = fluxes(ue, x, east(x))
            fn, anti_n = fluxes(un, x, at_n(c, k))
            ae[k] = anti_e
            an[k] = anti_n
            if k >= levels:
                face[k] = fn
            out = (fe - west(fe)) + (fn - at_s(face, k, fn))
            if uu is not None:
                fu, anti_u = fluxes(uu, below(c, k, None), x)
                au[k] = anti_u
                out = out - fu
            if k >= levels:
                out = out + jnp.where(highest, 0.0, roll(fu, 8, 1))
            else:
                if k > 0:
                    out = out + above_low[n]
                above_low[n] = fu if uu is not None else None
            lowered = x - out
            low[k] = lowered
            dry = wet == 0.0
            hi[k] = jnp.where(dry, -BIG, jnp.maximum(x, lowered))
            lo[k] = jnp.where(dry, BIG, jnp.minimum(x, lowered))

    for k in order:
        for c, low, ae, an, au, hi, lo, rise, drop in tracers:
            top_value = hi[k]
            around = [east(top_value), west(top_value), at_n(hi, k), at_s(hi, k), below(hi, k, -BIG), above(hi, k, -BIG)]
            for x in around:
                if x is not None:
                    top_value = jnp.maximum(top_value, x)
            low_value = lo[k]
            around = [east(low_value), west(low_value), at_n(lo, k), at_s(lo, k), below(lo, k, BIG), above(lo, k, BIG)]
            for x in around:
                if x is not None:
                    low_value = jnp.minimum(low_value, x)
            anti_e, anti_n = ae[k], an[k]
            outward = [anti_e, anti_n]
            inward = [west(anti_e), at_s(an, k)]
            if k >= levels or k < levels - 1:
                inward.append(au[k])
            over = above(au, k, 0.0)
            if over is not None:
                outward.append(over)
            gain = sum(jnp.maximum(x, 0.0) for x in inward) - sum(jnp.minimum(x, 0.0) for x in outward)
            loss = sum(jnp.maximum(x, 0.0) for x in outward) - sum(jnp.minimum(x, 0.0) for x in inward)
            lowered = low[k]
            rise[k] = jnp.minimum(1.0, (top_value - lowered) / jnp.maximum(gain, FLUX_FLOOR))
            drop[k] = jnp.minimum(1.0, (lowered - low_value) / jnp.maximum(loss, FLUX_FLOOR))

    def limited(anti, rise_a, drop_a, rise_b, drop_b):
        return anti * jnp.where(anti >= 0.0, jnp.minimum(rise_b, drop_a), jnp.minimum(rise_a, drop_b))

    for c, low, ae, an, au, hi, lo, rise, drop in tracers:
        k = south
        hi[k] = limited(an[k], rise[k], drop[k], at_n(rise, k), at_n(drop, k))
    values = [None, None]
    above_up = [None, None]
    for k in range(levels):
        q, inv = number[k], inverse[k]
        for n, (c, low, ae, an, au, hi, lo, rise, drop) in enumerate(tracers):
            r, d = rise[k], drop[k]
            fe = limited(ae[k], r, d, east(r), east(d))
            fn = limited(an[k], r, d, at_n(rise, k), at_n(drop, k))
            out = (fe - west(fe)) + (fn - at_s(hi, k, fn))
            if k < levels - 1:
                fu = limited(au[k], rise[k + 1], drop[k + 1], r, d)
                out = out - fu
            if k > 0:
                out = out + above_up[n]
            above_up[n] = fu
            x = (low[k] - out)[0:rows]
            if k > 0:
                x = x + q * values[n]
            values[n] = x * inv
            lo[k, 0:rows] = values[n]
    for n, (tracer, out) in enumerate(zip(tracers, (new_t, new_s))):
        x = values[n]
        out[levels - 1] = x
        for k in range(levels - 2, -1, -1):
            x = tracer[6][k, 0:rows] + (number[k + 1] * inverse[k]) * x
            out[k] = x


def call(body, outs, args, scratch=(), aliases=None, limit=8, cost=(2_000_000, 2_000_000)):
    vmem = pl.BlockSpec(memory_space=pltpu.VMEM)
    return pl.pallas_call(
        body,
        out_shape=tuple(jax.ShapeDtypeStruct(x, F32) for x in outs),
        in_specs=[vmem] * len(args),
        out_specs=tuple(vmem for _ in outs),
        scratch_shapes=[pltpu.VMEM(x, F32) for x in scratch],
        input_output_aliases=aliases or {},
        compiler_params=pltpu.CompilerParams(vmem_limit_bytes=limit * 2**20),
        cost_estimate=pl.CostEstimate(flops=cost[0], bytes_accessed=cost[1], transcendentals=0),
    )(*args)


def local(n_lon, n_lat, t, s, u, v, w, dc, flag, depth):
    levels, rows, lanes = t.shape
    wide = rows + 8

    def number(i, j):
        return (i % n_lon) * n_lat + j

    grid = [(i, j) for i in range(n_lon) for j in range(n_lat)]

    def beside(i):
        return i - 1 if i % 2 == 0 else i + 1

    cores = [(number(i, j), number(i ^ 1, j)) for i, j in grid]
    chips = [(number(i, j), number(beside(i), j)) for i, j in grid]
    inner = [(number(i, j), number(beside(i), j)) for i, j in grid if 0 <= beside(i) < n_lon]
    lats = [(number(i, j), number(i, n_lat - 1 - j)) for i, j in grid]
    folds = [(number(i, n_lat - 1), number(n_lon - 1 - i, n_lat - 1)) for i in range(1, n_lon - 1)]

    core, chip, chip1, lat1, top, bottom = call(
        pack,
        [(levels + 1, rows, lanes), (levels + 5, rows, lanes), (8, lanes)] + [(2, rows, lanes)] * 3,
        (t, s, u, v, w, flag, depth),
    )
    chip1_in = lax.ppermute(chip1, AXES, inner)
    lat1_in = lax.ppermute(lat1, AXES, lats)
    core_in = lax.ppermute(core, AXES, cores)
    numbers, inverse = call(coefficients, [(levels, rows, lanes)] * 2, (dc, flag, depth))
    chip, core2, fold = call(
        repack,
        [chip.shape, (8, lanes), (2, wide, lanes)],
        (top, core_in, chip1_in, lat1_in, chip),
        aliases={4: 0},
        limit=2,
    )
    chip_in = lax.ppermute(chip, AXES, chips)
    fold_in = lax.ppermute(fold, AXES, folds)
    core2_in = lax.ppermute(core2, AXES, cores)
    slab = (wide, lanes)
    scratch = [(levels + 2, *slab)] * 6 + [(2, *slab), (8, *slab)] + [(levels + 2, *slab)] * 16
    return call(
        step,
        [(levels, rows, lanes)] * 2,
        (t, s, u, v, w, flag, depth, numbers, inverse, core_in, chip_in, core2_in,
          fold_in, lat1_in, top, bottom),
        scratch,
        limit=16,
    )


def solution(mesh):
    n_lon, n_lat = mesh.shape["lon"], mesh.shape["lat"]
    cube = P(None, "lon", "lat")
    plane = P("lon", "lat")
    return jax.shard_map(
        lambda *args: tuple(local(n_lon, n_lat, *args)),
        mesh=mesh,
        in_specs=(cube,) * 6 + (plane,) * 2,
        out_specs=(cube, cube),
        check_vma=False,
    )
```

```python
import jax
import jax.numpy as jnp
from jax import lax
from jax.experimental import pallas as pl
from jax.experimental.pallas import tpu as pltpu
from jax.sharding import PartitionSpec as P

FLUX_FLOOR = 0.01
BIG = 1e30
AXES = ("lon", "lat")
F32 = jnp.float32


OWN = 12
UNROLL = (4, 4, 4)
SPOTS = (("t", 0, 0, 3), ("s", 0, 3, 3), ("u", 0, 6, 2), ("v", 1, 0, 3), ("w", 1, 3, 2), ("m", 1, 5, 3))


def roll(x, shift, axis):
    if not isinstance(shift, int):
        return pltpu.roll(x, shift, axis)
    shift = shift % x.shape[axis]
    return x if shift == 0 else pltpu.roll(x, shift, axis)


def place():
    return lax.axis_index("lon"), lax.axis_index("lat")


def wet_of(flag, depth, level):
    return jnp.where((level < depth) & (flag > 0), 1.0, 0.0).astype(F32)


def pack(
    t_any, s_any, u_any, v_any, w_any, dc_any, flag_any, depth_any,
    core, chip, chip1, lat1, top, bottom, t, s, u, v, w, dc, flag, depth, sems,
):
    sources = (flag_any, depth_any, t_any, s_any, u_any, v_any, w_any, dc_any)
    targets = (flag, depth, t, s, u, v, w, dc)
    copies = [pltpu.make_async_copy(x, y, sems.at[n]) for n, (x, y) in enumerate(zip(sources, targets))]
    for copy in copies:
        copy.start()
    levels, rows, lanes = t.shape
    i, j = place()
    even = lax.rem(i, 2) == 0
    lane = lax.broadcasted_iota(jnp.int32, (rows, lanes), 1)
    group, spot = lane >> 3, lane & 7
    zero = jnp.zeros((rows, lanes), F32)
    tops, bottoms = [zero, zero], [zero, zero]
    core[levels] = zero
    chip[levels] = zero
    chip1[...] = jnp.zeros(chip1.shape, F32)
    for copy in copies:
        copy.wait()
    flags, depths = flag[...], depth[...]
    wets = []
    for k in range(levels):
        wet = wet_of(flags, depths, k)
        wets.append(wet)
        here = dict(t=t[k], s=s[k], u=u[k], v=v[k], w=w[k] if k < levels - 1 else zero, m=wet)
        for name, slab, start, count in SPOTS:
            mine = (group == k) & (spot >= start) & (spot < start + count)
            tops[slab] = jnp.where(mine, roll(here[name], 8 * k + start - (lanes - count), 1), tops[slab])
            bottoms[slab] = jnp.where(mine, roll(here[name], 8 * k + start, 1), bottoms[slab])
    for slab in range(2):
        top[slab] = tops[slab]
        bottom[slab] = bottoms[slab]
        lat1[slab] = jnp.where(j == 0, tops[slab], bottoms[slab])

    def sides(out, east, tail):
        a, b, c = (rows - 3, rows - 3, rows - 2) if east else (0, 0, 0)
        for k in range(levels):
            out[k, 0:3] = t[k, a : a + 3]
            out[k, 3:6] = s[k, a : a + 3]
            out[k, 6:9] = u[k, a : a + 3]
            out[k, 9:11] = v[k, c : c + 2]
            if k < levels - 1:
                out[k, 11:13] = w[k, c : c + 2]
            else:
                out[k, 11:13] = jnp.zeros((2, lanes), F32)
            out[k, 13:16] = wets[k][b : b + 3]
        edges(out.at[levels], east)
        if tail is not None:
            edges(tail, east)

    def edges(out, east):
        a = rows - 3 if east else 0
        for n, x in enumerate(tops + (bottoms if out.shape[0] > 8 else [])):
            out[3 * n : 3 * n + 3] = x[a : a + 3]

    @pl.when(even)
    def _():
        sides(core, True, None)
        sides(chip, False, chip1)

    @pl.when(jnp.logical_not(even))
    def _():
        sides(core, False, None)
        sides(chip, True, chip1)


def repack(top, core, chip1, lat1, packed, chip, core2, fold):
    i, j = place()
    even = lax.rem(i, 2) == 0
    levels = core.shape[0] - 1
    base = levels + 1
    rows, lanes = top.shape[1:]
    for slab in range(2):
        fold[slab] = jnp.zeros((rows + 8, lanes), F32)
        fold[slab, 4 : 4 + rows] = top[slab]
    chip[base] = jnp.zeros((rows, lanes), F32)
    core2[...] = jnp.zeros(core2.shape, F32)

    def fill(even):
        for slab in range(2):
            near, far = core[levels, 3 * slab : 3 * slab + 3], chip1[3 * slab : 3 * slab + 3]
            east, west = (near, far) if even else (far, near)
            fold[slab, 1:4] = west
            fold[slab, rows + 4 : rows + 7] = east
            a, b = (rows - 3, 0) if even else (0, rows - 3)
            core2[3 * slab : 3 * slab + 3] = lat1[slab, a : a + 3]
            chip[base, 3 * slab : 3 * slab + 3] = lat1[slab, b : b + 3]

    @pl.when(even)
    def _():
        fill(True)

    @pl.when(jnp.logical_not(even))
    def _():
        fill(False)

    for slab in range(2):
        for part in range(3):
            piece = fold[slab, 8 * part : 8 * part + 8]
            at = slab * 24 + 8 * part
            chip[base + 1 + at // 16, at % 16 : at % 16 + 8] = piece


def prepare(t, s, u, v, w, dc, flag, depth, number, inverse, ct, cs, cu, cv, cw, cm):
    levels, rows, lanes = t.shape
    flags, depths = flag[...], depth[...]
    zero = jnp.zeros(flags.shape, F32)
    q = [zero]
    for k in range(1, levels):
        q.append(dc[k - 1] * wet_of(flags, depths, k))
    q.append(zero)
    ratio = zero
    for k in range(levels):
        denom = 1.0 + q[k] + q[k + 1] - q[k] * ratio
        inv = 1.0 / denom
        ratio = q[k + 1] * inv
        number[k] = q[k]
        inverse[k] = inv
    for ref in (ct, cs, cu, cv, cw, cm):
        for k in (0, levels + 1):
            ref[k] = jnp.zeros(ref.shape[1:], F32)
    for k in range(levels):
        ct[k + 1, OWN : OWN + rows] = t[k]
        cs[k + 1, OWN : OWN + rows] = s[k]
        cu[k + 1, OWN : OWN + rows] = u[k]
        cv[k + 1, OWN : OWN + rows] = v[k]
        cw[k + 1, OWN : OWN + rows] = w[k] if k < levels - 1 else zero
        cm[k + 1, OWN : OWN + rows] = wet_of(flags, depths, k)


def step(
    ct_in, cs_in, cu_in, cv_in, cw_in, cm_in, number, inverse, core, chip, core2, fold, lat1, top, bottom,
    new_t, new_s, ct, cs, cu, cv, cw, cm,
    mirror, edge,
    low_t, low_s, ae_t, ae_s, an_t, an_s, au_t, au_s, hi_t, hi_s, lo_t, lo_s, up_t, up_s, dn_t, dn_s, fe_t, fe_s,
    fn_t, fn_s,
):
    i, j = place()
    n_lon, n_lat = lax.axis_size("lon"), lax.axis_size("lat")
    even = lax.rem(i, 2) == 0
    first, last, is_top, is_low = i == 0, i == n_lon - 1, j == n_lat - 1, j == 0
    levels, rows, lanes = number.shape
    wide = rows + 8
    lane = lax.broadcasted_iota(jnp.int32, (wide, lanes), 1)
    spot = lane & 7
    cells = (ct, cs, cu, cv, cw, cm)
    north, south = levels + 2, levels + 3
    here = pl.ds(8, wide)
    to_east = pl.ds(9, wide)
    to_west = pl.ds(7, wide)

    for slab in range(2):
        edge[slab, 4 : 4 + rows] = top[slab]
        edge[2 + slab, 4 : 4 + rows] = bottom[slab]
        edge[4 + slab, 4 : 4 + rows] = lat1[slab]
        for part in range(3):
            at = slab * 24 + 8 * part
            wrapped = chip[levels + 2 + at // 16, at % 16 : at % 16 + 8]
            edge[6 + slab, 8 * part : 8 * part + 8] = jnp.where(
                first | last, wrapped, fold[slab, 8 * part : 8 * part + 8]
            )

    def fill(even):
        for src, src2, east in ((core, core2, even), (chip, chip.at[levels + 1], not even)):
            a = OWN + rows if east else OWN - 3
            b = OWN + rows if east else OWN - 2
            for k in range(levels):
                ct[k + 1, a : a + 3] = src[k, 0:3]
                cs[k + 1, a : a + 3] = src[k, 3:6]
                cu[k + 1, a : a + 3] = src[k, 6:9]
                cv[k + 1, b : b + 2] = src[k, 9:11]
                cw[k + 1, b : b + 2] = src[k, 11:13]
                cm[k + 1, a : a + 3] = src[k, 13:16]
            a -= 8
            for n in range(4):
                edge[n, a : a + 3] = src[levels, 3 * n : 3 * n + 3]
            for n in range(2):
                edge[4 + n, a : a + 3] = src2[3 * n : 3 * n + 3]

    @pl.when(even)
    def _():
        fill(True)

    @pl.when(jnp.logical_not(even))
    def _():
        fill(False)

    @pl.when(first)
    def _():
        for slab in range(2):
            edge[6 + slab, rows + 4 : rows + 7] = top[slab, 0:3]

    @pl.when(last)
    def _():
        for slab in range(2):
            edge[6 + slab, 1:4] = top[slab, rows - 3 : rows]

    for slab in range(2):
        for r in range(wide):
            q = wide - 1 - r
            mirror[slab, r : r + 1] = edge[6 + slab, q : q + 1]

    own_n = (edge[0], edge[1])
    own_s = (edge[2], edge[3])
    other = (edge[4], edge[5])
    mir = (mirror[0], mirror[1])

    def pick(pairs):
        out = jnp.zeros((wide, lanes), F32)
        for at, value in pairs:
            out = jnp.where(spot == at, value, out)
        return out

    def mirrored(name):
        _, slab, start, count = next(x for x in SPOTS if x[0] == name)
        x = mir[slab]
        if name == "u":
            x = -roll(x, -1, 0)
            return pick([(3 + d, roll(x, 3 + d - (start + 1 - d), 1)) for d in range(2)])
        if name == "v":
            return pick([(3 + d, -roll(x, 3 + d - (start + 1 - d), 1)) for d in range(2)])
        last_one = start + count - 1
        return pick([(3 + d, roll(x, 3 + d - (last_one - d), 1)) for d in range(count)])

    cut = spot > 5
    for ref, (name, slab, start, count) in zip(cells, SPOTS):
        lead = 3 - count
        head = roll(own_n[slab], lead - start, 1)
        if name == "v":
            folded = 0.5 * (head - mir[slab])
            head = jnp.where((spot == 2) & is_top, folded, head)
        beyond = jnp.where(is_top, mirrored(name), roll(other[slab], 3 - start, 1))
        value_n = jnp.where(spot < 3, head, beyond)
        before = roll(other[slab], lead - start, 1)
        tail = roll(own_s[slab], 3 - start, 1)
        if name == "m":
            before = jnp.where(is_low, 0.0, before)
        value_s = jnp.where(spot < 3, before, tail)
        if name == "m":
            value_n = jnp.where(cut, 0.0, value_n)
            value_s = jnp.where(cut, 0.0, value_s)
        ref[north, here] = value_n
        ref[south, here] = value_s

    def at_n(ref, k, strip):
        if strip:
            return roll(ref[k, here], -1, 1)
        beyond = roll(ref[north, here], 8 * (levels - k) + 4, 1)
        return jnp.where(lane == lanes - 1, beyond, roll(ref[k, here], -1, 1))

    def at_s(ref, k, strip, value=None):
        value = ref[k, here] if value is None else value
        if strip:
            return roll(value, 1, 1)
        before = roll(ref[south, here], 8 * (levels - k) + 6, 1)
        return jnp.where(lane == 0, before, roll(value, 1, 1))

    lowest = lane >= 8 * (levels - 1)
    highest = lane < 8

    def below(ref, k, strip, edge_value=None):
        if not strip:
            return ref[k + 1, here]
        x = roll(ref[k, here], -8, 1)
        return x if edge_value is None else jnp.where(lowest, edge_value, x)

    def above(ref, k, strip, edge_value=None):
        if not strip:
            return ref[k - 1, here]
        x = roll(ref[k, here], 8, 1)
        return x if edge_value is None else jnp.where(highest, edge_value, x)

    tracers = (
        (ct, low_t, ae_t, an_t, au_t, hi_t, lo_t, up_t, dn_t, fe_t, fn_t),
        (cs, low_s, ae_s, an_s, au_s, hi_s, lo_s, up_s, dn_s, fe_s, fn_s),
    )
    nothing = jnp.zeros((wide, lanes), F32)
    for c, low, ae, an, au, hi, lo, rise, drop, fe, fn in tracers:
        au[0, here] = nothing
        for k in (0, levels + 1):
            hi[k, here] = nothing - BIG
            lo[k, here] = nothing + BIG
            rise[k, here] = nothing
            drop[k, here] = nothing

    def first_pass(k, above_low, strip):
        wet = cm[k, here]
        v_here = cv[k, here]
        if not strip:
            v_edge = roll(cv[north, here], 8 * (levels - k) + 5, 1)
            v_here = jnp.where(lane == lanes - 1, v_edge, v_here)
        ue = cu[k, here] * (wet * cm[k, to_east])
        un = v_here * (wet * at_n(cm, k, strip))
        uu = cw[k, here] * (wet * below(cm, k, strip, 0.0))
        parts = [(jnp.maximum(x, 0.0), jnp.minimum(x, 0.0), 0.5 * jnp.abs(x)) for x in (ue, un, uu)]
        carry = []
        for n, (c, low, ae, an, au, hi, lo, _, _, face_e, face_n) in enumerate(tracers):
            x = c[k, here]

            def fluxes(part, a, b):
                return part[0] * a + part[1] * b, part[2] * (b - a)

            fe, anti_e = fluxes(parts[0], x, c[k, to_east])
            fn, anti_n = fluxes(parts[1], x, at_n(c, k, strip))
            fu, anti_u = fluxes(parts[2], below(c, k, strip), x)
            ae[k, here] = anti_e
            an[k, here] = anti_n
            au[k, here] = anti_u
            face_e[k, here] = fe
            if strip:
                face_n[k, here] = fn
                over = jnp.where(highest, 0.0, roll(fu, 8, 1))
            else:
                over = above_low[n]
            out = (fe - face_e[k, to_west]) + (fn - at_s(face_n, k, strip, fn)) + (over - fu)
            carry.append(fu)
            lowered = x - out
            low[k, here] = lowered
            dry = wet == 0.0
            hi[k, here] = jnp.where(dry, -BIG, jnp.maximum(x, lowered))
            lo[k, here] = jnp.where(dry, BIG, jnp.minimum(x, lowered))
        return tuple(carry)

    for k in (north, south):
        first_pass(k, None, True)
    lax.fori_loop(1, levels + 1, lambda k, x: first_pass(k, x, False), (nothing, nothing), unroll=UNROLL[0])

    def second_pass(k, strip):
        for c, low, ae, an, au, hi, lo, rise, drop, _, _ in tracers:
            top_value, low_value = hi[k, here], lo[k, here]
            for x in (hi[k, to_east], hi[k, to_west], at_n(hi, k, strip), at_s(hi, k, strip),
                      below(hi, k, strip, -BIG), above(hi, k, strip, -BIG)):
                top_value = jnp.maximum(top_value, x)
            for x in (lo[k, to_east], lo[k, to_west], at_n(lo, k, strip), at_s(lo, k, strip),
                      below(lo, k, strip, BIG), above(lo, k, strip, BIG)):
                low_value = jnp.minimum(low_value, x)
            outward = (ae[k, here], an[k, here], above(au, k, strip, 0.0))
            inward = (ae[k, to_west], at_s(an, k, strip), au[k, here])
            gain = sum(jnp.maximum(x, 0.0) for x in inward) - sum(jnp.minimum(x, 0.0) for x in outward)
            loss = sum(jnp.maximum(x, 0.0) for x in outward) - sum(jnp.minimum(x, 0.0) for x in inward)
            lowered = low[k, here]
            rise[k, here] = jnp.minimum(1.0, (top_value - lowered) / jnp.maximum(gain, FLUX_FLOOR))
            drop[k, here] = jnp.minimum(1.0, (lowered - low_value) / jnp.maximum(loss, FLUX_FLOOR))

    for k in (north, south):
        second_pass(k, True)

    def second_body(k, x):
        second_pass(k, False)
        return x

    lax.fori_loop(1, levels + 1, second_body, 0, unroll=UNROLL[1])

    def limited(anti, rise_a, drop_a, rise_b, drop_b):
        return anti * jnp.where(anti >= 0.0, jnp.minimum(rise_b, drop_a), jnp.minimum(rise_a, drop_b))

    for c, low, ae, an, au, hi, lo, rise, drop, face_e, face_n in tracers:
        k = south
        face_n[k, here] = limited(
            an[k, here], rise[k, here], drop[k, here], at_n(rise, k, True), at_n(drop, k, True)
        )

    def third_pass(k, carry):
        above_flux, values = carry[0:2], carry[2:4]
        fluxes, solved = [], []
        q, inv = number[k - 1], inverse[k - 1]
        for n, (c, low, ae, an, au, hi, lo, rise, drop, face_e, face_n) in enumerate(tracers):
            r, d = rise[k, here], drop[k, here]
            fe = limited(ae[k, here], r, d, rise[k, to_east], drop[k, to_east])
            fn = limited(an[k, here], r, d, at_n(rise, k, False), at_n(drop, k, False))
            fu = limited(au[k, here], rise[k + 1, here], drop[k + 1, here], r, d)
            face_e[k, here] = fe
            out = (fe - face_e[k, to_west]) + (fn - at_s(face_n, k, False, fn)) + (above_flux[n] - fu)
            fluxes.append(fu)
            hi[k, here] = low[k, here] - out
            x = hi[k, OWN : OWN + rows] + q * values[n]
            x = x * inv
            lo[k, 0:rows] = x
            solved.append(x)
        return tuple(fluxes) + tuple(solved)

    no_rows = jnp.zeros((rows, lanes), F32)
    carry = lax.fori_loop(1, levels + 1, third_pass, (nothing, nothing, no_rows, no_rows), unroll=UNROLL[2])
    solved = list(carry[2:4])
    new_t[levels - 1] = solved[0]
    new_s[levels - 1] = solved[1]
    for k in range(levels - 2, -1, -1):
        ratio = number[k + 1] * inverse[k]
        for n, out in enumerate((new_t, new_s)):
            solved[n] = tracers[n][6][k + 1, 0:rows] + ratio * solved[n]
            out[k] = solved[n]


def call(body, outs, args, scratch=(), aliases=None, limit=8, where=pltpu.VMEM):
    vmem = pl.BlockSpec(memory_space=pltpu.VMEM)
    outs = [x if hasattr(x, "dtype") else jax.ShapeDtypeStruct(x, F32) for x in outs]
    return pl.pallas_call(
        body,
        out_shape=tuple(outs),
        in_specs=[pl.BlockSpec(memory_space=where)] * len(args),
        out_specs=tuple(vmem for _ in outs),
        scratch_shapes=[x if not isinstance(x, tuple) else pltpu.VMEM(x, F32) for x in scratch],
        input_output_aliases=aliases or {},
        compiler_params=pltpu.CompilerParams(vmem_limit_bytes=limit * 2**20),
        cost_estimate=pl.CostEstimate(flops=2_000_000, bytes_accessed=2_000_000, transcendentals=0),
    )(*args)


def local(n_lon, n_lat, *args):
    levels, rows, lanes = args[0].shape
    wide = rows + 8

    def number(i, j):
        return (i % n_lon) * n_lat + j

    grid = [(i, j) for i in range(n_lon) for j in range(n_lat)]

    def beside(i):
        return i - 1 if i % 2 == 0 else i + 1

    cores = [(number(i, j), number(i ^ 1, j)) for i, j in grid]
    chips = [(number(i, j), number(beside(i), j)) for i, j in grid]
    inner = [(number(i, j), number(beside(i), j)) for i, j in grid if 0 <= beside(i) < n_lon]
    lats = [(number(i, j), number(i, n_lat - 1 - j)) for i, j in grid]
    folds = [(number(i, n_lat - 1), number(n_lon - 1 - i, n_lat - 1)) for i in range(1, n_lon - 1)]

    core, chip, chip1, lat1, top, bottom, *held = call(
        pack,
        [(levels + 1, rows, lanes), (levels + 5, rows, lanes), (8, lanes)]
        + [(2, rows, lanes)] * 3
        + [jax.ShapeDtypeStruct(x.shape, x.dtype) for x in args],
        [pltpu.with_memory_space_constraint(x, pltpu.HBM) for x in args],
        [pltpu.SemaphoreType.DMA((len(args),))],
        where=pltpu.HBM,
    )
    chip1_in = lax.ppermute(chip1, AXES, inner)
    lat1_in = lax.ppermute(lat1, AXES, lats)
    core_in = lax.ppermute(core, AXES, cores)
    numbers, inverse, *cells = call(
        prepare, [(levels, rows, lanes)] * 2 + [(levels + 4, 40, lanes)] * 6, held
    )
    chip, core2, fold = call(
        repack,
        [chip.shape, (8, lanes), (2, wide, lanes)],
        (top, core_in, chip1_in, lat1_in, chip),
        aliases={4: 0},
        limit=2,
    )
    chip_in = lax.ppermute(chip, AXES, chips)
    fold_in = lax.ppermute(fold, AXES, folds)
    core2_in = lax.ppermute(core2, AXES, cores)
    cell = (levels + 4, 40, lanes)
    return call(
        step,
        [(levels, rows, lanes)] * 2 + [cell] * 6,
        (*cells, numbers, inverse, core_in, chip_in, core2_in, fold_in, lat1_in, top, bottom),
        [(2, wide, lanes), (8, wide, lanes)] + [cell] * 20,
        aliases={n: 2 + n for n in range(6)},
        limit=24,
    )[:2]


def solution(mesh):
    n_lon, n_lat = mesh.shape["lon"], mesh.shape["lat"]
    cube = P(None, "lon", "lat")
    plane = P("lon", "lat")
    return jax.shard_map(
        lambda *args: tuple(local(n_lon, n_lat, *args)),
        mesh=mesh,
        in_specs=(cube,) * 6 + (plane,) * 2,
        out_specs=(cube, cube),
        check_vma=False,
    )
```

```python
import jax
import jax.numpy as jnp
from jax import lax
from jax.experimental import pallas as pl
from jax.experimental.pallas import tpu as pltpu
from jax.sharding import PartitionSpec as P


FLUX_FLOOR = 0.01
BIG = 1e30
AXES = ("lon", "lat")
F32 = jnp.float32


SPOTS = (("t", 0, 3), ("s", 3, 3), ("u", 6, 2), ("v", 8, 3), ("w", 11, 2), ("m", 13, 3))
OWN = 12
UNROLL = (4, 4, 4)


def roll(x, shift, axis):
    if not isinstance(shift, int):
        return pltpu.roll(x, shift, axis)
    shift = shift % x.shape[axis]
    return x if shift == 0 else pltpu.roll(x, shift, axis)


def position():
    return lax.axis_index("lon"), lax.axis_index("lat")


def by_parity(body):
    even = lax.rem(lax.axis_index("lon"), 2) == 0

    @pl.when(even)
    def _():
        body(True)

    @pl.when(jnp.logical_not(even))
    def _():
        body(False)


def lanes_of(rows, lanes):
    lane = lax.broadcasted_iota(jnp.int32, (rows, lanes), 1)
    return lane, lane >> 4, lane & 15


def wet_of(flag, depth, level):
    return jnp.where((level < depth) & (flag > 0), 1.0, 0.0).astype(F32)


def pack(
    t_any, s_any, u_any, v_any, w_any, dc_any, flag_any, depth_any,
    core, chip, chip1, diag1, lat1, top, own, t, s, u, v, w, dc, flag, depth, sems,
):
    sources = (flag_any, depth_any, t_any, s_any, u_any, v_any, w_any, dc_any)
    targets = (flag, depth, t, s, u, v, w, dc)
    copies = [pltpu.make_async_copy(x, y, sems.at[n]) for n, (x, y) in enumerate(zip(sources, targets))]
    for copy in copies:
        copy.start()
    levels, rows, lanes = t.shape
    _, j = position()
    _, group, spot = lanes_of(rows, lanes)
    zero = jnp.zeros((rows, lanes), F32)
    core[levels] = zero
    chip1[...] = jnp.zeros(chip1.shape, F32)
    diag1[...] = jnp.zeros(diag1.shape, F32)
    for copy in copies:
        copy.wait()
    flags, depths = flag[...], depth[...]
    fields = dict(t=t, s=s, u=u, v=v, w=w)
    held = {}
    for n, (name, _, _) in enumerate(SPOTS):
        for parity in range(2):
            out = zero
            for g in range(levels // 2):
                k = 2 * g + parity
                if name == "w" and k == levels - 1:
                    continue
                x = wet_of(flags, depths, k) if name == "m" else fields[name][k]
                out = jnp.where(group == g, roll(x, 16 * g + 6, 1), out)
            own[n, parity] = out
            held[name, parity] = out
    tops, afar = [], []
    for parity in range(2):
        up, down = zero, zero
        for name, start, count in SPOTS:
            mine = (spot >= start) & (spot < start + count)
            up = jnp.where(mine, roll(held[name, parity], start - (6 - count), 1), up)
            down = jnp.where(mine, roll(held[name, parity], start - 6, 1), down)
        top[parity] = up
        afar.append(jnp.where(j == 0, up, down))
        lat1[parity] = afar[parity]
        tops.append(up)

    def sides(out, east):
        a, c = (rows - 3, rows - 2) if east else (0, 0)
        for k in range(levels):
            out[k, 0:3] = t[k, a : a + 3]
            out[k, 3:6] = s[k, a : a + 3]
            out[k, 6:9] = u[k, a : a + 3]
            out[k, 9:11] = v[k, c : c + 2]
            if k < levels - 1:
                out[k, 11:13] = w[k, c : c + 2]
            else:
                out[k, 11:13] = jnp.zeros((2, lanes), F32)
            out[k, 13:16] = wet_of(flags, depths, k)[a : a + 3]

    def fill(even):
        sides(core, even)
        sides(chip, not even)
        for out, east, edges in ((core.at[levels], even, tops), (chip1, not even, tops), (diag1, not even, afar)):
            a = rows - 3 if east else 0
            for n, x in enumerate(edges):
                out[3 * n : 3 * n + 3] = x[a : a + 3]

    by_parity(fill)


def repack(top, core, chip1, lat1, core2, fold):
    levels = core.shape[0] - 1
    rows, _ = top.shape[1:]
    wide = rows + 8
    fold[...] = jnp.zeros(fold.shape, F32)
    core2[...] = jnp.zeros(core2.shape, F32)
    for parity in range(2):
        fold[wide * parity + 4 : wide * parity + 4 + rows] = top[parity]

    def fill(even):
        for parity in range(2):
            near, far = core[levels, 3 * parity : 3 * parity + 3], chip1[3 * parity : 3 * parity + 3]
            east, west = (near, far) if even else (far, near)
            at = wide * parity
            fold[at + 1 : at + 4] = west
            fold[at + rows + 4 : at + rows + 7] = east
            a, b = (rows - 3, 0) if even else (0, rows - 3)
            core2[3 * parity : 3 * parity + 3] = lat1[parity, a : a + 3]
            at = 2 * wide + 3 * parity
            fold[at : at + 3] = lat1[parity, b : b + 3]

    by_parity(fill)


def prepare(t, s, u, v, w, dc, flag, depth, number, inverse, ct, cs, cu, cv, cw, cm):
    levels, rows, _ = t.shape
    flags, depths = flag[...], depth[...]
    zero = jnp.zeros(flags.shape, F32)
    q = [zero]
    for k in range(1, levels):
        q.append(dc[k - 1] * wet_of(flags, depths, k))
    q.append(zero)
    ratio = zero
    for k in range(levels):
        denom = 1.0 + q[k] + q[k + 1] - q[k] * ratio
        inv = 1.0 / denom
        ratio = q[k + 1] * inv
        number[k] = q[k]
        inverse[k] = inv
    for ref in (ct, cs, cu, cv, cw, cm):
        for k in (0, levels + 1):
            ref[k] = jnp.zeros(ref.shape[1:], F32)
    for k in range(levels):
        ct[k + 1, OWN : OWN + rows] = t[k]
        cs[k + 1, OWN : OWN + rows] = s[k]
        cu[k + 1, OWN : OWN + rows] = u[k]
        cv[k + 1, OWN : OWN + rows] = v[k]
        cw[k + 1, OWN : OWN + rows] = w[k] if k < levels - 1 else zero
        cm[k + 1, OWN : OWN + rows] = wet_of(flags, depths, k)


def low_and_anti(speed):
    parts = jnp.maximum(speed, 0.0), jnp.minimum(speed, 0.0), 0.5 * jnp.abs(speed)
    return lambda a, b: (parts[0] * a + parts[1] * b, parts[2] * (b - a))


def limited(anti, rise_a, drop_a, rise_b, drop_b):
    return anti * jnp.where(anti >= 0.0, jnp.minimum(rise_b, drop_a), jnp.minimum(rise_a, drop_b))


def ratios(lowered, top_value, low_value, inward, outward):
    gain = sum(jnp.maximum(x, 0.0) for x in inward) - sum(jnp.minimum(x, 0.0) for x in outward)
    loss = gain + (sum(outward) - sum(inward))
    rise = jnp.minimum(1.0, (top_value - lowered) / jnp.maximum(gain, FLUX_FLOOR))
    drop = jnp.minimum(1.0, (lowered - low_value) / jnp.maximum(loss, FLUX_FLOOR))
    return rise, drop


def main(
    ct_in, cs_in, cu_in, cv_in, cw_in, cm_in, core, chip,
    adv_t, adv_s, sides, ct, cs, cu, cv, cw, cm,
    low_t, low_s, ae_t, ae_s, an_t, an_s, au_t, au_s, hi_t, hi_s, lo_t, lo_s, up_t, up_s, dn_t, dn_s, fe_t, fe_s,
):
    levels, rows, lanes = adv_t.shape
    wide = rows + 8
    here, to_east, to_west = pl.ds(8, wide), pl.ds(9, wide), pl.ds(7, wide)
    inner = pl.ds(OWN, rows)

    def fill(even):
        for src, east in ((core, even), (chip, not even)):
            a = OWN + rows if east else OWN - 3
            b = OWN + rows if east else OWN - 2
            for k in range(levels):
                ct[k + 1, a : a + 3] = src[k, 0:3]
                cs[k + 1, a : a + 3] = src[k, 3:6]
                cu[k + 1, a : a + 3] = src[k, 6:9]
                cv[k + 1, b : b + 2] = src[k, 9:11]
                cw[k + 1, b : b + 2] = src[k, 11:13]
                cm[k + 1, a : a + 3] = src[k, 13:16]

    by_parity(fill)

    tracers = (
        (ct, low_t, ae_t, an_t, au_t, hi_t, lo_t, up_t, dn_t, fe_t, adv_t),
        (cs, low_s, ae_s, an_s, au_s, hi_s, lo_s, up_s, dn_s, fe_s, adv_s),
    )
    nothing = jnp.zeros((wide, lanes), F32)
    for _, low, ae, an, au, hi, lo, rise, drop, _, _ in tracers:
        au[0, here] = nothing
        for k in (0, levels + 1):
            hi[k, here] = nothing - BIG
            lo[k, here] = nothing + BIG
            rise[k, here] = nothing
            drop[k, here] = nothing

    def first_pass(k, carry):
        wet = cm[k, here]
        east = low_and_anti(cu[k, here] * (wet * cm[k, to_east]))
        north = low_and_anti(cv[k, here] * (wet * roll(wet, -1, 1)))
        upward = low_and_anti(cw[k, here] * (wet * cm[k + 1, here]))
        fluxes = []
        for n, (c, low, ae, an, au, hi, lo, _, _, face, _) in enumerate(tracers):
            x = c[k, here]
            fe, ae[k, here] = east(x, c[k, to_east])
            fn, an[k, here] = north(x, roll(x, -1, 1))
            fu, au[k, here] = upward(c[k + 1, here], x)
            face[k, here] = fe
            fluxes.append(fu)
            lowered = x - ((fe - face[k, to_west]) + (fn - roll(fn, 1, 1)) + (carry[n] - fu))
            low[k, here] = lowered
            dry = wet == 0.0
            hi[k, here] = jnp.where(dry, -BIG, jnp.maximum(x, lowered))
            lo[k, here] = jnp.where(dry, BIG, jnp.minimum(x, lowered))
        return tuple(fluxes)

    lax.fori_loop(1, levels + 1, first_pass, (nothing, nothing), unroll=UNROLL[0])

    def second_pass(k, carry):
        for _, low, ae, an, au, hi, lo, rise, drop, _, _ in tracers:
            top_value, low_value = hi[k, here], lo[k, here]
            for x in (hi[k, to_east], hi[k, to_west], roll(top_value, -1, 1), roll(top_value, 1, 1),
                      hi[k + 1, here], hi[k - 1, here]):
                top_value = jnp.maximum(top_value, x)
            for x in (lo[k, to_east], lo[k, to_west], roll(low_value, -1, 1), roll(low_value, 1, 1),
                      lo[k + 1, here], lo[k - 1, here]):
                low_value = jnp.minimum(low_value, x)
            anti_n = an[k, here]
            rise[k, here], drop[k, here] = ratios(
                low[k, here], top_value, low_value,
                (ae[k, to_west], roll(anti_n, 1, 1), au[k, here]), (ae[k, here], anti_n, au[k - 1, here]),
            )
        return carry

    lax.fori_loop(1, levels + 1, second_pass, 0, unroll=UNROLL[1])

    def third_pass(k, carry):
        fluxes = []
        for n, (_, low, ae, an, au, _, _, rise, drop, face, adv) in enumerate(tracers):
            r, d = rise[k, here], drop[k, here]
            fe = limited(ae[k, here], r, d, rise[k, to_east], drop[k, to_east])
            face[k, here] = fe
            r, d = rise[k, inner], drop[k, inner]
            fn = limited(an[k, inner], r, d, roll(r, -1, 1), roll(d, -1, 1))
            fu = limited(au[k, inner], rise[k + 1, inner], drop[k + 1, inner], r, d)
            fluxes.append(fu)
            out = (face[k, inner] - face[k, pl.ds(OWN - 1, rows)]) + (fn - roll(fn, 1, 1)) + (carry[n] - fu)
            adv[k - 1] = low[k, inner] - out
        return tuple(fluxes)

    no_flux = jnp.zeros((rows, lanes), F32)
    lax.fori_loop(1, levels + 1, third_pass, (no_flux, no_flux), unroll=UNROLL[2])

    _, group, _ = lanes_of(rows, lanes)
    for n, src in enumerate((core, chip)):
        for parity in range(2):
            out = no_flux
            for g in range(levels // 2):
                out = jnp.where(group == g, roll(src[2 * g + parity], 16 * g + 6, 1), out)
            sides[n, parity] = out


def finish(
    adv_t, adv_s, number, inverse, own, sides, top, lat1, core2, diag1, fold,
    new_t, new_s,
    ct, cs, cu, cv, cw, cm, edge, mirror,
    low_t, low_s, ae_t, ae_s, an_t, an_s, au_t, au_s, hi_t, hi_s, lo_t, lo_s, up_t, up_s, dn_t, dn_s, fe_t, fe_s,
):
    i, j = position()
    n_lon, n_lat = lax.axis_size("lon"), lax.axis_size("lat")
    first, last, is_top, is_low = i == 0, i == n_lon - 1, j == n_lat - 1, j == 0
    levels, rows, lanes = adv_t.shape
    wide = rows + 8
    _, group, spot = lanes_of(wide, lanes)
    here, to_east, to_west = pl.ds(8, wide), pl.ds(9, wide), pl.ds(7, wide)
    cells = (ct, cs, cu, cv, cw, cm)
    starts = (0, 3, 6, 9, 11, 13)
    counts = (3, 3, 3, 2, 2, 3)

    for n, ref in enumerate(cells):
        for parity in range(2):
            ref[2 + parity, OWN : OWN + rows] = own[n, parity]
    for parity in range(2):
        edge[parity, 4 : 4 + rows] = lat1[parity]
        edge[2 + parity] = fold[wide * parity : wide * parity + wide]

    def fill(even):
        for n, (src, east) in enumerate(((core2, even), (diag1, not even))):
            for ref, start, count in zip(cells, starts, counts):
                a = OWN + rows if east else OWN - count
                for parity in range(2):
                    ref[2 + parity, a : a + count] = sides[n, parity, start : start + count]
            a = 4 + rows if east else 1
            for parity in range(2):
                edge[parity, a : a + 3] = src[3 * parity : 3 * parity + 3]

    by_parity(fill)

    @pl.when(first)
    def _():
        for parity in range(2):
            edge[parity, 1:4] = fold[2 * wide + 3 * parity : 2 * wide + 3 * parity + 3]
            edge[2 + parity, rows + 4 : rows + 7] = top[parity, 0:3]

    @pl.when(last)
    def _():
        for parity in range(2):
            edge[parity, rows + 4 : rows + 7] = fold[2 * wide + 3 * parity : 2 * wide + 3 * parity + 3]
            edge[2 + parity, 1:4] = top[parity, rows - 3 : rows]

    for parity in range(2):
        for r in range(wide):
            q = wide - 1 - r
            mirror[parity, r : r + 1] = edge[2 + parity, q : q + 1]

    for parity in range(2):
        other, mir = edge[parity], mirror[parity]
        for ref, (name, start, count) in zip(cells, SPOTS):
            mine = ref[2 + parity, here]
            source = mir
            if name == "u":
                source = -roll(mir, -1, 0)
            if name == "v":
                source = -mir
            beyond = roll(other, 6 - start, 1)
            lead = start + 1 if name == "v" else start + count - 1
            for d in range(2 if name == "v" else count):
                beyond = jnp.where((spot == 6 + d) & is_top, roll(source, 6 + d - (lead - d), 1), beyond)
            value_n = jnp.where(spot < 6, mine, beyond)
            if name == "v":
                folded = 0.5 * (mine + roll(source, 5 - (start + 2), 1))
                value_n = jnp.where((spot == 5) & is_top, folded, value_n)
            value_s = jnp.where(spot < 6, roll(other, 6 - count - start, 1), mine)
            if name == "m":
                value_n = jnp.where(spot > 8, 0.0, value_n)
                value_s = jnp.where((spot < 3) | (spot > 11) | ((spot < 6) & is_low), 0.0, value_s)
            ref[parity, here] = value_n
            ref[2 + parity, here] = value_s

    lowest = group == levels // 2 - 1
    highest = group == 0

    def below(ref, k, edge_value=None):
        if k % 2 == 0:
            return ref[k + 1, here]
        x = roll(ref[k - 1, here], -16, 1)
        return x if edge_value is None else jnp.where(lowest, edge_value, x)

    def above(ref, k, edge_value):
        if k % 2 == 1:
            return ref[k - 1, here]
        return jnp.where(highest, edge_value, roll(ref[k + 1, here], 16, 1))

    tracers = (
        (ct, low_t, ae_t, an_t, au_t, hi_t, lo_t, up_t, dn_t, fe_t),
        (cs, low_s, ae_s, an_s, au_s, hi_s, lo_s, up_s, dn_s, fe_s),
    )
    for strip in (0, 2):
        ends = (strip, strip + 1)
        tops = [[None, None], [None, None]]
        for k in ends:
            wet = cm[k, here]
            east = low_and_anti(cu[k, here] * (wet * cm[k, to_east]))
            north = low_and_anti(cv[k, here] * (wet * roll(wet, -1, 1)))
            upward = low_and_anti(cw[k, here] * (wet * below(cm, k, 0.0)))
            for n, (c, low, ae, an, au, hi, lo, _, _, face) in enumerate(tracers):
                x = c[k, here]
                fe, ae[k, here] = east(x, c[k, to_east])
                fn, an[k, here] = north(x, roll(x, -1, 1))
                fu, au[k, here] = upward(below(c, k), x)
                face[k, here] = fe
                tops[n][k % 2] = fu
                low[k, here] = x - ((fe - face[k, to_west]) + (fn - roll(fn, 1, 1)) - fu)
        for k in ends:
            dry = cm[k, here] == 0.0
            for n, (c, low, ae, an, au, hi, lo, _, _, _) in enumerate(tracers):
                over = tops[n][0] if k % 2 == 1 else jnp.where(highest, 0.0, roll(tops[n][1], 16, 1))
                x, lowered = c[k, here], low[k, here] - over
                low[k, here] = lowered
                hi[k, here] = jnp.where(dry, -BIG, jnp.maximum(x, lowered))
                lo[k, here] = jnp.where(dry, BIG, jnp.minimum(x, lowered))
        for k in ends:
            for _, low, ae, an, au, hi, lo, rise, drop, _ in tracers:
                top_value, low_value = hi[k, here], lo[k, here]
                for x in (hi[k, to_east], hi[k, to_west], roll(top_value, -1, 1), roll(top_value, 1, 1),
                          below(hi, k, -BIG), above(hi, k, -BIG)):
                    top_value = jnp.maximum(top_value, x)
                for x in (lo[k, to_east], lo[k, to_west], roll(low_value, -1, 1), roll(low_value, 1, 1),
                          below(lo, k, BIG), above(lo, k, BIG)):
                    low_value = jnp.minimum(low_value, x)
                anti_n = an[k, here]
                rise[k, here], drop[k, here] = ratios(
                    low[k, here], top_value, low_value,
                    (ae[k, to_west], roll(anti_n, 1, 1), au[k, here]), (ae[k, here], anti_n, above(au, k, 0.0)),
                )
        for k in ends:
            for _, low, ae, an, au, hi, _, rise, drop, face in tracers:
                r, d = rise[k, here], drop[k, here]
                face[k, here] = limited(ae[k, here], r, d, rise[k, to_east], drop[k, to_east])
                hi[k, here] = limited(au[k, here], below(rise, k), below(drop, k), r, d)
        for k in ends:
            for _, low, ae, an, au, hi, lo, rise, drop, face in tracers:
                r, d = rise[k, here], drop[k, here]
                fn = limited(an[k, here], r, d, roll(r, -1, 1), roll(d, -1, 1))
                out = (face[k, here] - face[k, to_west]) + (fn - roll(fn, 1, 1))
                lo[k, here] = low[k, here] - (out + (above(hi, k, 0.0) - hi[k, here]))

    _, _, place = lanes_of(rows, lanes)
    ends = []
    for tracer in tracers:
        lo = tracer[6]
        ends.append([
            jnp.where(place < 6, lo[parity, OWN : OWN + rows], lo[2 + parity, OWN : OWN + rows])
            for parity in range(2)
        ])
    lane, _, _ = lanes_of(rows, lanes)
    outer = (lane < 3) | (lane >= lanes - 3)
    solved = [None, None]
    for k in range(levels):
        q, inv = number[k], inverse[k]
        for n, adv in enumerate((adv_t, adv_s)):
            x = jnp.where(outer, roll(ends[n][k % 2], -(16 * (k // 2) + 6), 1), adv[k])
            if k > 0:
                x = x + q * solved[n]
            solved[n] = x * inv
            (new_t, new_s)[n][k] = solved[n]
    for k in range(levels - 2, -1, -1):
        ratio = number[k + 1] * inverse[k]
        for n, out in enumerate((new_t, new_s)):
            solved[n] = out[k] + ratio * solved[n]
            out[k] = solved[n]


def call(body, outs, args, scratch=(), aliases=None, limit=8, flops=2_000_000):
    vmem = pl.BlockSpec(memory_space=pltpu.VMEM)
    outs = [x if hasattr(x, "dtype") else jax.ShapeDtypeStruct(x, F32) for x in outs]
    where = pltpu.HBM if body is pack else pltpu.VMEM
    return pl.pallas_call(
        body,
        out_shape=tuple(outs),
        in_specs=[pl.BlockSpec(memory_space=where)] * len(args),
        out_specs=tuple(vmem for _ in outs),
        scratch_shapes=[x if not isinstance(x, tuple) else pltpu.VMEM(x, F32) for x in scratch],
        input_output_aliases=aliases or {},
        compiler_params=pltpu.CompilerParams(vmem_limit_bytes=limit * 2**20),
        cost_estimate=pl.CostEstimate(flops=flops, bytes_accessed=2_000_000, transcendentals=0),
    )(*args)


def local(n_lon, n_lat, *args):
    levels, rows, lanes = args[0].shape
    wide = rows + 8

    def number(i, j):
        return (i % n_lon) * n_lat + j

    grid = [(i, j) for i in range(n_lon) for j in range(n_lat)]
    north = n_lat - 1

    def beside(i):
        return i - 1 if i % 2 == 0 else i + 1

    cores = [(number(i, j), number(i ^ 1, j)) for i, j in grid]
    chips = [(number(i, j), number(beside(i), j)) for i, j in grid]
    inner = [(number(i, j), number(beside(i), j)) for i, j in grid if 0 <= beside(i) < n_lon]
    diags = [(number(i, j), number(beside(i), n_lat - 1 - j)) for i, j in grid if 0 <= beside(i) < n_lon]
    lats = [(number(i, j), number(i, n_lat - 1 - j)) for i, j in grid]
    folds = [(number(i, j), number(n_lon - 1 - i, j)) for i, j in grid if j == north or i in (0, n_lon - 1)]

    def send(x, pairs):
        return lax.ppermute(x, AXES, pairs)

    core, chip, chip1, diag1, lat1, top, own, *held = call(
        pack,
        [(levels + 1, rows, lanes), (levels, rows, lanes), (8, lanes), (8, lanes), (2, rows, lanes), (2, rows, lanes),
         (6, 2, rows, lanes)] + [jax.ShapeDtypeStruct(x.shape, x.dtype) for x in args],
        [pltpu.with_memory_space_constraint(x, pltpu.HBM) for x in args],
        [pltpu.SemaphoreType.DMA((len(args),))],
    )
    chip1_in = send(chip1, inner)
    lat1_in = send(lat1, lats)
    core_in = send(core, cores)
    diag1_in = send(diag1, diags)
    chip_in = send(chip, chips)
    cell = (levels + 2, 40, lanes)
    numbers, inverse, *cells = call(prepare, [(levels, rows, lanes)] * 2 + [cell] * 6, held)
    core2, fold = call(repack, [(8, lanes), (2 * wide + 8, lanes)], (top, core_in, chip1_in, lat1_in), limit=2)
    fold_in = send(fold, folds)
    core2_in = send(core2, cores)
    adv_t, adv_s, sides, *_ = call(
        main,
        [(levels, rows, lanes)] * 2 + [(2, 2, rows, lanes)] + [cell] * 6,
        (*cells, core_in, chip_in),
        [cell] * 18,
        aliases={n: 3 + n for n in range(6)},
        limit=20,
        flops=20_000_000,
    )
    strip = (4, 40, lanes)
    return call(
        finish,
        [(levels, rows, lanes)] * 2,
        (adv_t, adv_s, numbers, inverse, own, sides, top, lat1_in, core2_in, diag1_in, fold_in),
        [strip] * 6 + [(4, wide, lanes), (2, wide, lanes)] + [strip] * 18,
    )


def solution(mesh):
    n_lon, n_lat = mesh.shape["lon"], mesh.shape["lat"]
    cube = P(None, "lon", "lat")
    plane = P("lon", "lat")
    return jax.shard_map(
        lambda *args: tuple(local(n_lon, n_lat, *args)),
        mesh=mesh,
        in_specs=(cube,) * 6 + (plane,) * 2,
        out_specs=(cube, cube),
        check_vma=False,
    )
```

```python
import jax
import jax.numpy as jnp
from jax import lax
from jax.experimental import pallas as pl
from jax.experimental.pallas import tpu as pltpu
from jax.sharding import PartitionSpec as P


FLUX_FLOOR = 0.01
BIG = 1e30
AXES = ("lon", "lat")
F32 = jnp.float32


SPOTS = (("t", 0, 3), ("s", 3, 3), ("u", 6, 2), ("v", 8, 3), ("w", 11, 2), ("m", 13, 3))
OWN = 12
UNROLL = (4, 4, 4)


def roll(x, shift, axis):
    if not isinstance(shift, int):
        return pltpu.roll(x, shift, axis)
    shift = shift % x.shape[axis]
    return x if shift == 0 else pltpu.roll(x, shift, axis)


def position():
    return lax.axis_index("lon"), lax.axis_index("lat")


def by_parity(body):
    even = lax.rem(lax.axis_index("lon"), 2) == 0

    @pl.when(even)
    def _():
        body(True)

    @pl.when(jnp.logical_not(even))
    def _():
        body(False)


def lanes_of(rows, lanes):
    lane = lax.broadcasted_iota(jnp.int32, (rows, lanes), 1)
    return lane, lane >> 4, lane & 15


def wet_of(flag, depth, level):
    return jnp.where((level < depth) & (flag > 0), 1.0, 0.0).astype(F32)


def pack(
    t_any, s_any, u_any, v_any, w_any, dc_any, flag_any, depth_any,
    core, chip, chip1, diag1, lat1, top, own, t, s, u, v, w, dc, flag, depth, sems,
):
    sources = (flag_any, depth_any, t_any, s_any, u_any, v_any, w_any, dc_any)
    targets = (flag, depth, t, s, u, v, w, dc)
    copies = [pltpu.make_async_copy(x, y, sems.at[n]) for n, (x, y) in enumerate(zip(sources, targets))]
    for copy in copies:
        copy.start()
    levels, rows, lanes = t.shape
    _, j = position()
    _, group, spot = lanes_of(rows, lanes)
    zero = jnp.zeros((rows, lanes), F32)
    core[levels] = zero
    chip1[...] = jnp.zeros(chip1.shape, F32)
    diag1[...] = jnp.zeros(diag1.shape, F32)
    for copy in copies:
        copy.wait()
    flags, depths = flag[...], depth[...]
    fields = dict(t=t, s=s, u=u, v=v, w=w)
    held = {}
    for n, (name, _, _) in enumerate(SPOTS):
        for parity in range(2):
            out = zero
            for g in range(levels // 2):
                k = 2 * g + parity
                if name == "w" and k == levels - 1:
                    continue
                x = wet_of(flags, depths, k) if name == "m" else fields[name][k]
                out = jnp.where(group == g, roll(x, 16 * g + 6, 1), out)
            own[n, parity] = out
            held[name, parity] = out
    tops, afar = [], []
    for parity in range(2):
        up, down = zero, zero
        for name, start, count in SPOTS:
            mine = (spot >= start) & (spot < start + count)
            up = jnp.where(mine, roll(held[name, parity], start - (6 - count), 1), up)
            down = jnp.where(mine, roll(held[name, parity], start - 6, 1), down)
        top[parity] = up
        afar.append(jnp.where(j == 0, up, down))
        lat1[parity] = afar[parity]
        tops.append(up)

    def sides(out, east):
        a, c = (rows - 3, rows - 2) if east else (0, 0)
        for k in range(levels):
            out[k, 0:3] = t[k, a : a + 3]
            out[k, 3:6] = s[k, a : a + 3]
            out[k, 6:9] = u[k, a : a + 3]
            out[k, 9:11] = v[k, c : c + 2]
            if k < levels - 1:
                out[k, 11:13] = w[k, c : c + 2]
            else:
                out[k, 11:13] = jnp.zeros((2, lanes), F32)
            out[k, 13:16] = wet_of(flags, depths, k)[a : a + 3]

    def fill(even):
        sides(core, even)
        sides(chip, not even)
        for out, east, edges in ((core.at[levels], even, tops), (chip1, not even, tops), (diag1, not even, afar)):
            a = rows - 3 if east else 0
            for n, x in enumerate(edges):
                out[3 * n : 3 * n + 3] = x[a : a + 3]

    by_parity(fill)


def repack(top, core, chip1, lat1, core2, fold):
    levels = core.shape[0] - 1
    rows, _ = top.shape[1:]
    wide = rows + 8
    fold[...] = jnp.zeros(fold.shape, F32)
    core2[...] = jnp.zeros(core2.shape, F32)
    for parity in range(2):
        fold[wide * parity + 4 : wide * parity + 4 + rows] = top[parity]

    def fill(even):
        for parity in range(2):
            near, far = core[levels, 3 * parity : 3 * parity + 3], chip1[3 * parity : 3 * parity + 3]
            east, west = (near, far) if even else (far, near)
            at = wide * parity
            fold[at + 1 : at + 4] = west
            fold[at + rows + 4 : at + rows + 7] = east
            a, b = (rows - 3, 0) if even else (0, rows - 3)
            core2[3 * parity : 3 * parity + 3] = lat1[parity, a : a + 3]
            at = 2 * wide + 3 * parity
            fold[at : at + 3] = lat1[parity, b : b + 3]

    by_parity(fill)


def prepare(t, s, u, v, w, dc, flag, depth, number, inverse, ct, cs, cu, cv, cw, cm):
    levels, rows, _ = t.shape
    flags, depths = flag[...], depth[...]
    zero = jnp.zeros(flags.shape, F32)
    q = [zero]
    for k in range(1, levels):
        q.append(dc[k - 1] * wet_of(flags, depths, k))
    q.append(zero)
    ratio = zero
    for k in range(levels):
        denom = 1.0 + q[k] + q[k + 1] - q[k] * ratio
        inv = 1.0 / denom
        ratio = q[k + 1] * inv
        number[k] = q[k]
        inverse[k] = inv
    for ref in (ct, cs, cu, cv, cw, cm):
        for k in (0, levels + 1):
            ref[k] = jnp.zeros(ref.shape[1:], F32)
    for k in range(levels):
        ct[k + 1, OWN : OWN + rows] = t[k]
        cs[k + 1, OWN : OWN + rows] = s[k]
        cu[k + 1, OWN : OWN + rows] = u[k]
        cv[k + 1, OWN : OWN + rows] = v[k]
        cw[k + 1, OWN : OWN + rows] = w[k] if k < levels - 1 else zero
        cm[k + 1, OWN : OWN + rows] = wet_of(flags, depths, k)


def low_and_anti(speed):
    parts = jnp.maximum(speed, 0.0), jnp.minimum(speed, 0.0), 0.5 * jnp.abs(speed)
    return lambda a, b: (parts[0] * a + parts[1] * b, parts[2] * (b - a))


def limited(anti, rise_a, drop_a, rise_b, drop_b):
    return anti * jnp.where(anti >= 0.0, jnp.minimum(rise_b, drop_a), jnp.minimum(rise_a, drop_b))


def ratios(lowered, top_value, low_value, inward, outward):
    gain = sum(jnp.maximum(x, 0.0) for x in inward) - sum(jnp.minimum(x, 0.0) for x in outward)
    loss = gain + (sum(outward) - sum(inward))
    rise = jnp.minimum(1.0, (top_value - lowered) / jnp.maximum(gain, FLUX_FLOOR))
    drop = jnp.minimum(1.0, (lowered - low_value) / jnp.maximum(loss, FLUX_FLOOR))
    return rise, drop


def main(
    ct_in, cs_in, cu_in, cv_in, cw_in, cm_in, core, chip,
    adv_t, adv_s, sides, ct, cs, cu, cv, cw, cm,
    low_t, low_s, ae_t, ae_s, an_t, an_s, au_t, au_s, hi_t, hi_s, lo_t, lo_s, up_t, up_s, dn_t, dn_s, fe_t, fe_s,
):
    levels, rows, lanes = adv_t.shape
    wide = rows + 8
    here, to_east, to_west = pl.ds(8, wide), pl.ds(9, wide), pl.ds(7, wide)
    inner = pl.ds(OWN, rows)

    def fill(even):
        for src, east in ((core, even), (chip, not even)):
            a = OWN + rows if east else OWN - 3
            b = OWN + rows if east else OWN - 2
            for k in range(levels):
                ct[k + 1, a : a + 3] = src[k, 0:3]
                cs[k + 1, a : a + 3] = src[k, 3:6]
                cu[k + 1, a : a + 3] = src[k, 6:9]
                cv[k + 1, b : b + 2] = src[k, 9:11]
                cw[k + 1, b : b + 2] = src[k, 11:13]
                cm[k + 1, a : a + 3] = src[k, 13:16]

    by_parity(fill)

    tracers = (
        (ct, low_t, ae_t, an_t, au_t, hi_t, lo_t, up_t, dn_t, fe_t, adv_t),
        (cs, low_s, ae_s, an_s, au_s, hi_s, lo_s, up_s, dn_s, fe_s, adv_s),
    )
    nothing = jnp.zeros((wide, lanes), F32)
    for _, low, ae, an, au, hi, lo, rise, drop, _, _ in tracers:
        au[0, here] = nothing
        for k in (0, levels + 1):
            hi[k, here] = nothing - BIG
            lo[k, here] = nothing + BIG
            rise[k, here] = nothing
            drop[k, here] = nothing

    def first_pass(k, carry):
        wet = cm[k, here]
        east = low_and_anti(cu[k, here] * (wet * cm[k, to_east]))
        north = low_and_anti(cv[k, here] * (wet * roll(wet, -1, 1)))
        upward = low_and_anti(cw[k, here] * (wet * cm[k + 1, here]))
        fluxes = []
        for n, (c, low, ae, an, au, hi, lo, _, _, face, _) in enumerate(tracers):
            x = c[k, here]
            fe, ae[k, here] = east(x, c[k, to_east])
            fn, an[k, here] = north(x, roll(x, -1, 1))
            fu, au[k, here] = upward(c[k + 1, here], x)
            face[k, here] = fe
            fluxes.append(fu)
            lowered = x - ((fe - face[k, to_west]) + (fn - roll(fn, 1, 1)) + (carry[n] - fu))
            low[k, here] = lowered
            dry = wet == 0.0
            hi[k, here] = jnp.where(dry, -BIG, jnp.maximum(x, lowered))
            lo[k, here] = jnp.where(dry, BIG, jnp.minimum(x, lowered))
        return tuple(fluxes)

    lax.fori_loop(1, levels + 1, first_pass, (nothing, nothing), unroll=UNROLL[0])

    def second_pass(k, carry):
        for _, low, ae, an, au, hi, lo, rise, drop, _, _ in tracers:
            top_value, low_value = hi[k, here], lo[k, here]
            for x in (hi[k, to_east], hi[k, to_west], roll(top_value, -1, 1), roll(top_value, 1, 1),
                      hi[k + 1, here], hi[k - 1, here]):
                top_value = jnp.maximum(top_value, x)
            for x in (lo[k, to_east], lo[k, to_west], roll(low_value, -1, 1), roll(low_value, 1, 1),
                      lo[k + 1, here], lo[k - 1, here]):
                low_value = jnp.minimum(low_value, x)
            anti_n = an[k, here]
            rise[k, here], drop[k, here] = ratios(
                low[k, here], top_value, low_value,
                (ae[k, to_west], roll(anti_n, 1, 1), au[k, here]), (ae[k, here], anti_n, au[k - 1, here]),
            )
        return carry

    lax.fori_loop(1, levels + 1, second_pass, 0, unroll=UNROLL[1])

    def third_pass(k, carry):
        fluxes = []
        for n, (_, low, ae, an, au, _, _, rise, drop, face, adv) in enumerate(tracers):
            r, d = rise[k, here], drop[k, here]
            fe = limited(ae[k, here], r, d, rise[k, to_east], drop[k, to_east])
            face[k, here] = fe
            r, d = rise[k, inner], drop[k, inner]
            fn = limited(an[k, inner], r, d, roll(r, -1, 1), roll(d, -1, 1))
            fu = limited(au[k, inner], rise[k + 1, inner], drop[k + 1, inner], r, d)
            fluxes.append(fu)
            out = (face[k, inner] - face[k, pl.ds(OWN - 1, rows)]) + (fn - roll(fn, 1, 1)) + (carry[n] - fu)
            adv[k - 1] = low[k, inner] - out
        return tuple(fluxes)

    no_flux = jnp.zeros((rows, lanes), F32)
    lax.fori_loop(1, levels + 1, third_pass, (no_flux, no_flux), unroll=UNROLL[2])

    _, group, _ = lanes_of(rows, lanes)
    for n, src in enumerate((core, chip)):
        for parity in range(2):
            out = no_flux
            for g in range(levels // 2):
                out = jnp.where(group == g, roll(src[2 * g + parity], 16 * g + 6, 1), out)
            sides[n, parity] = out


def finish(
    adv_t, adv_s, number, inverse, own, sides, top, lat1, core2, diag1, fold,
    new_t, new_s,
    ct, cs, cu, cv, cw, cm, edge, mirror,
    low_t, low_s, ae_t, ae_s, an_t, an_s, au_t, au_s, hi_t, hi_s, lo_t, lo_s, up_t, up_s, dn_t, dn_s, fe_t, fe_s,
):
    i, j = position()
    n_lon, n_lat = lax.axis_size("lon"), lax.axis_size("lat")
    first, last, is_top, is_low = i == 0, i == n_lon - 1, j == n_lat - 1, j == 0
    levels, rows, lanes = adv_t.shape
    wide = rows + 8
    _, group, spot = lanes_of(wide, lanes)
    here, to_east, to_west = pl.ds(8, wide), pl.ds(9, wide), pl.ds(7, wide)
    cells = (ct, cs, cu, cv, cw, cm)
    starts = (0, 3, 6, 9, 11, 13)
    counts = (3, 3, 3, 2, 2, 3)

    for n, ref in enumerate(cells):
        for parity in range(2):
            ref[2 + parity, OWN : OWN + rows] = own[n, parity]
    for parity in range(2):
        edge[parity, 4 : 4 + rows] = lat1[parity]
        edge[2 + parity] = fold[wide * parity : wide * parity + wide]

    def fill(even):
        for n, (src, east) in enumerate(((core2, even), (diag1, not even))):
            for ref, start, count in zip(cells, starts, counts):
                a = OWN + rows if east else OWN - count
                for parity in range(2):
                    ref[2 + parity, a : a + count] = sides[n, parity, start : start + count]
            a = 4 + rows if east else 1
            for parity in range(2):
                edge[parity, a : a + 3] = src[3 * parity : 3 * parity + 3]

    by_parity(fill)

    @pl.when(first)
    def _():
        for parity in range(2):
            edge[parity, 1:4] = fold[2 * wide + 3 * parity : 2 * wide + 3 * parity + 3]
            edge[2 + parity, rows + 4 : rows + 7] = top[parity, 0:3]

    @pl.when(last)
    def _():
        for parity in range(2):
            edge[parity, rows + 4 : rows + 7] = fold[2 * wide + 3 * parity : 2 * wide + 3 * parity + 3]
            edge[2 + parity, 1:4] = top[parity, rows - 3 : rows]

    for parity in range(2):
        for r in range(wide):
            q = wide - 1 - r
            mirror[parity, r : r + 1] = edge[2 + parity, q : q + 1]

    for parity in range(2):
        other, mir = edge[parity], mirror[parity]
        for ref, (name, start, count) in zip(cells, SPOTS):
            mine = ref[2 + parity, here]
            source = mir
            if name == "u":
                source = -roll(mir, -1, 0)
            if name == "v":
                source = -mir
            beyond = roll(other, 6 - start, 1)
            lead = start + 1 if name == "v" else start + count - 1
            for d in range(2 if name == "v" else count):
                beyond = jnp.where((spot == 6 + d) & is_top, roll(source, 6 + d - (lead - d), 1), beyond)
            value_n = jnp.where(spot < 6, mine, beyond)
            if name == "v":
                folded = 0.5 * (mine + roll(source, 5 - (start + 2), 1))
                value_n = jnp.where((spot == 5) & is_top, folded, value_n)
            value_s = jnp.where(spot < 6, roll(other, 6 - count - start, 1), mine)
            if name == "m":
                value_n = jnp.where(spot > 8, 0.0, value_n)
                value_s = jnp.where((spot < 3) | (spot > 11) | ((spot < 6) & is_low), 0.0, value_s)
            ref[parity, here] = value_n
            ref[2 + parity, here] = value_s

    lowest = group == levels // 2 - 1
    highest = group == 0

    def below(ref, k, edge_value=None):
        if k % 2 == 0:
            return ref[k + 1, here]
        x = roll(ref[k - 1, here], -16, 1)
        return x if edge_value is None else jnp.where(lowest, edge_value, x)

    def above(ref, k, edge_value):
        if k % 2 == 1:
            return ref[k - 1, here]
        return jnp.where(highest, edge_value, roll(ref[k + 1, here], 16, 1))

    tracers = (
        (ct, low_t, ae_t, an_t, au_t, hi_t, lo_t, up_t, dn_t, fe_t),
        (cs, low_s, ae_s, an_s, au_s, hi_s, lo_s, up_s, dn_s, fe_s),
    )
    for strip in (0, 2):
        ends = (strip, strip + 1)
        tops = [[None, None], [None, None]]
        for k in ends:
            wet = cm[k, here]
            east = low_and_anti(cu[k, here] * (wet * cm[k, to_east]))
            north = low_and_anti(cv[k, here] * (wet * roll(wet, -1, 1)))
            upward = low_and_anti(cw[k, here] * (wet * below(cm, k, 0.0)))
            for n, (c, low, ae, an, au, hi, lo, _, _, face) in enumerate(tracers):
                x = c[k, here]
                fe, ae[k, here] = east(x, c[k, to_east])
                fn, an[k, here] = north(x, roll(x, -1, 1))
                fu, au[k, here] = upward(below(c, k), x)
                face[k, here] = fe
                tops[n][k % 2] = fu
                low[k, here] = x - ((fe - face[k, to_west]) + (fn - roll(fn, 1, 1)) - fu)
        for k in ends:
            dry = cm[k, here] == 0.0
            for n, (c, low, ae, an, au, hi, lo, _, _, _) in enumerate(tracers):
                over = tops[n][0] if k % 2 == 1 else jnp.where(highest, 0.0, roll(tops[n][1], 16, 1))
                x, lowered = c[k, here], low[k, here] - over
                low[k, here] = lowered
                hi[k, here] = jnp.where(dry, -BIG, jnp.maximum(x, lowered))
                lo[k, here] = jnp.where(dry, BIG, jnp.minimum(x, lowered))
        for k in ends:
            for _, low, ae, an, au, hi, lo, rise, drop, _ in tracers:
                top_value, low_value = hi[k, here], lo[k, here]
                for x in (hi[k, to_east], hi[k, to_west], roll(top_value, -1, 1), roll(top_value, 1, 1),
                          below(hi, k, -BIG), above(hi, k, -BIG)):
                    top_value = jnp.maximum(top_value, x)
                for x in (lo[k, to_east], lo[k, to_west], roll(low_value, -1, 1), roll(low_value, 1, 1),
                          below(lo, k, BIG), above(lo, k, BIG)):
                    low_value = jnp.minimum(low_value, x)
                anti_n = an[k, here]
                rise[k, here], drop[k, here] = ratios(
                    low[k, here], top_value, low_value,
                    (ae[k, to_west], roll(anti_n, 1, 1), au[k, here]), (ae[k, here], anti_n, above(au, k, 0.0)),
                )
        for k in ends:
            for _, low, ae, an, au, hi, _, rise, drop, face in tracers:
                r, d = rise[k, here], drop[k, here]
                face[k, here] = limited(ae[k, here], r, d, rise[k, to_east], drop[k, to_east])
                hi[k, here] = limited(au[k, here], below(rise, k), below(drop, k), r, d)
        for k in ends:
            for _, low, ae, an, au, hi, lo, rise, drop, face in tracers:
                r, d = rise[k, here], drop[k, here]
                fn = limited(an[k, here], r, d, roll(r, -1, 1), roll(d, -1, 1))
                out = (face[k, here] - face[k, to_west]) + (fn - roll(fn, 1, 1))
                lo[k, here] = low[k, here] - (out + (above(hi, k, 0.0) - hi[k, here]))

    _, _, place = lanes_of(rows, lanes)
    ends = []
    for tracer in tracers:
        lo = tracer[6]
        ends.append([
            jnp.where(place < 6, lo[parity, OWN : OWN + rows], lo[2 + parity, OWN : OWN + rows])
            for parity in range(2)
        ])
    lane, _, _ = lanes_of(rows, lanes)
    outer = (lane < 3) | (lane >= lanes - 3)
    solved = [None, None]
    for k in range(levels):
        q, inv = number[k], inverse[k]
        for n, adv in enumerate((adv_t, adv_s)):
            x = jnp.where(outer, roll(ends[n][k % 2], -(16 * (k // 2) + 6), 1), adv[k])
            if k > 0:
                x = x + q * solved[n]
            solved[n] = x * inv
            (new_t, new_s)[n][k] = solved[n]
    for k in range(levels - 2, -1, -1):
        ratio = number[k + 1] * inverse[k]
        for n, out in enumerate((new_t, new_s)):
            solved[n] = out[k] + ratio * solved[n]
            out[k] = solved[n]


def call(body, outs, args, scratch=(), aliases=None, limit=8, flops=2_000_000):
    vmem = pl.BlockSpec(memory_space=pltpu.VMEM)
    outs = [x if hasattr(x, "dtype") else jax.ShapeDtypeStruct(x, F32) for x in outs]
    where = pltpu.HBM if body is pack else pltpu.VMEM
    return pl.pallas_call(
        body,
        out_shape=tuple(outs),
        in_specs=[pl.BlockSpec(memory_space=where)] * len(args),
        out_specs=tuple(vmem for _ in outs),
        scratch_shapes=[x if not isinstance(x, tuple) else pltpu.VMEM(x, F32) for x in scratch],
        input_output_aliases=aliases or {},
        compiler_params=pltpu.CompilerParams(vmem_limit_bytes=limit * 2**20),
        cost_estimate=pl.CostEstimate(flops=flops, bytes_accessed=2_000_000, transcendentals=0),
    )(*args)


def local(n_lon, n_lat, *args):
    levels, rows, lanes = args[0].shape
    wide = rows + 8

    def number(i, j):
        return (i % n_lon) * n_lat + j

    grid = [(i, j) for i in range(n_lon) for j in range(n_lat)]

    def beside(i):
        return i - 1 if i % 2 == 0 else i + 1

    cores = [(number(i, j), number(i ^ 1, j)) for i, j in grid]
    chips = [(number(i, j), number(beside(i), j)) for i, j in grid]
    lats = [(number(i, j), number(i, n_lat - 1 - j)) for i, j in grid]
    folds = [(number(i, j), number(n_lon - 1 - i, j)) for i, j in grid]
    ends = [(number(i, j), number(i, n_lat - 1 - j)) for i, j in grid if i in (0, n_lon - 1)]
    inner = [(number(i, j), number(beside(i), j)) for i, j in grid if 0 < i < n_lon - 1] + ends
    diags = [(number(i, j), number(beside(i), n_lat - 1 - j)) for i, j in grid if 0 < i < n_lon - 1] + ends

    def send(x, pairs):
        return lax.ppermute(x, AXES, pairs)

    core, chip, chip1, diag1, lat1, top, own, *held = call(
        pack,
        [(levels + 1, rows, lanes), (levels, rows, lanes), (8, lanes), (8, lanes), (2, rows, lanes), (2, rows, lanes),
         (6, 2, rows, lanes)] + [jax.ShapeDtypeStruct(x.shape, x.dtype) for x in args],
        [pltpu.with_memory_space_constraint(x, pltpu.HBM) for x in args],
        [pltpu.SemaphoreType.DMA((len(args),))],
    )
    chip1_in = send(chip1, inner)
    lat1_in = send(lat1, lats)
    core_in = send(core, cores)
    diag1_in = send(diag1, diags)
    chip_in = send(chip, chips)
    cell = (levels + 2, 40, lanes)
    numbers, inverse, *cells = call(prepare, [(levels, rows, lanes)] * 2 + [cell] * 6, held)
    core2, fold = call(repack, [(8, lanes), (2 * wide + 8, lanes)], (top, core_in, chip1_in, lat1_in), limit=2)
    fold_in = send(fold, folds)
    core2_in = send(core2, cores)
    adv_t, adv_s, sides, *_ = call(
        main,
        [(levels, rows, lanes)] * 2 + [(2, 2, rows, lanes)] + [cell] * 6,
        (*cells, core_in, chip_in),
        [cell] * 18,
        aliases={n: 3 + n for n in range(6)},
        limit=20,
        flops=20_000_000,
    )
    strip = (4, 40, lanes)
    return call(
        finish,
        [(levels, rows, lanes)] * 2,
        (adv_t, adv_s, numbers, inverse, own, sides, top, lat1_in, core2_in, diag1_in, fold_in),
        [strip] * 6 + [(4, wide, lanes), (2, wide, lanes)] + [strip] * 18,
    )


def solution(mesh):
    n_lon, n_lat = mesh.shape["lon"], mesh.shape["lat"]
    cube = P(None, "lon", "lat")
    plane = P("lon", "lat")
    return jax.shard_map(
        lambda *args: tuple(local(n_lon, n_lat, *args)),
        mesh=mesh,
        in_specs=(cube,) * 6 + (plane,) * 2,
        out_specs=(cube, cube),
        check_vma=False,
    )
```

```python
import jax
import jax.numpy as jnp
from jax import lax
from jax.experimental import pallas as pl
from jax.experimental.pallas import tpu as pltpu
from jax.sharding import PartitionSpec as P


FLUX_FLOOR = 0.01
BIG = 1e30
AXES = ("lon", "lat")
F32 = jnp.float32


SPOTS = (("t", 0, 3), ("s", 3, 3), ("u", 6, 2), ("v", 8, 3), ("w", 11, 2), ("m", 13, 3))
OWN = 12
UNROLL = (4, 4, 4)


def roll(x, shift, axis):
    if not isinstance(shift, int):
        return pltpu.roll(x, shift, axis)
    shift = shift % x.shape[axis]
    return x if shift == 0 else pltpu.roll(x, shift, axis)


def position():
    return lax.axis_index("lon"), lax.axis_index("lat")


def by_parity(body):
    even = lax.rem(lax.axis_index("lon"), 2) == 0

    @pl.when(even)
    def _():
        body(True)

    @pl.when(jnp.logical_not(even))
    def _():
        body(False)


def lanes_of(rows, lanes):
    lane = lax.broadcasted_iota(jnp.int32, (rows, lanes), 1)
    return lane, lane >> 4, lane & 15


def wet_of(flag, depth, level):
    return jnp.where((level < depth) & (flag > 0), 1.0, 0.0).astype(F32)


def pack(
    t_any, s_any, u_any, v_any, w_any, dc_any, flag_any, depth_any,
    core, chip, chip1, bound, top, own, t, s, u, v, w, dc, flag, depth, sems,
):
    sources = (flag_any, depth_any, t_any, s_any, u_any, v_any, w_any, dc_any)
    targets = (flag, depth, t, s, u, v, w, dc)
    copies = [pltpu.make_async_copy(x, y, sems.at[n]) for n, (x, y) in enumerate(zip(sources, targets))]
    for copy in copies:
        copy.start()
    levels, rows, lanes = t.shape
    _, j = position()
    _, group, spot = lanes_of(rows, lanes)
    zero = jnp.zeros((rows, lanes), F32)
    core[levels] = zero
    chip1[...] = jnp.zeros(chip1.shape, F32)
    for copy in copies:
        copy.wait()
    flags, depths = flag[...], depth[...]
    fields = dict(t=t, s=s, u=u, v=v, w=w)
    held = {}
    for n, (name, _, _) in enumerate(SPOTS):
        for parity in range(2):
            out = zero
            for g in range(levels // 2):
                k = 2 * g + parity
                if name == "w" and k == levels - 1:
                    continue
                x = wet_of(flags, depths, k) if name == "m" else fields[name][k]
                out = jnp.where(group == g, roll(x, 16 * g + 6, 1), out)
            own[n, parity] = out
            held[name, parity] = out
    tops, afar = [], []
    for parity in range(2):
        up, down = zero, zero
        for name, start, count in SPOTS:
            mine = (spot >= start) & (spot < start + count)
            up = jnp.where(mine, roll(held[name, parity], start - (6 - count), 1), up)
            down = jnp.where(mine, roll(held[name, parity], start - 6, 1), down)
        top[parity] = up
        afar.append(jnp.where(j == 0, up, down))
        bound[parity] = afar[parity]
        tops.append(up)

    def sides(out, east):
        a, c = (rows - 3, rows - 2) if east else (0, 0)
        for k in range(levels):
            out[k, 0:3] = t[k, a : a + 3]
            out[k, 3:6] = s[k, a : a + 3]
            out[k, 6:9] = u[k, a : a + 3]
            out[k, 9:11] = v[k, c : c + 2]
            if k < levels - 1:
                out[k, 11:13] = w[k, c : c + 2]
            else:
                out[k, 11:13] = jnp.zeros((2, lanes), F32)
            out[k, 13:16] = wet_of(flags, depths, k)[a : a + 3]

    def fill(even):
        sides(core, even)
        sides(chip, not even)
        for out, east in ((core.at[levels], even), (chip1, not even)):
            a = rows - 3 if east else 0
            for n, x in enumerate(tops + afar):
                out[3 * n : 3 * n + 3] = x[a : a + 3]

    by_parity(fill)


def repack(top, bound, core, chip1, fold, lat):
    levels = core.shape[0] - 1
    rows, _ = top.shape[1:]
    wide = rows + 8
    fold[...] = jnp.zeros(fold.shape, F32)
    lat[...] = jnp.zeros(lat.shape, F32)
    for parity in range(2):
        fold[wide * parity + 4 : wide * parity + 4 + rows] = top[parity]
        lat[wide * parity + 4 : wide * parity + 4 + rows] = bound[parity]
    fold[2 * wide : 2 * wide + 6] = chip1[6:12]

    def fill(even):
        for n, out in enumerate((fold, lat)):
            for parity in range(2):
                part = 6 * n + 3 * parity
                near, far = core[levels, part : part + 3], chip1[part : part + 3]
                east, west = (near, far) if even else (far, near)
                at = wide * parity
                out[at + 1 : at + 4] = west
                out[at + rows + 4 : at + rows + 7] = east

    by_parity(fill)


def columns(src, east, cells, levels, rows):
    ct, cs, cu, cv, cw, cm = cells
    a = OWN + rows if east else OWN - 3
    b = OWN + rows if east else OWN - 2
    for k in range(levels):
        ct[k + 1, a : a + 3] = src[k, 0:3]
        cs[k + 1, a : a + 3] = src[k, 3:6]
        cu[k + 1, a : a + 3] = src[k, 6:9]
        cv[k + 1, b : b + 2] = src[k, 9:11]
        cw[k + 1, b : b + 2] = src[k, 11:13]
        cm[k + 1, a : a + 3] = src[k, 13:16]


def at_strips(src, out, levels, rows, lanes):
    _, group, _ = lanes_of(rows, lanes)
    for parity in range(2):
        x = jnp.zeros((rows, lanes), F32)
        for g in range(levels // 2):
            x = jnp.where(group == g, roll(src[2 * g + parity], 16 * g + 6, 1), x)
        out[parity] = x


def prepare(t, s, u, v, w, dc, flag, depth, core, number, inverse, core_side, ct, cs, cu, cv, cw, cm):
    levels, rows, lanes = t.shape
    flags, depths = flag[...], depth[...]
    zero = jnp.zeros(flags.shape, F32)
    q = [zero]
    for k in range(1, levels):
        q.append(dc[k - 1] * wet_of(flags, depths, k))
    q.append(zero)
    ratio = zero
    for k in range(levels):
        denom = 1.0 + q[k] + q[k + 1] - q[k] * ratio
        inv = 1.0 / denom
        ratio = q[k + 1] * inv
        number[k] = q[k]
        inverse[k] = inv
    for ref in (ct, cs, cu, cv, cw, cm):
        for k in (0, levels + 1):
            ref[k] = jnp.zeros(ref.shape[1:], F32)
    for k in range(levels):
        ct[k + 1, OWN : OWN + rows] = t[k]
        cs[k + 1, OWN : OWN + rows] = s[k]
        cu[k + 1, OWN : OWN + rows] = u[k]
        cv[k + 1, OWN : OWN + rows] = v[k]
        cw[k + 1, OWN : OWN + rows] = w[k] if k < levels - 1 else zero
        cm[k + 1, OWN : OWN + rows] = wet_of(flags, depths, k)
    at_strips(core, core_side, levels, rows, lanes)
    by_parity(lambda even: columns(core, even, (ct, cs, cu, cv, cw, cm), levels, rows))


def low_and_anti(speed):
    parts = jnp.maximum(speed, 0.0), jnp.minimum(speed, 0.0), 0.5 * jnp.abs(speed)
    return lambda a, b: (parts[0] * a + parts[1] * b, parts[2] * (b - a))


def limited(anti, rise_a, drop_a, rise_b, drop_b):
    return anti * jnp.where(anti >= 0.0, jnp.minimum(rise_b, drop_a), jnp.minimum(rise_a, drop_b))


def ratios(lowered, top_value, low_value, inward, outward):
    gain = sum(jnp.maximum(x, 0.0) for x in inward) - sum(jnp.minimum(x, 0.0) for x in outward)
    loss = gain + (sum(outward) - sum(inward))
    rise = jnp.minimum(1.0, (top_value - lowered) / jnp.maximum(gain, FLUX_FLOOR))
    drop = jnp.minimum(1.0, (lowered - low_value) / jnp.maximum(loss, FLUX_FLOOR))
    return rise, drop


def main(
    ct_in, cs_in, cu_in, cv_in, cw_in, cm_in, chip,
    adv_t, adv_s, chip_side, ct, cs, cu, cv, cw, cm,
    low_t, low_s, ae_t, ae_s, an_t, an_s, au_t, au_s, hi_t, hi_s, lo_t, lo_s, up_t, up_s, dn_t, dn_s, fe_t, fe_s,
):
    levels, rows, lanes = adv_t.shape
    wide = rows + 8
    here, to_east, to_west = pl.ds(8, wide), pl.ds(9, wide), pl.ds(7, wide)
    inner = pl.ds(OWN, rows)

    by_parity(lambda even: columns(chip, not even, (ct, cs, cu, cv, cw, cm), levels, rows))

    tracers = (
        (ct, low_t, ae_t, an_t, au_t, hi_t, lo_t, up_t, dn_t, fe_t, adv_t),
        (cs, low_s, ae_s, an_s, au_s, hi_s, lo_s, up_s, dn_s, fe_s, adv_s),
    )
    nothing = jnp.zeros((wide, lanes), F32)
    for _, low, ae, an, au, hi, lo, rise, drop, _, _ in tracers:
        au[0, here] = nothing
        for k in (0, levels + 1):
            hi[k, here] = nothing - BIG
            lo[k, here] = nothing + BIG
            rise[k, here] = nothing
            drop[k, here] = nothing

    def first_pass(k, carry):
        wet = cm[k, here]
        east = low_and_anti(cu[k, here] * (wet * cm[k, to_east]))
        north = low_and_anti(cv[k, here] * (wet * roll(wet, -1, 1)))
        upward = low_and_anti(cw[k, here] * (wet * cm[k + 1, here]))
        fluxes = []
        for n, (c, low, ae, an, au, hi, lo, _, _, face, _) in enumerate(tracers):
            x = c[k, here]
            fe, ae[k, here] = east(x, c[k, to_east])
            fn, an[k, here] = north(x, roll(x, -1, 1))
            fu, au[k, here] = upward(c[k + 1, here], x)
            face[k, here] = fe
            fluxes.append(fu)
            lowered = x - ((fe - face[k, to_west]) + (fn - roll(fn, 1, 1)) + (carry[n] - fu))
            low[k, here] = lowered
            dry = wet == 0.0
            hi[k, here] = jnp.where(dry, -BIG, jnp.maximum(x, lowered))
            lo[k, here] = jnp.where(dry, BIG, jnp.minimum(x, lowered))
        return tuple(fluxes)

    lax.fori_loop(1, levels + 1, first_pass, (nothing, nothing), unroll=UNROLL[0])

    def second_pass(k, carry):
        for _, low, ae, an, au, hi, lo, rise, drop, _, _ in tracers:
            top_value, low_value = hi[k, here], lo[k, here]
            for x in (hi[k, to_east], hi[k, to_west], roll(top_value, -1, 1), roll(top_value, 1, 1),
                      hi[k + 1, here], hi[k - 1, here]):
                top_value = jnp.maximum(top_value, x)
            for x in (lo[k, to_east], lo[k, to_west], roll(low_value, -1, 1), roll(low_value, 1, 1),
                      lo[k + 1, here], lo[k - 1, here]):
                low_value = jnp.minimum(low_value, x)
            anti_n = an[k, here]
            rise[k, here], drop[k, here] = ratios(
                low[k, here], top_value, low_value,
                (ae[k, to_west], roll(anti_n, 1, 1), au[k, here]), (ae[k, here], anti_n, au[k - 1, here]),
            )
        return carry

    lax.fori_loop(1, levels + 1, second_pass, 0, unroll=UNROLL[1])

    def third_pass(k, carry):
        fluxes = []
        for n, (_, low, ae, an, au, _, _, rise, drop, face, adv) in enumerate(tracers):
            r, d = rise[k, here], drop[k, here]
            fe = limited(ae[k, here], r, d, rise[k, to_east], drop[k, to_east])
            face[k, here] = fe
            r, d = rise[k, inner], drop[k, inner]
            fn = limited(an[k, inner], r, d, roll(r, -1, 1), roll(d, -1, 1))
            fu = limited(au[k, inner], rise[k + 1, inner], drop[k + 1, inner], r, d)
            fluxes.append(fu)
            out = (face[k, inner] - face[k, pl.ds(OWN - 1, rows)]) + (fn - roll(fn, 1, 1)) + (carry[n] - fu)
            adv[k - 1] = low[k, inner] - out
        return tuple(fluxes)

    no_flux = jnp.zeros((rows, lanes), F32)
    lax.fori_loop(1, levels + 1, third_pass, (no_flux, no_flux), unroll=UNROLL[2])

    at_strips(chip, chip_side, levels, rows, lanes)


def finish(
    adv_t, adv_s, number, inverse, own, core_side, chip_side, top, lat, fold,
    new_t, new_s,
    ct, cs, cu, cv, cw, cm, edge, mirror,
    low_t, low_s, ae_t, ae_s, an_t, an_s, au_t, au_s, hi_t, hi_s, lo_t, lo_s, up_t, up_s, dn_t, dn_s, fe_t, fe_s,
):
    i, j = position()
    n_lon, n_lat = lax.axis_size("lon"), lax.axis_size("lat")
    first, last, is_top, is_low = i == 0, i == n_lon - 1, j == n_lat - 1, j == 0
    levels, rows, lanes = adv_t.shape
    wide = rows + 8
    _, group, spot = lanes_of(wide, lanes)
    here, to_east, to_west = pl.ds(8, wide), pl.ds(9, wide), pl.ds(7, wide)
    cells = (ct, cs, cu, cv, cw, cm)
    starts = (0, 3, 6, 9, 11, 13)
    counts = (3, 3, 3, 2, 2, 3)

    for n, ref in enumerate(cells):
        for parity in range(2):
            ref[2 + parity, OWN : OWN + rows] = own[n, parity]
    for parity in range(2):
        edge[parity] = lat[wide * parity : wide * parity + wide]
        edge[2 + parity] = fold[wide * parity : wide * parity + wide]

    def fill(even):
        for side, east in ((core_side, even), (chip_side, not even)):
            for ref, start, count in zip(cells, starts, counts):
                a = OWN + rows if east else OWN - count
                for parity in range(2):
                    ref[2 + parity, a : a + count] = side[parity, start : start + count]

    by_parity(fill)

    @pl.when(first)
    def _():
        for parity in range(2):
            edge[parity, 1:4] = fold[2 * wide + 3 * parity : 2 * wide + 3 * parity + 3]
            edge[2 + parity, rows + 4 : rows + 7] = top[parity, 0:3]

    @pl.when(last)
    def _():
        for parity in range(2):
            edge[parity, rows + 4 : rows + 7] = fold[2 * wide + 3 * parity : 2 * wide + 3 * parity + 3]
            edge[2 + parity, 1:4] = top[parity, rows - 3 : rows]

    for parity in range(2):
        for r in range(wide):
            q = wide - 1 - r
            mirror[parity, r : r + 1] = edge[2 + parity, q : q + 1]

    for parity in range(2):
        other, mir = edge[parity], mirror[parity]
        for ref, (name, start, count) in zip(cells, SPOTS):
            mine = ref[2 + parity, here]
            source = mir
            if name == "u":
                source = -roll(mir, -1, 0)
            if name == "v":
                source = -mir
            beyond = roll(other, 6 - start, 1)
            lead = start + 1 if name == "v" else start + count - 1
            for d in range(2 if name == "v" else count):
                beyond = jnp.where((spot == 6 + d) & is_top, roll(source, 6 + d - (lead - d), 1), beyond)
            value_n = jnp.where(spot < 6, mine, beyond)
            if name == "v":
                folded = 0.5 * (mine + roll(source, 5 - (start + 2), 1))
                value_n = jnp.where((spot == 5) & is_top, folded, value_n)
            value_s = jnp.where(spot < 6, roll(other, 6 - count - start, 1), mine)
            if name == "m":
                value_n = jnp.where(spot > 8, 0.0, value_n)
                value_s = jnp.where((spot < 3) | (spot > 11) | ((spot < 6) & is_low), 0.0, value_s)
            ref[parity, here] = value_n
            ref[2 + parity, here] = value_s

    lowest = group == levels // 2 - 1
    highest = group == 0

    def below(ref, k, edge_value=None):
        if k % 2 == 0:
            return ref[k + 1, here]
        x = roll(ref[k - 1, here], -16, 1)
        return x if edge_value is None else jnp.where(lowest, edge_value, x)

    def above(ref, k, edge_value):
        if k % 2 == 1:
            return ref[k - 1, here]
        return jnp.where(highest, edge_value, roll(ref[k + 1, here], 16, 1))

    tracers = (
        (ct, low_t, ae_t, an_t, au_t, hi_t, lo_t, up_t, dn_t, fe_t),
        (cs, low_s, ae_s, an_s, au_s, hi_s, lo_s, up_s, dn_s, fe_s),
    )
    for strip in (0, 2):
        ends = (strip, strip + 1)
        tops = [[None, None], [None, None]]
        for k in ends:
            wet = cm[k, here]
            east = low_and_anti(cu[k, here] * (wet * cm[k, to_east]))
            north = low_and_anti(cv[k, here] * (wet * roll(wet, -1, 1)))
            upward = low_and_anti(cw[k, here] * (wet * below(cm, k, 0.0)))
            for n, (c, low, ae, an, au, hi, lo, _, _, face) in enumerate(tracers):
                x = c[k, here]
                fe, ae[k, here] = east(x, c[k, to_east])
                fn, an[k, here] = north(x, roll(x, -1, 1))
                fu, au[k, here] = upward(below(c, k), x)
                face[k, here] = fe
                tops[n][k % 2] = fu
                low[k, here] = x - ((fe - face[k, to_west]) + (fn - roll(fn, 1, 1)) - fu)
        for k in ends:
            dry = cm[k, here] == 0.0
            for n, (c, low, ae, an, au, hi, lo, _, _, _) in enumerate(tracers):
                over = tops[n][0] if k % 2 == 1 else jnp.where(highest, 0.0, roll(tops[n][1], 16, 1))
                x, lowered = c[k, here], low[k, here] - over
                low[k, here] = lowered
                hi[k, here] = jnp.where(dry, -BIG, jnp.maximum(x, lowered))
                lo[k, here] = jnp.where(dry, BIG, jnp.minimum(x, lowered))
        for k in ends:
            for _, low, ae, an, au, hi, lo, rise, drop, _ in tracers:
                top_value, low_value = hi[k, here], lo[k, here]
                for x in (hi[k, to_east], hi[k, to_west], roll(top_value, -1, 1), roll(top_value, 1, 1),
                          below(hi, k, -BIG), above(hi, k, -BIG)):
                    top_value = jnp.maximum(top_value, x)
                for x in (lo[k, to_east], lo[k, to_west], roll(low_value, -1, 1), roll(low_value, 1, 1),
                          below(lo, k, BIG), above(lo, k, BIG)):
                    low_value = jnp.minimum(low_value, x)
                anti_n = an[k, here]
                rise[k, here], drop[k, here] = ratios(
                    low[k, here], top_value, low_value,
                    (ae[k, to_west], roll(anti_n, 1, 1), au[k, here]), (ae[k, here], anti_n, above(au, k, 0.0)),
                )
        for k in ends:
            for _, low, ae, an, au, hi, _, rise, drop, face in tracers:
                r, d = rise[k, here], drop[k, here]
                face[k, here] = limited(ae[k, here], r, d, rise[k, to_east], drop[k, to_east])
                hi[k, here] = limited(au[k, here], below(rise, k), below(drop, k), r, d)
        for k in ends:
            for _, low, ae, an, au, hi, lo, rise, drop, face in tracers:
                r, d = rise[k, here], drop[k, here]
                fn = limited(an[k, here], r, d, roll(r, -1, 1), roll(d, -1, 1))
                out = (face[k, here] - face[k, to_west]) + (fn - roll(fn, 1, 1))
                lo[k, here] = low[k, here] - (out + (above(hi, k, 0.0) - hi[k, here]))

    _, _, place = lanes_of(rows, lanes)
    ends = []
    for tracer in tracers:
        lo = tracer[6]
        ends.append([
            jnp.where(place < 6, lo[parity, OWN : OWN + rows], lo[2 + parity, OWN : OWN + rows])
            for parity in range(2)
        ])
    lane, _, _ = lanes_of(rows, lanes)
    outer = (lane < 3) | (lane >= lanes - 3)
    solved = [None, None]
    for k in range(levels):
        q, inv = number[k], inverse[k]
        for n, adv in enumerate((adv_t, adv_s)):
            x = jnp.where(outer, roll(ends[n][k % 2], -(16 * (k // 2) + 6), 1), adv[k])
            if k > 0:
                x = x + q * solved[n]
            solved[n] = x * inv
            (new_t, new_s)[n][k] = solved[n]
    for k in range(levels - 2, -1, -1):
        ratio = number[k + 1] * inverse[k]
        for n, out in enumerate((new_t, new_s)):
            solved[n] = out[k] + ratio * solved[n]
            out[k] = solved[n]


def call(body, outs, args, scratch=(), aliases=None, limit=8, flops=2_000_000):
    vmem = pl.BlockSpec(memory_space=pltpu.VMEM)
    outs = [x if hasattr(x, "dtype") else jax.ShapeDtypeStruct(x, F32) for x in outs]
    where = pltpu.HBM if body is pack else pltpu.VMEM
    return pl.pallas_call(
        body,
        out_shape=tuple(outs),
        in_specs=[pl.BlockSpec(memory_space=where)] * len(args),
        out_specs=tuple(vmem for _ in outs),
        scratch_shapes=[x if not isinstance(x, tuple) else pltpu.VMEM(x, F32) for x in scratch],
        input_output_aliases=aliases or {},
        compiler_params=pltpu.CompilerParams(vmem_limit_bytes=limit * 2**20),
        cost_estimate=pl.CostEstimate(flops=flops, bytes_accessed=2_000_000, transcendentals=0),
    )(*args)


def local(n_lon, n_lat, *args):
    levels, rows, lanes = args[0].shape
    wide = rows + 8

    def number(i, j):
        return (i % n_lon) * n_lat + j

    grid = [(i, j) for i in range(n_lon) for j in range(n_lat)]

    def beside(i):
        return i - 1 if i % 2 == 0 else i + 1

    cores = [(number(i, j), number(i ^ 1, j)) for i, j in grid]
    chips = [(number(i, j), number(beside(i), j)) for i, j in grid]
    lats = [(number(i, j), number(i, n_lat - 1 - j)) for i, j in grid]
    folds = [(number(i, j), number(n_lon - 1 - i, j)) for i, j in grid]
    ends = [(number(i, j), number(i, n_lat - 1 - j)) for i, j in grid if i in (0, n_lon - 1)]
    inner = [(number(i, j), number(beside(i), j)) for i, j in grid if 0 < i < n_lon - 1] + ends

    def send(x, pairs):
        return lax.ppermute(x, AXES, pairs)

    core, chip, chip1, bound, top, own, *held = call(
        pack,
        [(levels + 1, rows, lanes), (levels, rows, lanes), (16, lanes)] + [(2, rows, lanes)] * 2
        + [(6, 2, rows, lanes)] + [jax.ShapeDtypeStruct(x.shape, x.dtype) for x in args],
        [pltpu.with_memory_space_constraint(x, pltpu.HBM) for x in args],
        [pltpu.SemaphoreType.DMA((len(args),))],
    )
    chip1_in = send(chip1, inner)
    core_in = send(core, cores)
    chip_in = send(chip, chips)
    cell = (levels + 2, 40, lanes)
    numbers, inverse, core_side, *cells = call(
        prepare, [(levels, rows, lanes)] * 2 + [(2, rows, lanes)] + [cell] * 6, (*held, core_in)
    )
    fold, lat = call(repack, [(2 * wide + 8, lanes), (2 * wide, lanes)], (top, bound, core_in, chip1_in), limit=2)
    fold_in = send(fold, folds)
    lat_in = send(lat, lats)
    adv_t, adv_s, chip_side, *_ = call(
        main,
        [(levels, rows, lanes)] * 2 + [(2, rows, lanes)] + [cell] * 6,
        (*cells, chip_in),
        [cell] * 18,
        aliases={n: 3 + n for n in range(6)},
        limit=20,
        flops=20_000_000,
    )
    strip = (4, 40, lanes)
    return call(
        finish,
        [(levels, rows, lanes)] * 2,
        (adv_t, adv_s, numbers, inverse, own, core_side, chip_side, top, lat_in, fold_in),
        [strip] * 6 + [(4, wide, lanes), (2, wide, lanes)] + [strip] * 18,
    )


def solution(mesh):
    n_lon, n_lat = mesh.shape["lon"], mesh.shape["lat"]
    cube = P(None, "lon", "lat")
    plane = P("lon", "lat")
    return jax.shard_map(
        lambda *args: tuple(local(n_lon, n_lat, *args)),
        mesh=mesh,
        in_specs=(cube,) * 6 + (plane,) * 2,
        out_specs=(cube, cube),
        check_vma=False,
    )
```

```python
import jax
import jax.numpy as jnp
from jax import lax
from jax.experimental import pallas as pl
from jax.experimental.pallas import tpu as pltpu
from jax.sharding import PartitionSpec as P


FLUX_FLOOR = 0.01
BIG = 1e30
AXES = ("lon", "lat")
F32 = jnp.float32


SPOTS = (("t", 0, 3), ("s", 3, 3), ("u", 6, 2), ("v", 8, 3), ("w", 11, 2), ("m", 13, 3))
OWN = 12
UNROLL = (8, 8, 8)


def roll(x, shift, axis):
    if not isinstance(shift, int):
        return pltpu.roll(x, shift, axis)
    shift = shift % x.shape[axis]
    return x if shift == 0 else pltpu.roll(x, shift, axis)


def position():
    return lax.axis_index("lon"), lax.axis_index("lat")


def by_parity(body):
    even = lax.rem(lax.axis_index("lon"), 2) == 0

    @pl.when(even)
    def _():
        body(True)

    @pl.when(jnp.logical_not(even))
    def _():
        body(False)


def lanes_of(rows, lanes):
    lane = lax.broadcasted_iota(jnp.int32, (rows, lanes), 1)
    return lane, lane >> 4, lane & 15


def wet_of(flag, depth, level):
    return jnp.where((level < depth) & (flag > 0), 1.0, 0.0).astype(F32)


def pack(
    t_any, s_any, u_any, v_any, w_any, dc_any, flag_any, depth_any,
    chip1, bound, top, own, t, s, u, v, w, dc, flag, depth, sems,
):
    sources = (flag_any, depth_any, t_any, s_any, u_any, v_any, w_any, dc_any)
    targets = (flag, depth, t, s, u, v, w, dc)
    copies = [pltpu.make_async_copy(x, y, sems.at[n]) for n, (x, y) in enumerate(zip(sources, targets))]
    for copy in copies:
        copy.start()
    levels, rows, lanes = t.shape
    _, j = position()
    _, group, spot = lanes_of(rows, lanes)
    zero = jnp.zeros((rows, lanes), F32)
    chip1[...] = jnp.zeros(chip1.shape, F32)
    for copy in copies[:2]:
        copy.wait()
    flags, depths = flag[...], depth[...]
    fields = dict(t=t, s=s, u=u, v=v, w=w)
    held = {}
    for n, name in ((5, "m"), (0, "t"), (1, "s"), (2, "u"), (3, "v"), (4, "w")):
        if name != "m":
            copies[2 + n].wait()
        for parity in range(2):
            out = zero
            for g in range(levels // 2):
                k = 2 * g + parity
                if name == "w" and k == levels - 1:
                    continue
                x = wet_of(flags, depths, k) if name == "m" else fields[name][k]
                out = jnp.where(group == g, roll(x, 16 * g + 6, 1), out)
            own[n, parity] = out
            held[name, parity] = out
    edges = []
    for parity in range(2):
        up, down, across = zero, zero, zero
        for name, start, count in SPOTS:
            x = held[name, parity]
            mine = (spot >= start) & (spot < start + count)
            up = jnp.where(mine, roll(x, start - (6 - count), 1), up)
            down = jnp.where(mine, roll(x, start - 6, 1), down)
            x = -x if name in ("u", "v") else x
            for d in range(count):
                at = (4, 3, 5)[d] if name == "v" else 5 - d
                across = jnp.where(spot == start + d, roll(x, start + d - at, 1), across)
        top[parity] = across
        bound[parity] = jnp.where(j == 0, up, down)
        edges.append(across)
    edges += [bound[0], bound[1]]

    def fill(even):
        a = 0 if even else rows - 3
        for n, x in enumerate(edges):
            chip1[3 * n : 3 * n + 3] = x[a : a + 3]

    by_parity(fill)
    copies[7].wait()


def pack_columns(t, s, u, v, w, flag, depth, bound, top, core, chip):
    levels, rows, lanes = t.shape
    flags, depths = flag[...], depth[...]
    core[levels] = jnp.zeros((rows, lanes), F32)

    def sides(out, east):
        a, c = (rows - 3, rows - 2) if east else (0, 0)
        for k in range(levels):
            out[k, 0:3] = t[k, a : a + 3]
            out[k, 3:6] = s[k, a : a + 3]
            out[k, 6:9] = u[k, a : a + 3]
            out[k, 9:11] = v[k, c : c + 2]
            if k < levels - 1:
                out[k, 11:13] = w[k, c : c + 2]
            else:
                out[k, 11:13] = jnp.zeros((2, lanes), F32)
            out[k, 13:16] = wet_of(flags, depths, k)[a : a + 3]

    def fill(even):
        sides(core, even)
        sides(chip, not even)
        a = rows - 3 if even else 0
        for n, x in enumerate((top, bound)):
            for parity in range(2):
                at = 6 * n + 3 * parity
                core[levels, at : at + 3] = x[parity, a : a + 3]

    by_parity(fill)


def repack(top, bound, core, chip1, fold, lat):
    levels = core.shape[0] - 1
    rows, _ = top.shape[1:]
    wide = rows + 8
    fold[...] = jnp.zeros(fold.shape, F32)
    lat[...] = jnp.zeros(lat.shape, F32)
    for parity in range(2):
        fold[wide * parity + 4 : wide * parity + 4 + rows] = top[parity]
        lat[wide * parity + 4 : wide * parity + 4 + rows] = bound[parity]
    fold[2 * wide : 2 * wide + 6] = chip1[6:12]

    def fill(even):
        for n, out in enumerate((fold, lat)):
            for parity in range(2):
                part = 6 * n + 3 * parity
                near, far = core[levels, part : part + 3], chip1[part : part + 3]
                east, west = (near, far) if even else (far, near)
                at = wide * parity
                out[at + 1 : at + 4] = west
                out[at + rows + 4 : at + rows + 7] = east

    by_parity(fill)


def columns(src, east, cells, levels, rows):
    ct, cs, cu, cv, cw, cm = cells
    a = OWN + rows if east else OWN - 3
    b = OWN + rows if east else OWN - 2
    for k in range(levels):
        ct[k + 1, a : a + 3] = src[k, 0:3]
        cs[k + 1, a : a + 3] = src[k, 3:6]
        cu[k + 1, a : a + 3] = src[k, 6:9]
        cv[k + 1, b : b + 2] = src[k, 9:11]
        cw[k + 1, b : b + 2] = src[k, 11:13]
        cm[k + 1, a : a + 3] = src[k, 13:16]


def at_strips(src, out, levels, rows, lanes):
    _, group, _ = lanes_of(rows, lanes)
    for parity in range(2):
        x = jnp.zeros((rows, lanes), F32)
        for g in range(levels // 2):
            x = jnp.where(group == g, roll(src[2 * g + parity], 16 * g + 6, 1), x)
        out[parity] = x


def prepare(t, s, u, v, w, dc, flag, depth, core, inverse, onward, back, core_side, ct, cs, cu, cv, cw, cm):
    levels, rows, lanes = t.shape
    flags, depths = flag[...], depth[...]
    zero = jnp.zeros(flags.shape, F32)
    q = [zero]
    for k in range(1, levels):
        q.append(dc[k - 1] * wet_of(flags, depths, k))
    q.append(zero)
    ratio = zero
    for k in range(levels):
        denom = 1.0 + q[k] + q[k + 1] - q[k] * ratio
        inv = 1.0 / denom
        ratio = q[k + 1] * inv
        inverse[k] = inv
        onward[k] = q[k] * inv
        back[k] = ratio
    for ref in (ct, cs, cu, cv, cw, cm):
        for k in (0, levels + 1):
            ref[k] = jnp.zeros(ref.shape[1:], F32)
    for k in range(levels):
        ct[k + 1, OWN : OWN + rows] = t[k]
        cs[k + 1, OWN : OWN + rows] = s[k]
        cu[k + 1, OWN : OWN + rows] = u[k]
        cv[k + 1, OWN : OWN + rows] = v[k]
        cw[k + 1, OWN : OWN + rows] = w[k] if k < levels - 1 else zero
        cm[k + 1, OWN : OWN + rows] = wet_of(flags, depths, k)
    at_strips(core, core_side, levels, rows, lanes)
    by_parity(lambda even: columns(core, even, (ct, cs, cu, cv, cw, cm), levels, rows))


def low_and_anti(speed):
    parts = jnp.maximum(speed, 0.0), jnp.minimum(speed, 0.0), 0.5 * jnp.abs(speed)
    return lambda a, b: (parts[0] * a + parts[1] * b, parts[2] * (b - a))


def limited(anti, rise_a, drop_a, rise_b, drop_b):
    return anti * jnp.where(anti >= 0.0, jnp.minimum(rise_b, drop_a), jnp.minimum(rise_a, drop_b))


def ratios(lowered, top_value, low_value, inward, outward):
    gain = sum(jnp.maximum(x, 0.0) for x in inward) - sum(jnp.minimum(x, 0.0) for x in outward)
    loss = gain + (sum(outward) - sum(inward))
    rise = jnp.minimum(1.0, (top_value - lowered) / jnp.maximum(gain, FLUX_FLOOR))
    drop = jnp.minimum(1.0, (lowered - low_value) / jnp.maximum(loss, FLUX_FLOOR))
    return rise, drop


def main(
    ct_in, cs_in, cu_in, cv_in, cw_in, cm_in, chip,
    adv_t, adv_s, chip_side, ct, cs, cu, cv, cw, cm,
    low_t, low_s, ae_t, ae_s, an_t, an_s, au_t, au_s, hi_t, hi_s, lo_t, lo_s, up_t, up_s, dn_t, dn_s, fe_t, fe_s,
):
    levels, rows, lanes = adv_t.shape
    wide = rows + 8
    here, to_east, to_west = pl.ds(8, wide), pl.ds(9, wide), pl.ds(7, wide)
    inner = pl.ds(OWN, rows)

    by_parity(lambda even: columns(chip, not even, (ct, cs, cu, cv, cw, cm), levels, rows))

    tracers = (
        (ct, low_t, ae_t, an_t, au_t, hi_t, lo_t, up_t, dn_t, fe_t, adv_t),
        (cs, low_s, ae_s, an_s, au_s, hi_s, lo_s, up_s, dn_s, fe_s, adv_s),
    )
    nothing = jnp.zeros((wide, lanes), F32)
    for _, low, ae, an, au, hi, lo, rise, drop, _, _ in tracers:
        au[0, here] = nothing
        for k in (0, levels + 1):
            hi[k, here] = nothing - BIG
            lo[k, here] = nothing + BIG
            rise[k, here] = nothing
            drop[k, here] = nothing

    def first_pass(k, carry):
        wet = cm[k, here]
        east = low_and_anti(cu[k, here] * (wet * cm[k, to_east]))
        north = low_and_anti(cv[k, here] * (wet * roll(wet, -1, 1)))
        upward = low_and_anti(cw[k, here] * (wet * cm[k + 1, here]))
        fluxes = []
        for n, (c, low, ae, an, au, hi, lo, _, _, face, _) in enumerate(tracers):
            x = c[k, here]
            fe, ae[k, here] = east(x, c[k, to_east])
            fn, an[k, here] = north(x, roll(x, -1, 1))
            fu, au[k, here] = upward(c[k + 1, here], x)
            face[k, here] = fe
            fluxes.append(fu)
            lowered = x - ((fe - face[k, to_west]) + (fn - roll(fn, 1, 1)) + (carry[n] - fu))
            low[k, here] = lowered
            dry = wet == 0.0
            hi[k, here] = jnp.where(dry, -BIG, jnp.maximum(x, lowered))
            lo[k, here] = jnp.where(dry, BIG, jnp.minimum(x, lowered))
        return tuple(fluxes)

    lax.fori_loop(1, levels + 1, first_pass, (nothing, nothing), unroll=UNROLL[0])

    def second_pass(k, carry):
        for _, low, ae, an, au, hi, lo, rise, drop, _, _ in tracers:
            top_value, low_value = hi[k, here], lo[k, here]
            for x in (hi[k, to_east], hi[k, to_west], roll(top_value, -1, 1), roll(top_value, 1, 1),
                      hi[k + 1, here], hi[k - 1, here]):
                top_value = jnp.maximum(top_value, x)
            for x in (lo[k, to_east], lo[k, to_west], roll(low_value, -1, 1), roll(low_value, 1, 1),
                      lo[k + 1, here], lo[k - 1, here]):
                low_value = jnp.minimum(low_value, x)
            anti_n = an[k, here]
            rise[k, here], drop[k, here] = ratios(
                low[k, here], top_value, low_value,
                (ae[k, to_west], roll(anti_n, 1, 1), au[k, here]), (ae[k, here], anti_n, au[k - 1, here]),
            )
        return carry

    lax.fori_loop(1, levels + 1, second_pass, 0, unroll=UNROLL[1])

    def third_pass(k, carry):
        fluxes = []
        for n, (_, low, ae, an, au, _, _, rise, drop, face, adv) in enumerate(tracers):
            r, d = rise[k, here], drop[k, here]
            fe = limited(ae[k, here], r, d, rise[k, to_east], drop[k, to_east])
            face[k, here] = fe
            r, d = rise[k, inner], drop[k, inner]
            fn = limited(an[k, inner], r, d, roll(r, -1, 1), roll(d, -1, 1))
            fu = limited(au[k, inner], rise[k + 1, inner], drop[k + 1, inner], r, d)
            fluxes.append(fu)
            out = (face[k, inner] - face[k, pl.ds(OWN - 1, rows)]) + (fn - roll(fn, 1, 1)) + (carry[n] - fu)
            adv[k - 1] = low[k, inner] - out
        return tuple(fluxes)

    no_flux = jnp.zeros((rows, lanes), F32)
    lax.fori_loop(1, levels + 1, third_pass, (no_flux, no_flux), unroll=UNROLL[2])

    at_strips(chip, chip_side, levels, rows, lanes)


def strip_advection(scratch, levels, rows, lanes):
    (ct, cs, cu, cv, cw, cm, low_t, low_s, ae_t, ae_s, an_t, an_s, au_t, au_s, hi_t, hi_s, lo_t, lo_s,
     up_t, up_s, dn_t, dn_s, fe_t, fe_s) = scratch
    wide = rows + 8
    _, group, _ = lanes_of(wide, lanes)
    here, to_east, to_west = pl.ds(8, wide), pl.ds(9, wide), pl.ds(7, wide)
    lowest = group == levels // 2 - 1
    highest = group == 0

    def below(ref, k, edge_value=None):
        if k % 2 == 0:
            return ref[k + 1, here]
        x = roll(ref[k - 1, here], -16, 1)
        return x if edge_value is None else jnp.where(lowest, edge_value, x)

    def above(ref, k, edge_value):
        if k % 2 == 1:
            return ref[k - 1, here]
        return jnp.where(highest, edge_value, roll(ref[k + 1, here], 16, 1))

    tracers = (
        (ct, low_t, ae_t, an_t, au_t, hi_t, lo_t, up_t, dn_t, fe_t),
        (cs, low_s, ae_s, an_s, au_s, hi_s, lo_s, up_s, dn_s, fe_s),
    )
    ends = (0, 1)
    tops = [[None, None], [None, None]]
    for k in ends:
        wet = cm[k, here]
        east = low_and_anti(cu[k, here] * (wet * cm[k, to_east]))
        north = low_and_anti(cv[k, here] * (wet * roll(wet, -1, 1)))
        upward = low_and_anti(cw[k, here] * (wet * below(cm, k, 0.0)))
        for n, (c, low, ae, an, au, hi, lo, _, _, face) in enumerate(tracers):
            x = c[k, here]
            fe, ae[k, here] = east(x, c[k, to_east])
            fn, an[k, here] = north(x, roll(x, -1, 1))
            fu, au[k, here] = upward(below(c, k), x)
            face[k, here] = fe
            tops[n][k % 2] = fu
            low[k, here] = x - ((fe - face[k, to_west]) + (fn - roll(fn, 1, 1)) - fu)
    for k in ends:
        dry = cm[k, here] == 0.0
        for n, (c, low, ae, an, au, hi, lo, _, _, _) in enumerate(tracers):
            over = tops[n][0] if k % 2 == 1 else jnp.where(highest, 0.0, roll(tops[n][1], 16, 1))
            x, lowered = c[k, here], low[k, here] - over
            low[k, here] = lowered
            hi[k, here] = jnp.where(dry, -BIG, jnp.maximum(x, lowered))
            lo[k, here] = jnp.where(dry, BIG, jnp.minimum(x, lowered))
    for k in ends:
        for _, low, ae, an, au, hi, lo, rise, drop, _ in tracers:
            top_value, low_value = hi[k, here], lo[k, here]
            for x in (hi[k, to_east], hi[k, to_west], roll(top_value, -1, 1), roll(top_value, 1, 1),
                      below(hi, k, -BIG), above(hi, k, -BIG)):
                top_value = jnp.maximum(top_value, x)
            for x in (lo[k, to_east], lo[k, to_west], roll(low_value, -1, 1), roll(low_value, 1, 1),
                      below(lo, k, BIG), above(lo, k, BIG)):
                low_value = jnp.minimum(low_value, x)
            anti_n = an[k, here]
            rise[k, here], drop[k, here] = ratios(
                low[k, here], top_value, low_value,
                (ae[k, to_west], roll(anti_n, 1, 1), au[k, here]), (ae[k, here], anti_n, above(au, k, 0.0)),
            )
    for k in ends:
        for _, low, ae, an, au, hi, _, rise, drop, face in tracers:
            r, d = rise[k, here], drop[k, here]
            face[k, here] = limited(ae[k, here], r, d, rise[k, to_east], drop[k, to_east])
            hi[k, here] = limited(au[k, here], below(rise, k), below(drop, k), r, d)
    for k in ends:
        for _, low, ae, an, au, hi, lo, rise, drop, face in tracers:
            r, d = rise[k, here], drop[k, here]
            fn = limited(an[k, here], r, d, roll(r, -1, 1), roll(d, -1, 1))
            out = (face[k, here] - face[k, to_west]) + (fn - roll(fn, 1, 1))
            lo[k, here] = low[k, here] - (out + (above(hi, k, 0.0) - hi[k, here]))


def strip_cells(scratch, own, core_side, chip_side):
    cells, rows = scratch[:6], own.shape[2]
    for n, ref in enumerate(cells):
        for parity in range(2):
            ref[parity, OWN : OWN + rows] = own[n, parity]

    def fill(even):
        for side, east in ((core_side, even), (chip_side, not even)):
            for ref, start, count in zip(cells, (0, 3, 6, 9, 11, 13), (3, 3, 3, 2, 2, 3)):
                a = OWN + rows if east else OWN - count
                for parity in range(2):
                    ref[parity, a : a + count] = side[parity, start : start + count]

    by_parity(fill)


def south_strip(scratch, own, core_side, chip_side, edge, levels, out):
    rows, lanes = own.shape[2:]
    wide = rows + 8
    _, _, spot = lanes_of(wide, lanes)
    _, j = position()
    here = pl.ds(8, wide)
    strip_cells(scratch, own, core_side, chip_side)
    for parity in range(2):
        for ref, (name, start, count) in zip(scratch, SPOTS):
            value = jnp.where(spot < 6, roll(edge[parity], 6 - count - start, 1), ref[parity, here])
            if name == "m":
                value = jnp.where((spot < 3) | (spot > 11) | ((spot < 6) & (j == 0)), 0.0, value)
            ref[parity, here] = value
    strip_advection(scratch, levels, rows, lanes)
    for n in range(2):
        for parity in range(2):
            out[n, parity] = scratch[16 + n][parity, OWN : OWN + rows]


def south(adv_t, own, core_side, chip_side, lat, out, edge, *scratch):
    levels, rows, _ = adv_t.shape
    for parity in range(2):
        edge[parity] = lat[(rows + 8) * parity : (rows + 8) * (parity + 1)]
    south_strip(scratch, own, core_side, chip_side, edge, levels, out)


def finish(
    adv_t, adv_s, inverse, onward, back, own, core_side, chip_side, top, lat, fold, south_in,
    new_t, new_s, edge, mirror, south_end, *scratch,
):
    i, j = position()
    n_lon, n_lat = lax.axis_size("lon"), lax.axis_size("lat")
    first, last, is_top = i == 0, i == n_lon - 1, j == n_lat - 1
    levels, rows, lanes = adv_t.shape
    wide = rows + 8
    _, _, spot = lanes_of(wide, lanes)
    here = pl.ds(8, wide)

    for parity in range(2):
        edge[parity] = lat[wide * parity : wide * parity + wide]
        edge[2 + parity] = fold[wide * parity : wide * parity + wide]
    south_end[...] = south_in[...]

    @pl.when(first)
    def _():
        for parity in range(2):
            edge[parity, 1:4] = fold[2 * wide + 3 * parity : 2 * wide + 3 * parity + 3]
            edge[2 + parity, rows + 4 : rows + 7] = top[parity, 0:3]

    @pl.when(last)
    def _():
        for parity in range(2):
            edge[parity, rows + 4 : rows + 7] = fold[2 * wide + 3 * parity : 2 * wide + 3 * parity + 3]
            edge[2 + parity, 1:4] = top[parity, rows - 3 : rows]

    @pl.when((first | last) & (j > 0))
    def _():
        south_strip(scratch, own, core_side, chip_side, edge, levels, south_end)

    for parity in range(2):
        for r in range(wide):
            q = wide - 1 - r
            mirror[parity, r : r + 1] = edge[2 + parity, q : q + 1]

    strip_cells(scratch, own, core_side, chip_side)
    _, u_start, u_count = SPOTS[2]
    for parity in range(2):
        other, mir = edge[parity], mirror[parity]
        mir = jnp.where((spot >= u_start) & (spot < u_start + u_count), roll(mir, -1, 0), mir)
        source = jnp.where(is_top, mir, other)
        for ref, (name, start, count) in zip(scratch, SPOTS):
            mine = ref[parity, here]
            value = jnp.where(spot < 6, mine, roll(source, 6 - start, 1))
            if name == "v":
                folded = 0.5 * (mine + roll(source, 5 - (start + 2), 1))
                value = jnp.where((spot == 5) & is_top, folded, value)
            if name == "m":
                value = jnp.where(spot > 8, 0.0, value)
            ref[parity, here] = value
    strip_advection(scratch, levels, rows, lanes)

    _, _, place = lanes_of(rows, lanes)
    ends = [
        [jnp.where(place < 6, scratch[16 + n][parity, OWN : OWN + rows], south_end[n, parity]) for parity in range(2)]
        for n in range(2)
    ]
    lane, _, _ = lanes_of(rows, lanes)
    outer = (lane < 3) | (lane >= lanes - 3)
    solved = [None, None]
    for k in range(levels):
        for n, (adv, out) in enumerate(((adv_t, new_t), (adv_s, new_s))):
            x = jnp.where(outer, roll(ends[n][k % 2], -(16 * (k // 2) + 6), 1), adv[k]) * inverse[k]
            solved[n] = x if k == 0 else x + onward[k] * solved[n]
            out[k] = solved[n]
    for k in range(levels - 2, -1, -1):
        for n, out in enumerate((new_t, new_s)):
            solved[n] = out[k] + back[k] * solved[n]
            out[k] = solved[n]


def call(body, outs, args, scratch=(), aliases=None, limit=8, flops=2_000_000):
    vmem = pl.BlockSpec(memory_space=pltpu.VMEM)
    outs = [x if hasattr(x, "dtype") else jax.ShapeDtypeStruct(x, F32) for x in outs]
    where = pltpu.HBM if body is pack else pltpu.VMEM
    return pl.pallas_call(
        body,
        out_shape=tuple(outs),
        in_specs=[pl.BlockSpec(memory_space=where)] * len(args),
        out_specs=tuple(vmem for _ in outs),
        scratch_shapes=[x if not isinstance(x, tuple) else pltpu.VMEM(x, F32) for x in scratch],
        input_output_aliases=aliases or {},
        compiler_params=pltpu.CompilerParams(vmem_limit_bytes=limit * 2**20),
        cost_estimate=pl.CostEstimate(flops=flops, bytes_accessed=2_000_000, transcendentals=0),
    )(*args)


def local(n_lon, n_lat, *args):
    levels, rows, lanes = args[0].shape
    wide = rows + 8

    def number(i, j):
        return (i % n_lon) * n_lat + j

    grid = [(i, j) for i in range(n_lon) for j in range(n_lat)]

    def beside(i):
        return i - 1 if i % 2 == 0 else i + 1

    cores = [(number(i, j), number(i ^ 1, j)) for i, j in grid]
    chips = [(number(i, j), number(beside(i), j)) for i, j in grid]
    lats = [(number(i, j), number(i, n_lat - 1 - j)) for i, j in grid]
    folds = [(number(i, j), number(n_lon - 1 - i, j)) for i, j in grid]
    ends = [(number(i, j), number(i, n_lat - 1 - j)) for i, j in grid if i in (0, n_lon - 1)]
    inner = [(number(i, j), number(beside(i), j)) for i, j in grid if 0 < i < n_lon - 1] + ends

    def send(x, pairs):
        return lax.ppermute(x, AXES, pairs)

    chip1, bound, top, own, *held = call(
        pack,
        [(16, lanes)] + [(2, rows, lanes)] * 2 + [(6, 2, rows, lanes)]
        + [jax.ShapeDtypeStruct(x.shape, x.dtype) for x in args],
        [pltpu.with_memory_space_constraint(x, pltpu.HBM) for x in args],
        [pltpu.SemaphoreType.DMA((len(args),))],
    )
    chip1_in = send(chip1, inner)
    core, chip = call(
        pack_columns,
        [(levels + 1, rows, lanes), (levels, rows, lanes)],
        (*held[:5], *held[6:], bound, top),
    )
    core_in = send(core, cores)
    chip_in = send(chip, chips)
    cell = (levels + 2, 40, lanes)
    inverse, onward, back, core_side, *cells = call(
        prepare, [(levels, rows, lanes)] * 3 + [(2, rows, lanes)] + [cell] * 6, (*held, core_in)
    )
    fold, lat = call(repack, [(2 * wide + 8, lanes), (2 * wide, lanes)], (top, bound, core_in, chip1_in), limit=2)
    fold_in = send(fold, folds)
    lat_in = send(lat, lats)
    adv_t, adv_s, chip_side, *_ = call(
        main,
        [(levels, rows, lanes)] * 2 + [(2, rows, lanes)] + [cell] * 6,
        (*cells, chip_in),
        [cell] * 18,
        aliases={n: 3 + n for n in range(6)},
        limit=20,
        flops=20_000_000,
    )
    strip = (2, 40, lanes)
    south_in = call(
        south,
        [(2, 2, rows, lanes)],
        (adv_t, own, core_side, chip_side, lat_in),
        [(2, wide, lanes)] + [strip] * 24,
    )[0]
    return call(
        finish,
        [(levels, rows, lanes)] * 2,
        (adv_t, adv_s, inverse, onward, back, own, core_side, chip_side, top, lat_in, fold_in, south_in),
        [(4, wide, lanes), (2, wide, lanes), (2, 2, rows, lanes)] + [strip] * 24,
    )


def solution(mesh):
    n_lon, n_lat = mesh.shape["lon"], mesh.shape["lat"]
    cube = P(None, "lon", "lat")
    plane = P("lon", "lat")
    return jax.shard_map(
        lambda *args: tuple(local(n_lon, n_lat, *args)),
        mesh=mesh,
        in_specs=(cube,) * 6 + (plane,) * 2,
        out_specs=(cube, cube),
        check_vma=False,
    )
```

```python
import jax
import jax.numpy as jnp
from jax import lax
from jax.experimental import pallas as pl
from jax.experimental.pallas import tpu as pltpu
from jax.sharding import PartitionSpec as P


FLUX_FLOOR = 0.01
BIG = 1e30
AXES = ("lon", "lat")
F32 = jnp.float32


SPOTS = (("t", 0, 3), ("s", 3, 3), ("u", 6, 2), ("v", 8, 3), ("w", 11, 2), ("m", 13, 3))
OWN = 12
UNROLL = (8, 8, 8)


def roll(x, shift, axis):
    if not isinstance(shift, int):
        return pltpu.roll(x, shift, axis)
    shift = shift % x.shape[axis]
    return x if shift == 0 else pltpu.roll(x, shift, axis)


def position():
    return lax.axis_index("lon"), lax.axis_index("lat")


def by_parity(body):
    even = lax.rem(lax.axis_index("lon"), 2) == 0

    @pl.when(even)
    def _():
        body(True)

    @pl.when(jnp.logical_not(even))
    def _():
        body(False)


def lanes_of(rows, lanes):
    lane = lax.broadcasted_iota(jnp.int32, (rows, lanes), 1)
    return lane, lane >> 4, lane & 15


def wet_of(flag, depth, level):
    return jnp.where((level < depth) & (flag > 0), 1.0, 0.0).astype(F32)


def pack(
    t_any, s_any, u_any, v_any, w_any, dc_any, flag_any, depth_any,
    chip1, bound, top, own, t, s, u, v, w, dc, flag, depth, sems,
):
    sources = (flag_any, depth_any, t_any, s_any, u_any, v_any, w_any, dc_any)
    targets = (flag, depth, t, s, u, v, w, dc)
    copies = [pltpu.make_async_copy(x, y, sems.at[n]) for n, (x, y) in enumerate(zip(sources, targets))]
    for copy in copies:
        copy.start()
    levels, rows, lanes = t.shape
    _, j = position()
    _, group, spot = lanes_of(rows, lanes)
    zero = jnp.zeros((rows, lanes), F32)
    chip1[...] = jnp.zeros(chip1.shape, F32)
    for copy in copies[:2]:
        copy.wait()
    flags, depths = flag[...], depth[...]
    fields = dict(t=t, s=s, u=u, v=v, w=w)
    held = {}
    for n, name in ((5, "m"), (0, "t"), (1, "s"), (2, "u"), (3, "v"), (4, "w")):
        if name != "m":
            copies[2 + n].wait()
        for parity in range(2):
            out = zero
            for g in range(levels // 2):
                k = 2 * g + parity
                if name == "w" and k == levels - 1:
                    continue
                x = wet_of(flags, depths, k) if name == "m" else fields[name][k]
                out = jnp.where(group == g, roll(x, 16 * g + 6, 1), out)
            own[n, parity] = out
            held[name, parity] = out
    edges = []
    for parity in range(2):
        up, down, across = zero, zero, zero
        for name, start, count in SPOTS:
            x = held[name, parity]
            mine = (spot >= start) & (spot < start + count)
            up = jnp.where(mine, roll(x, start - (6 - count), 1), up)
            down = jnp.where(mine, roll(x, start - 6, 1), down)
            x = -x if name in ("u", "v") else x
            for d in range(count):
                at = (4, 3, 5)[d] if name == "v" else 5 - d
                across = jnp.where(spot == start + d, roll(x, start + d - at, 1), across)
        top[parity] = across
        bound[parity] = jnp.where(j == 0, up, down)
        edges.append(across)
    edges += [bound[0], bound[1]]

    def fill(even):
        a = 0 if even else rows - 3
        for n, x in enumerate(edges):
            chip1[3 * n : 3 * n + 3] = x[a : a + 3]

    by_parity(fill)
    copies[7].wait()


def pack_columns(t, s, u, v, w, flag, depth, bound, top, core, chip):
    levels, rows, lanes = t.shape
    flags, depths = flag[...], depth[...]
    core[levels] = jnp.zeros((rows, lanes), F32)

    def sides(out, east):
        a, c = (rows - 3, rows - 2) if east else (0, 0)
        for k in range(levels):
            out[k, 0:3] = t[k, a : a + 3]
            out[k, 3:6] = s[k, a : a + 3]
            out[k, 6:9] = u[k, a : a + 3]
            out[k, 9:11] = v[k, c : c + 2]
            if k < levels - 1:
                out[k, 11:13] = w[k, c : c + 2]
            else:
                out[k, 11:13] = jnp.zeros((2, lanes), F32)
            out[k, 13:16] = wet_of(flags, depths, k)[a : a + 3]

    def fill(even):
        sides(core, even)
        sides(chip, not even)
        a = rows - 3 if even else 0
        for n, x in enumerate((top, bound)):
            for parity in range(2):
                at = 6 * n + 3 * parity
                core[levels, at : at + 3] = x[parity, a : a + 3]

    by_parity(fill)


def repack(top, bound, core, chip1, fold, lat):
    levels = core.shape[0] - 1
    rows, _ = top.shape[1:]
    wide = rows + 8
    fold[...] = jnp.zeros(fold.shape, F32)
    lat[...] = jnp.zeros(lat.shape, F32)
    for parity in range(2):
        fold[wide * parity + 4 : wide * parity + 4 + rows] = top[parity]
        lat[wide * parity + 4 : wide * parity + 4 + rows] = bound[parity]
    fold[2 * wide : 2 * wide + 6] = chip1[6:12]

    def fill(even):
        for n, out in enumerate((fold, lat)):
            for parity in range(2):
                part = 6 * n + 3 * parity
                near, far = core[levels, part : part + 3], chip1[part : part + 3]
                east, west = (near, far) if even else (far, near)
                at = wide * parity
                out[at + 1 : at + 4] = west
                out[at + rows + 4 : at + rows + 7] = east

    by_parity(fill)


def columns(src, east, cells, levels, rows):
    ct, cs, cu, cv, cw, cm = cells
    a = OWN + rows if east else OWN - 3
    b = OWN + rows if east else OWN - 2
    for k in range(levels):
        ct[k + 1, a : a + 3] = src[k, 0:3]
        cs[k + 1, a : a + 3] = src[k, 3:6]
        cu[k + 1, a : a + 3] = src[k, 6:9]
        cv[k + 1, b : b + 2] = src[k, 9:11]
        cw[k + 1, b : b + 2] = src[k, 11:13]
        cm[k + 1, a : a + 3] = src[k, 13:16]


def at_strips(src, out, levels, rows, lanes):
    _, group, _ = lanes_of(rows, lanes)
    for parity in range(2):
        x = jnp.zeros((rows, lanes), F32)
        for g in range(levels // 2):
            x = jnp.where(group == g, roll(src[2 * g + parity], 16 * g + 6, 1), x)
        out[parity] = x


def prepare(t, s, u, v, w, dc, flag, depth, core, inverse, onward, back, core_side, ct, cs, cu, cv, cw, cm):
    levels, rows, lanes = t.shape
    flags, depths = flag[...], depth[...]
    zero = jnp.zeros(flags.shape, F32)
    q = [zero]
    for k in range(1, levels):
        q.append(dc[k - 1] * wet_of(flags, depths, k))
    q.append(zero)
    ratio = zero
    for k in range(levels):
        denom = 1.0 + q[k] + q[k + 1] - q[k] * ratio
        inv = 1.0 / denom
        ratio = q[k + 1] * inv
        inverse[k] = inv
        onward[k] = q[k] * inv
        back[k] = ratio
    for ref in (ct, cs, cu, cv, cw, cm):
        for k in (0, levels + 1):
            ref[k] = jnp.zeros(ref.shape[1:], F32)
    for k in range(levels):
        ct[k + 1, OWN : OWN + rows] = t[k]
        cs[k + 1, OWN : OWN + rows] = s[k]
        cu[k + 1, OWN : OWN + rows] = u[k]
        cv[k + 1, OWN : OWN + rows] = v[k]
        cw[k + 1, OWN : OWN + rows] = w[k] if k < levels - 1 else zero
        cm[k + 1, OWN : OWN + rows] = wet_of(flags, depths, k)
    at_strips(core, core_side, levels, rows, lanes)
    by_parity(lambda even: columns(core, even, (ct, cs, cu, cv, cw, cm), levels, rows))


def low_and_anti(speed):
    parts = jnp.maximum(speed, 0.0), jnp.minimum(speed, 0.0), 0.5 * jnp.abs(speed)
    return lambda a, b: (parts[0] * a + parts[1] * b, parts[2] * (b - a))


def limited(anti, rise_a, drop_a, rise_b, drop_b):
    return anti * jnp.where(anti >= 0.0, jnp.minimum(rise_b, drop_a), jnp.minimum(rise_a, drop_b))


def ratios(lowered, top_value, low_value, inward, outward):
    (a, b, c), (x, y, z) = inward, outward
    gain = (jnp.maximum(a, 0.0) + jnp.maximum(b, 0.0) + jnp.maximum(c, 0.0)) - (
        jnp.minimum(x, 0.0) + jnp.minimum(y, 0.0) + jnp.minimum(z, 0.0)
    )
    loss = gain + ((x - a) + (y - b) + (z - c))
    rise = jnp.minimum(1.0, (top_value - lowered) / jnp.maximum(gain, FLUX_FLOOR))
    drop = jnp.minimum(1.0, (lowered - low_value) / jnp.maximum(loss, FLUX_FLOOR))
    return rise, drop


def main(
    ct_in, cs_in, cu_in, cv_in, cw_in, cm_in, chip,
    adv_t, adv_s, chip_side, ct, cs, cu, cv, cw, cm,
    low_t, low_s, ae_t, ae_s, an_t, an_s, au_t, au_s, hi_t, hi_s, lo_t, lo_s, up_t, up_s, dn_t, dn_s, fe_t, fe_s,
):
    levels, rows, lanes = adv_t.shape
    wide = rows + 8
    here, to_east, to_west = pl.ds(8, wide), pl.ds(9, wide), pl.ds(7, wide)
    inner = pl.ds(OWN, rows)

    by_parity(lambda even: columns(chip, not even, (ct, cs, cu, cv, cw, cm), levels, rows))

    tracers = (
        (ct, low_t, ae_t, an_t, au_t, hi_t, lo_t, up_t, dn_t, fe_t, adv_t),
        (cs, low_s, ae_s, an_s, au_s, hi_s, lo_s, up_s, dn_s, fe_s, adv_s),
    )
    nothing = jnp.zeros((wide, lanes), F32)
    for _, low, ae, an, au, hi, lo, rise, drop, _, _ in tracers:
        au[0, here] = nothing
        for k in (0, levels + 1):
            hi[k, here] = nothing - BIG
            lo[k, here] = nothing + BIG
            rise[k, here] = nothing
            drop[k, here] = nothing

    def first_pass(k, carry):
        wet = cm[k, here]
        east = low_and_anti(cu[k, here] * (wet * cm[k, to_east]))
        north = low_and_anti(cv[k, here] * (wet * roll(wet, -1, 1)))
        upward = low_and_anti(cw[k, here] * (wet * cm[k + 1, here]))
        fluxes = []
        for n, (c, low, ae, an, au, hi, lo, _, _, face, _) in enumerate(tracers):
            x = c[k, here]
            fe, ae[k, here] = east(x, c[k, to_east])
            fn, an[k, here] = north(x, roll(x, -1, 1))
            fu, au[k, here] = upward(c[k + 1, here], x)
            face[k, here] = fe
            fluxes.append(fu)
            lowered = x - ((fe - face[k, to_west]) + (fn - roll(fn, 1, 1)) + (carry[n] - fu))
            low[k, here] = lowered
            dry = wet == 0.0
            hi[k, here] = jnp.where(dry, -BIG, jnp.maximum(x, lowered))
            lo[k, here] = jnp.where(dry, BIG, jnp.minimum(x, lowered))
        return tuple(fluxes)

    lax.fori_loop(1, levels + 1, first_pass, (nothing, nothing), unroll=UNROLL[0])

    def second_pass(k, carry):
        for _, low, ae, an, au, hi, lo, rise, drop, _, _ in tracers:
            top_value, low_value = hi[k, here], lo[k, here]
            for x in (hi[k, to_east], hi[k, to_west], roll(top_value, -1, 1), roll(top_value, 1, 1),
                      hi[k + 1, here], hi[k - 1, here]):
                top_value = jnp.maximum(top_value, x)
            for x in (lo[k, to_east], lo[k, to_west], roll(low_value, -1, 1), roll(low_value, 1, 1),
                      lo[k + 1, here], lo[k - 1, here]):
                low_value = jnp.minimum(low_value, x)
            anti_n = an[k, here]
            rise[k, here], drop[k, here] = ratios(
                low[k, here], top_value, low_value,
                (ae[k, to_west], roll(anti_n, 1, 1), au[k, here]), (ae[k, here], anti_n, au[k - 1, here]),
            )
        return carry

    lax.fori_loop(1, levels + 1, second_pass, 0, unroll=UNROLL[1])

    def third_pass(k, carry):
        fluxes = []
        for n, (_, low, ae, an, au, _, _, rise, drop, face, adv) in enumerate(tracers):
            r, d = rise[k, here], drop[k, here]
            fe = limited(ae[k, here], r, d, rise[k, to_east], drop[k, to_east])
            face[k, here] = fe
            r, d = rise[k, inner], drop[k, inner]
            fn = limited(an[k, inner], r, d, roll(r, -1, 1), roll(d, -1, 1))
            fu = limited(au[k, inner], rise[k + 1, inner], drop[k + 1, inner], r, d)
            fluxes.append(fu)
            out = (face[k, inner] - face[k, pl.ds(OWN - 1, rows)]) + (fn - roll(fn, 1, 1)) + (carry[n] - fu)
            adv[k - 1] = low[k, inner] - out
        return tuple(fluxes)

    no_flux = jnp.zeros((rows, lanes), F32)
    lax.fori_loop(1, levels + 1, third_pass, (no_flux, no_flux), unroll=UNROLL[2])

    at_strips(chip, chip_side, levels, rows, lanes)


def strip_advection(scratch, levels, rows, lanes):
    (ct, cs, cu, cv, cw, cm, low_t, low_s, ae_t, ae_s, an_t, an_s, au_t, au_s, hi_t, hi_s, lo_t, lo_s,
     up_t, up_s, dn_t, dn_s, fe_t, fe_s) = scratch
    wide = rows + 8
    _, group, _ = lanes_of(wide, lanes)
    here, to_east, to_west = pl.ds(8, wide), pl.ds(9, wide), pl.ds(7, wide)
    lowest = group == levels // 2 - 1
    highest = group == 0

    def below(ref, k, edge_value=None):
        if k % 2 == 0:
            return ref[k + 1, here]
        x = roll(ref[k - 1, here], -16, 1)
        return x if edge_value is None else jnp.where(lowest, edge_value, x)

    def above(ref, k, edge_value):
        if k % 2 == 1:
            return ref[k - 1, here]
        return jnp.where(highest, edge_value, roll(ref[k + 1, here], 16, 1))

    tracers = (
        (ct, low_t, ae_t, an_t, au_t, hi_t, lo_t, up_t, dn_t, fe_t),
        (cs, low_s, ae_s, an_s, au_s, hi_s, lo_s, up_s, dn_s, fe_s),
    )
    ends = (0, 1)
    tops = [[None, None], [None, None]]
    for k in ends:
        wet = cm[k, here]
        east = low_and_anti(cu[k, here] * (wet * cm[k, to_east]))
        north = low_and_anti(cv[k, here] * (wet * roll(wet, -1, 1)))
        upward = low_and_anti(cw[k, here] * (wet * below(cm, k, 0.0)))
        for n, (c, low, ae, an, au, hi, lo, _, _, face) in enumerate(tracers):
            x = c[k, here]
            fe, ae[k, here] = east(x, c[k, to_east])
            fn, an[k, here] = north(x, roll(x, -1, 1))
            fu, au[k, here] = upward(below(c, k), x)
            face[k, here] = fe
            tops[n][k % 2] = fu
            low[k, here] = x - ((fe - face[k, to_west]) + (fn - roll(fn, 1, 1)) - fu)
    for k in ends:
        dry = cm[k, here] == 0.0
        for n, (c, low, ae, an, au, hi, lo, _, _, _) in enumerate(tracers):
            over = tops[n][0] if k % 2 == 1 else jnp.where(highest, 0.0, roll(tops[n][1], 16, 1))
            x, lowered = c[k, here], low[k, here] - over
            low[k, here] = lowered
            hi[k, here] = jnp.where(dry, -BIG, jnp.maximum(x, lowered))
            lo[k, here] = jnp.where(dry, BIG, jnp.minimum(x, lowered))
    for k in ends:
        for _, low, ae, an, au, hi, lo, rise, drop, _ in tracers:
            top_value, low_value = hi[k, here], lo[k, here]
            for x in (hi[k, to_east], hi[k, to_west], roll(top_value, -1, 1), roll(top_value, 1, 1),
                      below(hi, k, -BIG), above(hi, k, -BIG)):
                top_value = jnp.maximum(top_value, x)
            for x in (lo[k, to_east], lo[k, to_west], roll(low_value, -1, 1), roll(low_value, 1, 1),
                      below(lo, k, BIG), above(lo, k, BIG)):
                low_value = jnp.minimum(low_value, x)
            anti_n = an[k, here]
            rise[k, here], drop[k, here] = ratios(
                low[k, here], top_value, low_value,
                (ae[k, to_west], roll(anti_n, 1, 1), au[k, here]), (ae[k, here], anti_n, above(au, k, 0.0)),
            )
    for k in ends:
        for _, low, ae, an, au, hi, _, rise, drop, face in tracers:
            r, d = rise[k, here], drop[k, here]
            face[k, here] = limited(ae[k, here], r, d, rise[k, to_east], drop[k, to_east])
            hi[k, here] = limited(au[k, here], below(rise, k), below(drop, k), r, d)
    for k in ends:
        for _, low, ae, an, au, hi, lo, rise, drop, face in tracers:
            r, d = rise[k, here], drop[k, here]
            fn = limited(an[k, here], r, d, roll(r, -1, 1), roll(d, -1, 1))
            out = (face[k, here] - face[k, to_west]) + (fn - roll(fn, 1, 1))
            lo[k, here] = low[k, here] - (out + (above(hi, k, 0.0) - hi[k, here]))


def strip_cells(scratch, own, core_side, chip_side):
    cells, rows = scratch[:6], own.shape[2]
    for n, ref in enumerate(cells):
        for parity in range(2):
            ref[parity, OWN : OWN + rows] = own[n, parity]

    def fill(even):
        for side, east in ((core_side, even), (chip_side, not even)):
            for ref, start, count in zip(cells, (0, 3, 6, 9, 11, 13), (3, 3, 3, 2, 2, 3)):
                a = OWN + rows if east else OWN - count
                for parity in range(2):
                    ref[parity, a : a + count] = side[parity, start : start + count]

    by_parity(fill)


def south_strip(scratch, own, core_side, chip_side, edge, levels, out):
    rows, lanes = own.shape[2:]
    wide = rows + 8
    _, _, spot = lanes_of(wide, lanes)
    _, j = position()
    here = pl.ds(8, wide)
    strip_cells(scratch, own, core_side, chip_side)
    for parity in range(2):
        for ref, (name, start, count) in zip(scratch, SPOTS):
            value = jnp.where(spot < 6, roll(edge[parity], 6 - count - start, 1), ref[parity, here])
            if name == "m":
                value = jnp.where((spot < 3) | (spot > 11) | ((spot < 6) & (j == 0)), 0.0, value)
            ref[parity, here] = value
    strip_advection(scratch, levels, rows, lanes)
    for n in range(2):
        for parity in range(2):
            out[n, parity] = scratch[16 + n][parity, OWN : OWN + rows]


def south(adv_t, own, core_side, chip_side, lat, out, edge, *scratch):
    levels, rows, _ = adv_t.shape
    for parity in range(2):
        edge[parity] = lat[(rows + 8) * parity : (rows + 8) * (parity + 1)]
    south_strip(scratch, own, core_side, chip_side, edge, levels, out)


def finish(
    adv_t, adv_s, inverse, onward, back, own, core_side, chip_side, top, lat, fold, south_in,
    out_t, out_s, edge, mirror, south_end, new_t, new_s, sems, *scratch,
):
    i, j = position()
    n_lon, n_lat = lax.axis_size("lon"), lax.axis_size("lat")
    first, last, is_top = i == 0, i == n_lon - 1, j == n_lat - 1
    levels, rows, lanes = adv_t.shape
    wide = rows + 8
    _, _, spot = lanes_of(wide, lanes)
    here = pl.ds(8, wide)

    for parity in range(2):
        edge[parity] = lat[wide * parity : wide * parity + wide]
        edge[2 + parity] = fold[wide * parity : wide * parity + wide]
    south_end[...] = south_in[...]

    @pl.when(first)
    def _():
        for parity in range(2):
            edge[parity, 1:4] = fold[2 * wide + 3 * parity : 2 * wide + 3 * parity + 3]
            edge[2 + parity, rows + 4 : rows + 7] = top[parity, 0:3]

    @pl.when(last)
    def _():
        for parity in range(2):
            edge[parity, rows + 4 : rows + 7] = fold[2 * wide + 3 * parity : 2 * wide + 3 * parity + 3]
            edge[2 + parity, 1:4] = top[parity, rows - 3 : rows]

    @pl.when((first | last) & (j > 0))
    def _():
        south_strip(scratch, own, core_side, chip_side, edge, levels, south_end)

    for parity in range(2):
        for r in range(wide):
            q = wide - 1 - r
            mirror[parity, r : r + 1] = edge[2 + parity, q : q + 1]

    strip_cells(scratch, own, core_side, chip_side)
    _, u_start, u_count = SPOTS[2]
    for parity in range(2):
        other, mir = edge[parity], mirror[parity]
        mir = jnp.where((spot >= u_start) & (spot < u_start + u_count), roll(mir, -1, 0), mir)
        source = jnp.where(is_top, mir, other)
        for ref, (name, start, count) in zip(scratch, SPOTS):
            mine = ref[parity, here]
            value = jnp.where(spot < 6, mine, roll(source, 6 - start, 1))
            if name == "v":
                folded = 0.5 * (mine + roll(source, 5 - (start + 2), 1))
                value = jnp.where((spot == 5) & is_top, folded, value)
            if name == "m":
                value = jnp.where(spot > 8, 0.0, value)
            ref[parity, here] = value
    strip_advection(scratch, levels, rows, lanes)

    _, _, place = lanes_of(rows, lanes)
    ends = [
        [jnp.where(place < 6, scratch[16 + n][parity, OWN : OWN + rows], south_end[n, parity]) for parity in range(2)]
        for n in range(2)
    ]
    lane, _, _ = lanes_of(rows, lanes)
    outer = (lane < 3) | (lane >= lanes - 3)
    solved = [None, None]
    for k in range(levels):
        for n, (adv, out) in enumerate(((adv_t, new_t), (adv_s, new_s))):
            x = jnp.where(outer, roll(ends[n][k % 2], -(16 * (k // 2) + 6), 1), adv[k]) * inverse[k]
            solved[n] = x if k == 0 else x + onward[k] * solved[n]
            out[k] = solved[n]
    half = levels // 2
    copies = []

    def leave(start):
        for held, out in ((new_t, out_t), (new_s, out_s)):
            part = pl.ds(start, half)
            copies.append(pltpu.make_async_copy(held.at[part], out.at[part], sems.at[len(copies)]))
            copies[-1].start()

    for k in range(levels - 2, -1, -1):
        for n, out in enumerate((new_t, new_s)):
            solved[n] = out[k] + back[k] * solved[n]
            out[k] = solved[n]
        if k == half:
            leave(half)
    leave(0)
    for copy in copies:
        copy.wait()


def call(body, outs, args, scratch=(), aliases=None, limit=8, flops=2_000_000):
    vmem = pl.BlockSpec(memory_space=pltpu.VMEM)
    outs = [x if hasattr(x, "dtype") else jax.ShapeDtypeStruct(x, F32) for x in outs]
    where = pltpu.HBM if body is pack else pltpu.VMEM
    vmem = pl.BlockSpec(memory_space=pltpu.HBM) if body is finish else vmem
    return pl.pallas_call(
        body,
        out_shape=tuple(outs),
        in_specs=[pl.BlockSpec(memory_space=where)] * len(args),
        out_specs=tuple(vmem for _ in outs),
        scratch_shapes=[x if not isinstance(x, tuple) else pltpu.VMEM(x, F32) for x in scratch],
        input_output_aliases=aliases or {},
        compiler_params=pltpu.CompilerParams(vmem_limit_bytes=limit * 2**20),
        cost_estimate=pl.CostEstimate(flops=flops, bytes_accessed=2_000_000, transcendentals=0),
    )(*args)


def local(n_lon, n_lat, *args):
    levels, rows, lanes = args[0].shape
    wide = rows + 8

    def number(i, j):
        return (i % n_lon) * n_lat + j

    grid = [(i, j) for i in range(n_lon) for j in range(n_lat)]

    def beside(i):
        return i - 1 if i % 2 == 0 else i + 1

    cores = [(number(i, j), number(i ^ 1, j)) for i, j in grid]
    chips = [(number(i, j), number(beside(i), j)) for i, j in grid]
    lats = [(number(i, j), number(i, n_lat - 1 - j)) for i, j in grid]
    folds = [(number(i, j), number(n_lon - 1 - i, j)) for i, j in grid]
    ends = [(number(i, j), number(i, n_lat - 1 - j)) for i, j in grid if i in (0, n_lon - 1)]
    inner = [(number(i, j), number(beside(i), j)) for i, j in grid if 0 < i < n_lon - 1] + ends

    def send(x, pairs):
        return lax.ppermute(x, AXES, pairs)

    chip1, bound, top, own, *held = call(
        pack,
        [(16, lanes)] + [(2, rows, lanes)] * 2 + [(6, 2, rows, lanes)]
        + [jax.ShapeDtypeStruct(x.shape, x.dtype) for x in args],
        [pltpu.with_memory_space_constraint(x, pltpu.HBM) for x in args],
        [pltpu.SemaphoreType.DMA((len(args),))],
    )
    chip1_in = send(chip1, inner)
    core, chip = call(
        pack_columns,
        [(levels + 1, rows, lanes), (levels, rows, lanes)],
        (*held[:5], *held[6:], bound, top),
    )
    core_in = send(core, cores)
    chip_in = send(chip, chips)
    cell = (levels + 2, 40, lanes)
    inverse, onward, back, core_side, *cells = call(
        prepare, [(levels, rows, lanes)] * 3 + [(2, rows, lanes)] + [cell] * 6, (*held, core_in)
    )
    fold, lat = call(repack, [(2 * wide + 8, lanes), (2 * wide, lanes)], (top, bound, core_in, chip1_in), limit=2)
    fold_in = send(fold, folds)
    lat_in = send(lat, lats)
    adv_t, adv_s, chip_side, *_ = call(
        main,
        [(levels, rows, lanes)] * 2 + [(2, rows, lanes)] + [cell] * 6,
        (*cells, chip_in),
        [cell] * 18,
        aliases={n: 3 + n for n in range(6)},
        limit=20,
        flops=20_000_000,
    )
    strip = (2, 40, lanes)
    south_in = call(
        south,
        [(2, 2, rows, lanes)],
        (adv_t, own, core_side, chip_side, lat_in),
        [(2, wide, lanes)] + [strip] * 24,
    )[0]
    return call(
        finish,
        [(levels, rows, lanes)] * 2,
        (adv_t, adv_s, inverse, onward, back, own, core_side, chip_side, top, lat_in, fold_in, south_in),
        [(4, wide, lanes), (2, wide, lanes), (2, 2, rows, lanes)] + [(levels, rows, lanes)] * 2
        + [pltpu.SemaphoreType.DMA((4,))] + [strip] * 24,
    )


def solution(mesh):
    n_lon, n_lat = mesh.shape["lon"], mesh.shape["lat"]
    cube = P(None, "lon", "lat")
    plane = P("lon", "lat")
    return jax.shard_map(
        lambda *args: tuple(local(n_lon, n_lat, *args)),
        mesh=mesh,
        in_specs=(cube,) * 6 + (plane,) * 2,
        out_specs=(cube, cube),
        check_vma=False,
    )
```

```python
import jax
import jax.numpy as jnp
from jax import lax
from jax.experimental import pallas as pl
from jax.experimental.pallas import tpu as pltpu
from jax.sharding import PartitionSpec as P


FLUX_FLOOR = 0.01
BIG = 1e30
AXES = ("lon", "lat")
F32 = jnp.float32


SPOTS = (("t", 0, 3), ("s", 3, 3), ("u", 6, 2), ("v", 8, 3), ("w", 11, 2), ("m", 13, 3))
OWN = 12
UNROLL = (8, 8, 8)


def roll(x, shift, axis):
    if not isinstance(shift, int):
        return pltpu.roll(x, shift, axis)
    shift = shift % x.shape[axis]
    return x if shift == 0 else pltpu.roll(x, shift, axis)


def position():
    return lax.axis_index("lon"), lax.axis_index("lat")


def by_parity(body):
    even = lax.rem(lax.axis_index("lon"), 2) == 0

    @pl.when(even)
    def _():
        body(True)

    @pl.when(jnp.logical_not(even))
    def _():
        body(False)


def lanes_of(rows, lanes):
    lane = lax.broadcasted_iota(jnp.int32, (rows, lanes), 1)
    return lane, lane >> 4, lane & 15


def wet_of(flag, depth, level):
    return jnp.where((level < depth) & (flag > 0), 1.0, 0.0).astype(F32)


def pack(
    t_any, s_any, u_any, v_any, w_any, dc_any, flag_any, depth_any,
    chip1, bound, top, own, t, s, u, v, w, dc, flag, depth, sems,
):
    sources = (flag_any, depth_any, t_any, s_any, u_any, v_any, w_any, dc_any)
    targets = (flag, depth, t, s, u, v, w, dc)
    copies = [pltpu.make_async_copy(x, y, sems.at[n]) for n, (x, y) in enumerate(zip(sources, targets))]
    for copy in copies:
        copy.start()
    levels, rows, lanes = t.shape
    _, j = position()
    _, group, spot = lanes_of(rows, lanes)
    zero = jnp.zeros((rows, lanes), F32)
    chip1[...] = jnp.zeros(chip1.shape, F32)
    for copy in copies[:2]:
        copy.wait()
    flags, depths = flag[...], depth[...]
    fields = dict(t=t, s=s, u=u, v=v, w=w)
    held = {}
    for n, name in ((5, "m"), (0, "t"), (1, "s"), (2, "u"), (3, "v"), (4, "w")):
        if name != "m":
            copies[2 + n].wait()
        for parity in range(2):
            out = zero
            for g in range(levels // 2):
                k = 2 * g + parity
                if name == "w" and k == levels - 1:
                    continue
                x = wet_of(flags, depths, k) if name == "m" else fields[name][k]
                out = jnp.where(group == g, roll(x, 16 * g + 6, 1), out)
            own[n, parity] = out
            held[name, parity] = out
    edges = []
    for parity in range(2):
        up, down, across = zero, zero, zero
        for name, start, count in SPOTS:
            x = held[name, parity]
            mine = (spot >= start) & (spot < start + count)
            up = jnp.where(mine, roll(x, start - (6 - count), 1), up)
            down = jnp.where(mine, roll(x, start - 6, 1), down)
            x = -x if name in ("u", "v") else x
            for d in range(count):
                at = (4, 3, 5)[d] if name == "v" else 5 - d
                across = jnp.where(spot == start + d, roll(x, start + d - at, 1), across)
        top[parity] = across
        bound[parity] = jnp.where(j == 0, up, down)
        edges.append(across)
    edges += [bound[0], bound[1]]

    def fill(even):
        a = 0 if even else rows - 3
        for n, x in enumerate(edges):
            chip1[3 * n : 3 * n + 3] = x[a : a + 3]

    by_parity(fill)
    copies[7].wait()


def pack_columns(t, s, u, v, w, flag, depth, bound, top, core, chip):
    levels, rows, lanes = t.shape
    flags, depths = flag[...], depth[...]
    core[levels] = jnp.zeros((rows, lanes), F32)

    def sides(out, east):
        a, c = (rows - 3, rows - 2) if east else (0, 0)
        for k in range(levels):
            out[k, 0:3] = t[k, a : a + 3]
            out[k, 3:6] = s[k, a : a + 3]
            out[k, 6:9] = u[k, a : a + 3]
            out[k, 9:11] = v[k, c : c + 2]
            if k < levels - 1:
                out[k, 11:13] = w[k, c : c + 2]
            else:
                out[k, 11:13] = jnp.zeros((2, lanes), F32)
            out[k, 13:16] = wet_of(flags, depths, k)[a : a + 3]

    def fill(even):
        sides(core, even)
        sides(chip, not even)
        a = rows - 3 if even else 0
        for n, x in enumerate((top, bound)):
            for parity in range(2):
                at = 6 * n + 3 * parity
                core[levels, at : at + 3] = x[parity, a : a + 3]

    by_parity(fill)


def repack(top, bound, core, chip1, fold, lat):
    levels = core.shape[0] - 1
    rows, _ = top.shape[1:]
    wide = rows + 8
    fold[...] = jnp.zeros(fold.shape, F32)
    lat[...] = jnp.zeros(lat.shape, F32)
    for parity in range(2):
        fold[wide * parity + 4 : wide * parity + 4 + rows] = top[parity]
        lat[wide * parity + 4 : wide * parity + 4 + rows] = bound[parity]
    fold[2 * wide : 2 * wide + 6] = chip1[6:12]

    def fill(even):
        for n, out in enumerate((fold, lat)):
            for parity in range(2):
                part = 6 * n + 3 * parity
                near, far = core[levels, part : part + 3], chip1[part : part + 3]
                east, west = (near, far) if even else (far, near)
                at = wide * parity
                out[at + 1 : at + 4] = west
                out[at + rows + 4 : at + rows + 7] = east

    by_parity(fill)


def columns(src, east, cells, levels, rows):
    ct, cs, cu, cv, cw, cm = cells
    a = OWN + rows if east else OWN - 3
    b = OWN + rows if east else OWN - 2
    for k in range(levels):
        ct[k + 1, a : a + 3] = src[k, 0:3]
        cs[k + 1, a : a + 3] = src[k, 3:6]
        cu[k + 1, a : a + 3] = src[k, 6:9]
        cv[k + 1, b : b + 2] = src[k, 9:11]
        cw[k + 1, b : b + 2] = src[k, 11:13]
        cm[k + 1, a : a + 3] = src[k, 13:16]


def at_strips(src, out, levels, rows, lanes):
    _, group, _ = lanes_of(rows, lanes)
    for parity in range(2):
        x = jnp.zeros((rows, lanes), F32)
        for g in range(levels // 2):
            x = jnp.where(group == g, roll(src[2 * g + parity], 16 * g + 6, 1), x)
        out[parity] = x


def prepare(t, s, u, v, w, dc, flag, depth, core, inverse, onward, back, core_side, ct, cs, cu, cv, cw, cm):
    levels, rows, lanes = t.shape
    flags, depths = flag[...], depth[...]
    zero = jnp.zeros(flags.shape, F32)
    q = [zero]
    for k in range(1, levels):
        q.append(dc[k - 1] * wet_of(flags, depths, k))
    q.append(zero)
    ratio = zero
    for k in range(levels):
        denom = 1.0 + q[k] + q[k + 1] - q[k] * ratio
        inv = 1.0 / denom
        ratio = q[k + 1] * inv
        inverse[k] = inv
        onward[k] = q[k] * inv
        back[k] = ratio
    for ref in (ct, cs, cu, cv, cw, cm):
        for k in (0, levels + 1):
            ref[k] = jnp.zeros(ref.shape[1:], F32)
    for k in range(levels):
        ct[k + 1, OWN : OWN + rows] = t[k]
        cs[k + 1, OWN : OWN + rows] = s[k]
        cu[k + 1, OWN : OWN + rows] = u[k]
        cv[k + 1, OWN : OWN + rows] = v[k]
        cw[k + 1, OWN : OWN + rows] = w[k] if k < levels - 1 else zero
        cm[k + 1, OWN : OWN + rows] = wet_of(flags, depths, k)
    at_strips(core, core_side, levels, rows, lanes)
    by_parity(lambda even: columns(core, even, (ct, cs, cu, cv, cw, cm), levels, rows))


def low_and_anti(speed):
    parts = jnp.maximum(speed, 0.0), jnp.minimum(speed, 0.0), 0.5 * jnp.abs(speed)
    return lambda a, b: (parts[0] * a + parts[1] * b, parts[2] * (b - a))


def limited(anti, rise_a, drop_a, rise_b, drop_b):
    return anti * jnp.where(anti >= 0.0, jnp.minimum(rise_b, drop_a), jnp.minimum(rise_a, drop_b))


def ratios(lowered, top_value, low_value, inward, outward):
    (a, b, c), (x, y, z) = inward, outward
    gain = (jnp.maximum(a, 0.0) + jnp.maximum(b, 0.0) + jnp.maximum(c, 0.0)) - (
        jnp.minimum(x, 0.0) + jnp.minimum(y, 0.0) + jnp.minimum(z, 0.0)
    )
    loss = gain + ((x - a) + (y - b) + (z - c))
    rise = jnp.minimum(1.0, (top_value - lowered) / jnp.maximum(gain, FLUX_FLOOR))
    drop = jnp.minimum(1.0, (lowered - low_value) / jnp.maximum(loss, FLUX_FLOOR))
    return rise, drop


def main(
    ct_in, cs_in, cu_in, cv_in, cw_in, cm_in, chip,
    adv_t, adv_s, chip_side, ct, cs, cu, cv, cw, cm,
    low_t, low_s, ae_t, ae_s, an_t, an_s, au_t, au_s, hi_t, hi_s, lo_t, lo_s, up_t, up_s, dn_t, dn_s, fe_t, fe_s,
):
    levels, rows, lanes = adv_t.shape
    wide = rows + 8
    here, to_east, to_west = pl.ds(8, wide), pl.ds(9, wide), pl.ds(7, wide)
    inner = pl.ds(OWN, rows)

    by_parity(lambda even: columns(chip, not even, (ct, cs, cu, cv, cw, cm), levels, rows))

    tracers = (
        (ct, low_t, ae_t, an_t, au_t, hi_t, lo_t, up_t, dn_t, fe_t, adv_t),
        (cs, low_s, ae_s, an_s, au_s, hi_s, lo_s, up_s, dn_s, fe_s, adv_s),
    )
    nothing = jnp.zeros((wide, lanes), F32)
    for _, low, ae, an, au, hi, lo, rise, drop, _, _ in tracers:
        au[0, here] = nothing
        for k in (0, levels + 1):
            hi[k, here] = nothing - BIG
            lo[k, here] = nothing + BIG
            rise[k, here] = nothing
            drop[k, here] = nothing

    def first_pass(k, carry):
        wet = cm[k, here]
        east = low_and_anti(cu[k, here] * (wet * cm[k, to_east]))
        north = low_and_anti(cv[k, here] * (wet * roll(wet, -1, 1)))
        upward = low_and_anti(cw[k, here] * (wet * cm[k + 1, here]))
        fluxes = []
        for n, (c, low, ae, an, au, hi, lo, _, _, face, _) in enumerate(tracers):
            x = c[k, here]
            fe, ae[k, here] = east(x, c[k, to_east])
            fn, an[k, here] = north(x, roll(x, -1, 1))
            fu, au[k, here] = upward(c[k + 1, here], x)
            face[k, here] = fe
            fluxes.append(fu)
            lowered = x - ((fe - face[k, to_west]) + (fn - roll(fn, 1, 1)) + (carry[n] - fu))
            low[k, here] = lowered
            dry = wet == 0.0
            hi[k, here] = jnp.where(dry, -BIG, jnp.maximum(x, lowered))
            lo[k, here] = jnp.where(dry, BIG, jnp.minimum(x, lowered))
        return tuple(fluxes)

    lax.fori_loop(1, levels + 1, first_pass, (nothing, nothing), unroll=UNROLL[0])

    def second_pass(k, carry):
        for _, low, ae, an, au, hi, lo, rise, drop, _, _ in tracers:
            top_value, low_value = hi[k, here], lo[k, here]
            for x in (hi[k, to_east], hi[k, to_west], roll(top_value, -1, 1), roll(top_value, 1, 1),
                      hi[k + 1, here], hi[k - 1, here]):
                top_value = jnp.maximum(top_value, x)
            for x in (lo[k, to_east], lo[k, to_west], roll(low_value, -1, 1), roll(low_value, 1, 1),
                      lo[k + 1, here], lo[k - 1, here]):
                low_value = jnp.minimum(low_value, x)
            anti_n = an[k, here]
            rise[k, here], drop[k, here] = ratios(
                low[k, here], top_value, low_value,
                (ae[k, to_west], roll(anti_n, 1, 1), au[k, here]), (ae[k, here], anti_n, au[k - 1, here]),
            )
        return carry

    lax.fori_loop(1, levels + 1, second_pass, 0, unroll=UNROLL[1])

    def third_pass(k, carry):
        fluxes = []
        for n, (_, low, ae, an, au, _, _, rise, drop, face, adv) in enumerate(tracers):
            r, d = rise[k, here], drop[k, here]
            fe = limited(ae[k, here], r, d, rise[k, to_east], drop[k, to_east])
            face[k, here] = fe
            r, d = rise[k, inner], drop[k, inner]
            fn = limited(an[k, inner], r, d, roll(r, -1, 1), roll(d, -1, 1))
            fu = limited(au[k, inner], rise[k + 1, inner], drop[k + 1, inner], r, d)
            fluxes.append(fu)
            out = (face[k, inner] - face[k, pl.ds(OWN - 1, rows)]) + (fn - roll(fn, 1, 1)) + (carry[n] - fu)
            adv[k - 1] = low[k, inner] - out
        return tuple(fluxes)

    no_flux = jnp.zeros((rows, lanes), F32)
    lax.fori_loop(1, levels + 1, third_pass, (no_flux, no_flux), unroll=UNROLL[2])

    at_strips(chip, chip_side, levels, rows, lanes)


def strip_advection(scratch, levels, rows, lanes):
    (ct, cs, cu, cv, cw, cm, low_t, low_s, ae_t, ae_s, an_t, an_s, au_t, au_s, hi_t, hi_s, lo_t, lo_s,
     up_t, up_s, dn_t, dn_s, fe_t, fe_s) = scratch
    wide = rows + 8
    _, group, _ = lanes_of(wide, lanes)
    here, to_east, to_west = pl.ds(8, wide), pl.ds(9, wide), pl.ds(7, wide)
    lowest = group == levels // 2 - 1
    highest = group == 0

    def below(ref, k, edge_value=None):
        if k % 2 == 0:
            return ref[k + 1, here]
        x = roll(ref[k - 1, here], -16, 1)
        return x if edge_value is None else jnp.where(lowest, edge_value, x)

    def above(ref, k, edge_value):
        if k % 2 == 1:
            return ref[k - 1, here]
        return jnp.where(highest, edge_value, roll(ref[k + 1, here], 16, 1))

    tracers = (
        (ct, low_t, ae_t, an_t, au_t, hi_t, lo_t, up_t, dn_t, fe_t),
        (cs, low_s, ae_s, an_s, au_s, hi_s, lo_s, up_s, dn_s, fe_s),
    )
    ends = (0, 1)
    tops = [[None, None], [None, None]]
    for k in ends:
        wet = cm[k, here]
        east = low_and_anti(cu[k, here] * (wet * cm[k, to_east]))
        north = low_and_anti(cv[k, here] * (wet * roll(wet, -1, 1)))
        upward = low_and_anti(cw[k, here] * (wet * below(cm, k, 0.0)))
        for n, (c, low, ae, an, au, hi, lo, _, _, face) in enumerate(tracers):
            x = c[k, here]
            fe, ae[k, here] = east(x, c[k, to_east])
            fn, an[k, here] = north(x, roll(x, -1, 1))
            fu, au[k, here] = upward(below(c, k), x)
            face[k, here] = fe
            tops[n][k % 2] = fu
            low[k, here] = x - ((fe - face[k, to_west]) + (fn - roll(fn, 1, 1)) - fu)
    for k in ends:
        dry = cm[k, here] == 0.0
        for n, (c, low, ae, an, au, hi, lo, _, _, _) in enumerate(tracers):
            over = tops[n][0] if k % 2 == 1 else jnp.where(highest, 0.0, roll(tops[n][1], 16, 1))
            x, lowered = c[k, here], low[k, here] - over
            low[k, here] = lowered
            hi[k, here] = jnp.where(dry, -BIG, jnp.maximum(x, lowered))
            lo[k, here] = jnp.where(dry, BIG, jnp.minimum(x, lowered))
    for k in ends:
        for _, low, ae, an, au, hi, lo, rise, drop, _ in tracers:
            top_value, low_value = hi[k, here], lo[k, here]
            for x in (hi[k, to_east], hi[k, to_west], roll(top_value, -1, 1), roll(top_value, 1, 1),
                      below(hi, k, -BIG), above(hi, k, -BIG)):
                top_value = jnp.maximum(top_value, x)
            for x in (lo[k, to_east], lo[k, to_west], roll(low_value, -1, 1), roll(low_value, 1, 1),
                      below(lo, k, BIG), above(lo, k, BIG)):
                low_value = jnp.minimum(low_value, x)
            anti_n = an[k, here]
            rise[k, here], drop[k, here] = ratios(
                low[k, here], top_value, low_value,
                (ae[k, to_west], roll(anti_n, 1, 1), au[k, here]), (ae[k, here], anti_n, above(au, k, 0.0)),
            )
    for k in ends:
        for _, low, ae, an, au, hi, _, rise, drop, face in tracers:
            r, d = rise[k, here], drop[k, here]
            face[k, here] = limited(ae[k, here], r, d, rise[k, to_east], drop[k, to_east])
            hi[k, here] = limited(au[k, here], below(rise, k), below(drop, k), r, d)
    for k in ends:
        for _, low, ae, an, au, hi, lo, rise, drop, face in tracers:
            r, d = rise[k, here], drop[k, here]
            fn = limited(an[k, here], r, d, roll(r, -1, 1), roll(d, -1, 1))
            out = (face[k, here] - face[k, to_west]) + (fn - roll(fn, 1, 1))
            lo[k, here] = low[k, here] - (out + (above(hi, k, 0.0) - hi[k, here]))


def strip_cells(cells, own, core_side, chip_side):
    rows = own.shape[2]
    for n, ref in enumerate(cells):
        for parity in range(2):
            ref[parity, OWN : OWN + rows] = own[n, parity]

    def fill(even):
        for side, east in ((core_side, even), (chip_side, not even)):
            for ref, start, count in zip(cells, (0, 3, 6, 9, 11, 13), (3, 3, 3, 2, 2, 3)):
                a = OWN + rows if east else OWN - count
                for parity in range(2):
                    ref[parity, a : a + count] = side[parity, start : start + count]

    by_parity(fill)


def south_strip(scratch, both, edge, levels, out):
    rows, lanes = out.shape[2:]
    wide = rows + 8
    _, _, spot = lanes_of(wide, lanes)
    _, j = position()
    here = pl.ds(8, wide)
    for parity in range(2):
        for ref, mine, (name, start, count) in zip(scratch, both, SPOTS):
            value = jnp.where(spot < 6, roll(edge[parity], 6 - count - start, 1), mine[parity, here])
            if name == "m":
                value = jnp.where((spot < 3) | (spot > 11) | ((spot < 6) & (j == 0)), 0.0, value)
            ref[parity, here] = value
    strip_advection(scratch, levels, rows, lanes)
    for n in range(2):
        for parity in range(2):
            out[n, parity] = scratch[16 + n][parity, OWN : OWN + rows]


def south(adv_t, own, core_side, chip_side, lat, out, *rest):
    levels, rows, _ = adv_t.shape
    both, edge, scratch = rest[:6], rest[6], rest[7:]
    strip_cells(both, own, core_side, chip_side)
    for parity in range(2):
        edge[parity] = lat[(rows + 8) * parity : (rows + 8) * (parity + 1)]
    south_strip(scratch, both, edge, levels, out)


def finish(
    adv_t, adv_s, inverse, onward, back, top, lat, fold, south_in, bt, bs, bu, bv, bw, bm,
    out_t, out_s, edge, mirror, south_end, new_t, new_s, sems, *scratch,
):
    i, j = position()
    n_lon, n_lat = lax.axis_size("lon"), lax.axis_size("lat")
    first, last, is_top = i == 0, i == n_lon - 1, j == n_lat - 1
    levels, rows, lanes = adv_t.shape
    wide = rows + 8
    _, _, spot = lanes_of(wide, lanes)
    here = pl.ds(8, wide)
    both = (bt, bs, bu, bv, bw, bm)

    for parity in range(2):
        edge[parity] = lat[wide * parity : wide * parity + wide]
        edge[2 + parity] = fold[wide * parity : wide * parity + wide]
    south_end[...] = south_in[...]

    @pl.when(first)
    def _():
        for parity in range(2):
            edge[parity, 1:4] = fold[2 * wide + 3 * parity : 2 * wide + 3 * parity + 3]
            edge[2 + parity, rows + 4 : rows + 7] = top[parity, 0:3]

    @pl.when(last)
    def _():
        for parity in range(2):
            edge[parity, rows + 4 : rows + 7] = fold[2 * wide + 3 * parity : 2 * wide + 3 * parity + 3]
            edge[2 + parity, 1:4] = top[parity, rows - 3 : rows]

    @pl.when((first | last) & (j > 0))
    def _():
        south_strip(scratch, both, edge, levels, south_end)

    for parity in range(2):
        for r in range(wide):
            q = wide - 1 - r
            mirror[parity, r : r + 1] = edge[2 + parity, q : q + 1]

    _, u_start, u_count = SPOTS[2]
    for parity in range(2):
        other, mir = edge[parity], mirror[parity]
        mir = jnp.where((spot >= u_start) & (spot < u_start + u_count), roll(mir, -1, 0), mir)
        source = jnp.where(is_top, mir, other)
        for ref, held, (name, start, count) in zip(scratch, both, SPOTS):
            mine = held[parity, here]
            value = jnp.where(spot < 6, mine, roll(source, 6 - start, 1))
            if name == "v":
                folded = 0.5 * (mine + roll(source, 5 - (start + 2), 1))
                value = jnp.where((spot == 5) & is_top, folded, value)
            if name == "m":
                value = jnp.where(spot > 8, 0.0, value)
            ref[parity, here] = value
    strip_advection(scratch, levels, rows, lanes)

    _, _, place = lanes_of(rows, lanes)
    ends = [
        [jnp.where(place < 6, scratch[16 + n][parity, OWN : OWN + rows], south_end[n, parity]) for parity in range(2)]
        for n in range(2)
    ]
    lane, _, _ = lanes_of(rows, lanes)
    outer = (lane < 3) | (lane >= lanes - 3)
    solved = [None, None]
    for k in range(levels):
        for n, (adv, out) in enumerate(((adv_t, new_t), (adv_s, new_s))):
            x = jnp.where(outer, roll(ends[n][k % 2], -(16 * (k // 2) + 6), 1), adv[k]) * inverse[k]
            solved[n] = x if k == 0 else x + onward[k] * solved[n]
            out[k] = solved[n]
    half = levels // 2
    copies = []

    def leave(start):
        for held, out in ((new_t, out_t), (new_s, out_s)):
            part = pl.ds(start, half)
            copies.append(pltpu.make_async_copy(held.at[part], out.at[part], sems.at[len(copies)]))
            copies[-1].start()

    for k in range(levels - 2, -1, -1):
        for n, out in enumerate((new_t, new_s)):
            solved[n] = out[k] + back[k] * solved[n]
            out[k] = solved[n]
        if k == half:
            leave(half)
    leave(0)
    for copy in copies:
        copy.wait()


def call(body, outs, args, scratch=(), aliases=None, limit=8, flops=2_000_000):
    vmem = pl.BlockSpec(memory_space=pltpu.VMEM)
    outs = [x if hasattr(x, "dtype") else jax.ShapeDtypeStruct(x, F32) for x in outs]
    where = pltpu.HBM if body is pack else pltpu.VMEM
    vmem = pl.BlockSpec(memory_space=pltpu.HBM) if body is finish else vmem
    return pl.pallas_call(
        body,
        out_shape=tuple(outs),
        in_specs=[pl.BlockSpec(memory_space=where)] * len(args),
        out_specs=tuple(vmem for _ in outs),
        scratch_shapes=[x if not isinstance(x, tuple) else pltpu.VMEM(x, F32) for x in scratch],
        input_output_aliases=aliases or {},
        compiler_params=pltpu.CompilerParams(vmem_limit_bytes=limit * 2**20),
        cost_estimate=pl.CostEstimate(flops=flops, bytes_accessed=2_000_000, transcendentals=0),
    )(*args)


def local(n_lon, n_lat, *args):
    levels, rows, lanes = args[0].shape
    wide = rows + 8

    def number(i, j):
        return (i % n_lon) * n_lat + j

    grid = [(i, j) for i in range(n_lon) for j in range(n_lat)]

    def beside(i):
        return i - 1 if i % 2 == 0 else i + 1

    cores = [(number(i, j), number(i ^ 1, j)) for i, j in grid]
    chips = [(number(i, j), number(beside(i), j)) for i, j in grid]
    lats = [(number(i, j), number(i, n_lat - 1 - j)) for i, j in grid]
    folds = [(number(i, j), number(n_lon - 1 - i, j)) for i, j in grid]
    ends = [(number(i, j), number(i, n_lat - 1 - j)) for i, j in grid if i in (0, n_lon - 1)]
    inner = [(number(i, j), number(beside(i), j)) for i, j in grid if 0 < i < n_lon - 1] + ends

    def send(x, pairs):
        return lax.ppermute(x, AXES, pairs)

    chip1, bound, top, own, *held = call(
        pack,
        [(16, lanes)] + [(2, rows, lanes)] * 2 + [(6, 2, rows, lanes)]
        + [jax.ShapeDtypeStruct(x.shape, x.dtype) for x in args],
        [pltpu.with_memory_space_constraint(x, pltpu.HBM) for x in args],
        [pltpu.SemaphoreType.DMA((len(args),))],
    )
    chip1_in = send(chip1, inner)
    core, chip = call(
        pack_columns,
        [(levels + 1, rows, lanes), (levels, rows, lanes)],
        (*held[:5], *held[6:], bound, top),
    )
    core_in = send(core, cores)
    chip_in = send(chip, chips)
    cell = (levels + 2, 40, lanes)
    inverse, onward, back, core_side, *cells = call(
        prepare, [(levels, rows, lanes)] * 3 + [(2, rows, lanes)] + [cell] * 6, (*held, core_in)
    )
    fold, lat = call(repack, [(2 * wide + 8, lanes), (2 * wide, lanes)], (top, bound, core_in, chip1_in), limit=2)
    fold_in = send(fold, folds)
    lat_in = send(lat, lats)
    adv_t, adv_s, chip_side, *_ = call(
        main,
        [(levels, rows, lanes)] * 2 + [(2, rows, lanes)] + [cell] * 6,
        (*cells, chip_in),
        [cell] * 18,
        aliases={n: 3 + n for n in range(6)},
        limit=20,
        flops=20_000_000,
    )
    strip = (2, 40, lanes)
    south_in, *both = call(
        south,
        [(2, 2, rows, lanes)] + [strip] * 6,
        (adv_t, own, core_side, chip_side, lat_in),
        [(2, wide, lanes)] + [strip] * 24,
    )
    return call(
        finish,
        [(levels, rows, lanes)] * 2,
        (adv_t, adv_s, inverse, onward, back, top, lat_in, fold_in, south_in, *both),
        [(4, wide, lanes), (2, wide, lanes), (2, 2, rows, lanes)] + [(levels, rows, lanes)] * 2
        + [pltpu.SemaphoreType.DMA((4,))] + [strip] * 24,
    )


def solution(mesh):
    n_lon, n_lat = mesh.shape["lon"], mesh.shape["lat"]
    cube = P(None, "lon", "lat")
    plane = P("lon", "lat")
    return jax.shard_map(
        lambda *args: tuple(local(n_lon, n_lat, *args)),
        mesh=mesh,
        in_specs=(cube,) * 6 + (plane,) * 2,
        out_specs=(cube, cube),
        check_vma=False,
    )
```

```python
import jax
import jax.numpy as jnp
from jax import lax
from jax.experimental import pallas as pl
from jax.experimental.pallas import tpu as pltpu
from jax.sharding import PartitionSpec as P


FLUX_FLOOR = 0.01
BIG = 1e30
AXES = ("lon", "lat")
F32 = jnp.float32


SPOTS = (("t", 0, 3), ("s", 3, 3), ("u", 6, 2), ("v", 8, 3), ("w", 11, 2), ("m", 13, 3))
OWN = 12
UNROLL = (8, 8, 8)


def roll(x, shift, axis):
    if not isinstance(shift, int):
        return pltpu.roll(x, shift, axis)
    shift = shift % x.shape[axis]
    return x if shift == 0 else pltpu.roll(x, shift, axis)


def position():
    return lax.axis_index("lon"), lax.axis_index("lat")


def by_parity(body):
    even = lax.rem(lax.axis_index("lon"), 2) == 0

    @pl.when(even)
    def _():
        body(True)

    @pl.when(jnp.logical_not(even))
    def _():
        body(False)


def lanes_of(rows, lanes):
    lane = lax.broadcasted_iota(jnp.int32, (rows, lanes), 1)
    return lane, lane >> 4, lane & 15


def wet_of(flag, depth, level):
    return jnp.where((level < depth) & (flag > 0), 1.0, 0.0).astype(F32)


def pack(
    t_any, s_any, u_any, v_any, w_any, dc_any, flag_any, depth_any,
    chip1, bound, top, own, t, s, u, v, w, dc, flag, depth, sems,
):
    sources = (flag_any, depth_any, t_any, s_any, u_any, v_any, w_any, dc_any)
    targets = (flag, depth, t, s, u, v, w, dc)
    copies = [pltpu.make_async_copy(x, y, sems.at[n]) for n, (x, y) in enumerate(zip(sources, targets))]
    for copy in copies:
        copy.start()
    levels, rows, lanes = t.shape
    _, j = position()
    _, group, spot = lanes_of(rows, lanes)
    zero = jnp.zeros((rows, lanes), F32)
    chip1[...] = jnp.zeros(chip1.shape, F32)
    for copy in copies[:2]:
        copy.wait()
    flags, depths = flag[...], depth[...]
    fields = dict(t=t, s=s, u=u, v=v, w=w)
    held = {}
    for n, name in ((5, "m"), (0, "t"), (1, "s"), (2, "u"), (3, "v"), (4, "w")):
        if name != "m":
            copies[2 + n].wait()
        for parity in range(2):
            out = zero
            for g in range(levels // 2):
                k = 2 * g + parity
                if name == "w" and k == levels - 1:
                    continue
                x = wet_of(flags, depths, k) if name == "m" else fields[name][k]
                out = jnp.where(group == g, roll(x, 16 * g + 6, 1), out)
            own[n, parity] = out
            held[name, parity] = out
    edges = []
    for parity in range(2):
        up, down, across = zero, zero, zero
        for name, start, count in SPOTS:
            x = held[name, parity]
            mine = (spot >= start) & (spot < start + count)
            up = jnp.where(mine, roll(x, start - (6 - count), 1), up)
            down = jnp.where(mine, roll(x, start - 6, 1), down)
            x = -x if name in ("u", "v") else x
            for d in range(count):
                at = (4, 3, 5)[d] if name == "v" else 5 - d
                across = jnp.where(spot == start + d, roll(x, start + d - at, 1), across)
        top[parity] = across
        bound[parity] = jnp.where(j == 0, up, down)
        edges.append(across)
    edges += [bound[0], bound[1]]

    def fill(even):
        a = 0 if even else rows - 3
        for n, x in enumerate(edges):
            chip1[3 * n : 3 * n + 3] = x[a : a + 3]

    by_parity(fill)
    copies[7].wait()


def pack_columns(t, s, u, v, w, flag, depth, bound, top, core, chip):
    levels, rows, lanes = t.shape
    flags, depths = flag[...], depth[...]
    core[levels] = jnp.zeros((rows, lanes), F32)

    def sides(out, east):
        a, c = (rows - 3, rows - 2) if east else (0, 0)
        for k in range(levels):
            out[k, 0:3] = t[k, a : a + 3]
            out[k, 3:6] = s[k, a : a + 3]
            out[k, 6:9] = u[k, a : a + 3]
            out[k, 9:11] = v[k, c : c + 2]
            if k < levels - 1:
                out[k, 11:13] = w[k, c : c + 2]
            else:
                out[k, 11:13] = jnp.zeros((2, lanes), F32)
            out[k, 13:16] = wet_of(flags, depths, k)[a : a + 3]

    def fill(even):
        sides(core, even)
        sides(chip, not even)
        a = rows - 3 if even else 0
        for n, x in enumerate((top, bound)):
            for parity in range(2):
                at = 6 * n + 3 * parity
                core[levels, at : at + 3] = x[parity, a : a + 3]

    by_parity(fill)


def repack(top, bound, core, chip1, fold, lat):
    levels = core.shape[0] - 1
    rows, _ = top.shape[1:]
    wide = rows + 8
    fold[...] = jnp.zeros(fold.shape, F32)
    lat[...] = jnp.zeros(lat.shape, F32)
    for parity in range(2):
        fold[wide * parity + 4 : wide * parity + 4 + rows] = top[parity]
        lat[wide * parity + 4 : wide * parity + 4 + rows] = bound[parity]
    fold[2 * wide : 2 * wide + 6] = chip1[6:12]

    def fill(even):
        for n, out in enumerate((fold, lat)):
            for parity in range(2):
                part = 6 * n + 3 * parity
                near, far = core[levels, part : part + 3], chip1[part : part + 3]
                east, west = (near, far) if even else (far, near)
                at = wide * parity
                out[at + 1 : at + 4] = west
                out[at + rows + 4 : at + rows + 7] = east

    by_parity(fill)


def columns(src, east, cells, levels, rows):
    ct, cs, cu, cv, cw, cm = cells
    a = OWN + rows if east else OWN - 3
    b = OWN + rows if east else OWN - 2
    for k in range(levels):
        ct[k + 1, a : a + 3] = src[k, 0:3]
        cs[k + 1, a : a + 3] = src[k, 3:6]
        cu[k + 1, a : a + 3] = src[k, 6:9]
        cv[k + 1, b : b + 2] = src[k, 9:11]
        cw[k + 1, b : b + 2] = src[k, 11:13]
        cm[k + 1, a : a + 3] = src[k, 13:16]


def at_strips(src, out, levels, rows, lanes):
    _, group, _ = lanes_of(rows, lanes)
    for parity in range(2):
        x = jnp.zeros((rows, lanes), F32)
        for g in range(levels // 2):
            x = jnp.where(group == g, roll(src[2 * g + parity], 16 * g + 6, 1), x)
        out[parity] = x


def prepare(t, s, u, v, w, dc, flag, depth, core, inverse, onward, back, ct, cs, cu, cv, cw, cm):
    levels, rows, _ = t.shape
    flags, depths = flag[...], depth[...]
    zero = jnp.zeros(flags.shape, F32)
    q = [zero]
    for k in range(1, levels):
        q.append(dc[k - 1] * wet_of(flags, depths, k))
    q.append(zero)
    ratio = zero
    for k in range(levels):
        denom = 1.0 + q[k] + q[k + 1] - q[k] * ratio
        inv = 1.0 / denom
        ratio = q[k + 1] * inv
        inverse[k] = inv
        onward[k] = q[k] * inv
        back[k] = ratio
    for ref in (ct, cs, cu, cv, cw, cm):
        for k in (0, levels + 1):
            ref[k] = jnp.zeros(ref.shape[1:], F32)
    for k in range(levels):
        ct[k + 1, OWN : OWN + rows] = t[k]
        cs[k + 1, OWN : OWN + rows] = s[k]
        cu[k + 1, OWN : OWN + rows] = u[k]
        cv[k + 1, OWN : OWN + rows] = v[k]
        cw[k + 1, OWN : OWN + rows] = w[k] if k < levels - 1 else zero
        cm[k + 1, OWN : OWN + rows] = wet_of(flags, depths, k)
    by_parity(lambda even: columns(core, even, (ct, cs, cu, cv, cw, cm), levels, rows))


def low_and_anti(speed):
    parts = jnp.maximum(speed, 0.0), jnp.minimum(speed, 0.0), 0.5 * jnp.abs(speed)
    return lambda a, b: (parts[0] * a + parts[1] * b, parts[2] * (b - a))


def limited(anti, rise_a, drop_a, rise_b, drop_b):
    return anti * jnp.where(anti >= 0.0, jnp.minimum(rise_b, drop_a), jnp.minimum(rise_a, drop_b))


def ratios(lowered, top_value, low_value, inward, outward):
    (a, b, c), (x, y, z) = inward, outward
    gain = (jnp.maximum(a, 0.0) + jnp.maximum(b, 0.0) + jnp.maximum(c, 0.0)) - (
        jnp.minimum(x, 0.0) + jnp.minimum(y, 0.0) + jnp.minimum(z, 0.0)
    )
    loss = gain + ((x - a) + (y - b) + (z - c))
    rise = jnp.minimum(1.0, (top_value - lowered) / jnp.maximum(gain, FLUX_FLOOR))
    drop = jnp.minimum(1.0, (lowered - low_value) / jnp.maximum(loss, FLUX_FLOOR))
    return rise, drop


def main(
    ct_in, cs_in, cu_in, cv_in, cw_in, cm_in, chip,
    adv_t, adv_s, chip_side, ct, cs, cu, cv, cw, cm,
    low_t, low_s, ae_t, ae_s, an_t, an_s, au_t, au_s, hi_t, hi_s, lo_t, lo_s, up_t, up_s, dn_t, dn_s, fe_t, fe_s,
):
    levels, rows, lanes = adv_t.shape
    wide = rows + 8
    here, to_east, to_west = pl.ds(8, wide), pl.ds(9, wide), pl.ds(7, wide)
    inner = pl.ds(OWN, rows)

    by_parity(lambda even: columns(chip, not even, (ct, cs, cu, cv, cw, cm), levels, rows))

    tracers = (
        (ct, low_t, ae_t, an_t, au_t, hi_t, lo_t, up_t, dn_t, fe_t, adv_t),
        (cs, low_s, ae_s, an_s, au_s, hi_s, lo_s, up_s, dn_s, fe_s, adv_s),
    )
    nothing = jnp.zeros((wide, lanes), F32)
    for _, low, ae, an, au, hi, lo, rise, drop, _, _ in tracers:
        au[0, here] = nothing
        for k in (0, levels + 1):
            hi[k, here] = nothing - BIG
            lo[k, here] = nothing + BIG
            rise[k, here] = nothing
            drop[k, here] = nothing

    def first_pass(k, carry):
        wet = cm[k, here]
        east = low_and_anti(cu[k, here] * (wet * cm[k, to_east]))
        north = low_and_anti(cv[k, here] * (wet * roll(wet, -1, 1)))
        upward = low_and_anti(cw[k, here] * (wet * cm[k + 1, here]))
        fluxes = []
        for n, (c, low, ae, an, au, hi, lo, _, _, face, _) in enumerate(tracers):
            x = c[k, here]
            fe, ae[k, here] = east(x, c[k, to_east])
            fn, an[k, here] = north(x, roll(x, -1, 1))
            fu, au[k, here] = upward(c[k + 1, here], x)
            face[k, here] = fe
            fluxes.append(fu)
            lowered = x - ((fe - face[k, to_west]) + (fn - roll(fn, 1, 1)) + (carry[n] - fu))
            low[k, here] = lowered
            dry = wet == 0.0
            hi[k, here] = jnp.where(dry, -BIG, jnp.maximum(x, lowered))
            lo[k, here] = jnp.where(dry, BIG, jnp.minimum(x, lowered))
        return tuple(fluxes)

    lax.fori_loop(1, levels + 1, first_pass, (nothing, nothing), unroll=UNROLL[0])

    def second_pass(k, carry):
        for _, low, ae, an, au, hi, lo, rise, drop, _, _ in tracers:
            top_value, low_value = hi[k, here], lo[k, here]
            for x in (hi[k, to_east], hi[k, to_west], roll(top_value, -1, 1), roll(top_value, 1, 1),
                      hi[k + 1, here], hi[k - 1, here]):
                top_value = jnp.maximum(top_value, x)
            for x in (lo[k, to_east], lo[k, to_west], roll(low_value, -1, 1), roll(low_value, 1, 1),
                      lo[k + 1, here], lo[k - 1, here]):
                low_value = jnp.minimum(low_value, x)
            anti_n = an[k, here]
            rise[k, here], drop[k, here] = ratios(
                low[k, here], top_value, low_value,
                (ae[k, to_west], roll(anti_n, 1, 1), au[k, here]), (ae[k, here], anti_n, au[k - 1, here]),
            )
        return carry

    lax.fori_loop(1, levels + 1, second_pass, 0, unroll=UNROLL[1])

    def third_pass(k, carry):
        fluxes = []
        for n, (_, low, ae, an, au, _, _, rise, drop, face, adv) in enumerate(tracers):
            r, d = rise[k, here], drop[k, here]
            fe = limited(ae[k, here], r, d, rise[k, to_east], drop[k, to_east])
            face[k, here] = fe
            r, d = rise[k, inner], drop[k, inner]
            fn = limited(an[k, inner], r, d, roll(r, -1, 1), roll(d, -1, 1))
            fu = limited(au[k, inner], rise[k + 1, inner], drop[k + 1, inner], r, d)
            fluxes.append(fu)
            out = (face[k, inner] - face[k, pl.ds(OWN - 1, rows)]) + (fn - roll(fn, 1, 1)) + (carry[n] - fu)
            adv[k - 1] = low[k, inner] - out
        return tuple(fluxes)

    no_flux = jnp.zeros((rows, lanes), F32)
    lax.fori_loop(1, levels + 1, third_pass, (no_flux, no_flux), unroll=UNROLL[2])

    at_strips(chip, chip_side, levels, rows, lanes)


def strip_advection(scratch, levels, rows, lanes):
    (ct, cs, cu, cv, cw, cm, low_t, low_s, ae_t, ae_s, an_t, an_s, au_t, au_s, hi_t, hi_s, lo_t, lo_s,
     up_t, up_s, dn_t, dn_s, fe_t, fe_s) = scratch
    wide = rows + 8
    _, group, _ = lanes_of(wide, lanes)
    here, to_east, to_west = pl.ds(8, wide), pl.ds(9, wide), pl.ds(7, wide)
    lowest = group == levels // 2 - 1
    highest = group == 0

    def below(ref, k, edge_value=None):
        if k % 2 == 0:
            return ref[k + 1, here]
        x = roll(ref[k - 1, here], -16, 1)
        return x if edge_value is None else jnp.where(lowest, edge_value, x)

    def above(ref, k, edge_value):
        if k % 2 == 1:
            return ref[k - 1, here]
        return jnp.where(highest, edge_value, roll(ref[k + 1, here], 16, 1))

    tracers = (
        (ct, low_t, ae_t, an_t, au_t, hi_t, lo_t, up_t, dn_t, fe_t),
        (cs, low_s, ae_s, an_s, au_s, hi_s, lo_s, up_s, dn_s, fe_s),
    )
    ends = (0, 1)
    tops = [[None, None], [None, None]]
    for k in ends:
        wet = cm[k, here]
        east = low_and_anti(cu[k, here] * (wet * cm[k, to_east]))
        north = low_and_anti(cv[k, here] * (wet * roll(wet, -1, 1)))
        upward = low_and_anti(cw[k, here] * (wet * below(cm, k, 0.0)))
        for n, (c, low, ae, an, au, hi, lo, _, _, face) in enumerate(tracers):
            x = c[k, here]
            fe, ae[k, here] = east(x, c[k, to_east])
            fn, an[k, here] = north(x, roll(x, -1, 1))
            fu, au[k, here] = upward(below(c, k), x)
            face[k, here] = fe
            tops[n][k % 2] = fu
            low[k, here] = x - ((fe - face[k, to_west]) + (fn - roll(fn, 1, 1)) - fu)
    for k in ends:
        dry = cm[k, here] == 0.0
        for n, (c, low, ae, an, au, hi, lo, _, _, _) in enumerate(tracers):
            over = tops[n][0] if k % 2 == 1 else jnp.where(highest, 0.0, roll(tops[n][1], 16, 1))
            x, lowered = c[k, here], low[k, here] - over
            low[k, here] = lowered
            hi[k, here] = jnp.where(dry, -BIG, jnp.maximum(x, lowered))
            lo[k, here] = jnp.where(dry, BIG, jnp.minimum(x, lowered))
    for k in ends:
        for _, low, ae, an, au, hi, lo, rise, drop, _ in tracers:
            top_value, low_value = hi[k, here], lo[k, here]
            for x in (hi[k, to_east], hi[k, to_west], roll(top_value, -1, 1), roll(top_value, 1, 1),
                      below(hi, k, -BIG), above(hi, k, -BIG)):
                top_value = jnp.maximum(top_value, x)
            for x in (lo[k, to_east], lo[k, to_west], roll(low_value, -1, 1), roll(low_value, 1, 1),
                      below(lo, k, BIG), above(lo, k, BIG)):
                low_value = jnp.minimum(low_value, x)
            anti_n = an[k, here]
            rise[k, here], drop[k, here] = ratios(
                low[k, here], top_value, low_value,
                (ae[k, to_west], roll(anti_n, 1, 1), au[k, here]), (ae[k, here], anti_n, above(au, k, 0.0)),
            )
    for k in ends:
        for _, low, ae, an, au, hi, _, rise, drop, face in tracers:
            r, d = rise[k, here], drop[k, here]
            face[k, here] = limited(ae[k, here], r, d, rise[k, to_east], drop[k, to_east])
            hi[k, here] = limited(au[k, here], below(rise, k), below(drop, k), r, d)
    for k in ends:
        for _, low, ae, an, au, hi, lo, rise, drop, face in tracers:
            r, d = rise[k, here], drop[k, here]
            fn = limited(an[k, here], r, d, roll(r, -1, 1), roll(d, -1, 1))
            out = (face[k, here] - face[k, to_west]) + (fn - roll(fn, 1, 1))
            lo[k, here] = low[k, here] - (out + (above(hi, k, 0.0) - hi[k, here]))


def strip_cells(cells, own, core_side, chip_side):
    rows = own.shape[2]
    for n, ref in enumerate(cells):
        for parity in range(2):
            ref[parity, OWN : OWN + rows] = own[n, parity]

    def fill(even):
        for side, east in ((core_side, even), (chip_side, not even)):
            for ref, start, count in zip(cells, (0, 3, 6, 9, 11, 13), (3, 3, 3, 2, 2, 3)):
                a = OWN + rows if east else OWN - count
                for parity in range(2):
                    ref[parity, a : a + count] = side[parity, start : start + count]

    by_parity(fill)


def south_strip(scratch, both, edge, levels, out):
    rows, lanes = out.shape[2:]
    wide = rows + 8
    _, _, spot = lanes_of(wide, lanes)
    _, j = position()
    here = pl.ds(8, wide)
    for parity in range(2):
        for ref, mine, (name, start, count) in zip(scratch, both, SPOTS):
            value = jnp.where(spot < 6, roll(edge[parity], 6 - count - start, 1), mine[parity, here])
            if name == "m":
                value = jnp.where((spot < 3) | (spot > 11) | ((spot < 6) & (j == 0)), 0.0, value)
            ref[parity, here] = value
    strip_advection(scratch, levels, rows, lanes)
    for n in range(2):
        for parity in range(2):
            out[n, parity] = scratch[16 + n][parity, OWN : OWN + rows]


def south(adv_t, own, core, chip_side, lat, out, *rest):
    levels, rows, lanes = adv_t.shape
    both, edge, core_side, scratch = rest[:6], rest[6], rest[7], rest[8:]
    at_strips(core, core_side, levels, rows, lanes)
    strip_cells(both, own, core_side, chip_side)
    for parity in range(2):
        edge[parity] = lat[(rows + 8) * parity : (rows + 8) * (parity + 1)]
    south_strip(scratch, both, edge, levels, out)


def finish(
    adv_t, adv_s, inverse, onward, back, top, lat, fold, south_in, bt, bs, bu, bv, bw, bm,
    out_t, out_s, edge, mirror, south_end, new_t, new_s, sems, *scratch,
):
    i, j = position()
    n_lon, n_lat = lax.axis_size("lon"), lax.axis_size("lat")
    first, last, is_top = i == 0, i == n_lon - 1, j == n_lat - 1
    levels, rows, lanes = adv_t.shape
    wide = rows + 8
    _, _, spot = lanes_of(wide, lanes)
    here = pl.ds(8, wide)
    both = (bt, bs, bu, bv, bw, bm)

    for parity in range(2):
        edge[parity] = lat[wide * parity : wide * parity + wide]
        edge[2 + parity] = fold[wide * parity : wide * parity + wide]
    south_end[...] = south_in[...]

    @pl.when(first)
    def _():
        for parity in range(2):
            edge[parity, 1:4] = fold[2 * wide + 3 * parity : 2 * wide + 3 * parity + 3]
            edge[2 + parity, rows + 4 : rows + 7] = top[parity, 0:3]

    @pl.when(last)
    def _():
        for parity in range(2):
            edge[parity, rows + 4 : rows + 7] = fold[2 * wide + 3 * parity : 2 * wide + 3 * parity + 3]
            edge[2 + parity, 1:4] = top[parity, rows - 3 : rows]

    @pl.when((first | last) & (j > 0))
    def _():
        south_strip(scratch, both, edge, levels, south_end)

    for parity in range(2):
        for r in range(wide):
            q = wide - 1 - r
            mirror[parity, r : r + 1] = edge[2 + parity, q : q + 1]

    _, u_start, u_count = SPOTS[2]
    for parity in range(2):
        other, mir = edge[parity], mirror[parity]
        mir = jnp.where((spot >= u_start) & (spot < u_start + u_count), roll(mir, -1, 0), mir)
        source = jnp.where(is_top, mir, other)
        for ref, held, (name, start, count) in zip(scratch, both, SPOTS):
            mine = held[parity, here]
            value = jnp.where(spot < 6, mine, roll(source, 6 - start, 1))
            if name == "v":
                folded = 0.5 * (mine + roll(source, 5 - (start + 2), 1))
                value = jnp.where((spot == 5) & is_top, folded, value)
            if name == "m":
                value = jnp.where(spot > 8, 0.0, value)
            ref[parity, here] = value
    strip_advection(scratch, levels, rows, lanes)

    _, _, place = lanes_of(rows, lanes)
    ends = [
        [jnp.where(place < 6, scratch[16 + n][parity, OWN : OWN + rows], south_end[n, parity]) for parity in range(2)]
        for n in range(2)
    ]
    lane, _, _ = lanes_of(rows, lanes)
    outer = (lane < 3) | (lane >= lanes - 3)
    solved = [None, None]
    for k in range(levels):
        for n, (adv, out) in enumerate(((adv_t, new_t), (adv_s, new_s))):
            x = jnp.where(outer, roll(ends[n][k % 2], -(16 * (k // 2) + 6), 1), adv[k]) * inverse[k]
            solved[n] = x if k == 0 else x + onward[k] * solved[n]
            out[k] = solved[n]
    half = levels // 2
    copies = []

    def leave(start):
        for held, out in ((new_t, out_t), (new_s, out_s)):
            part = pl.ds(start, half)
            copies.append(pltpu.make_async_copy(held.at[part], out.at[part], sems.at[len(copies)]))
            copies[-1].start()

    for k in range(levels - 2, -1, -1):
        for n, out in enumerate((new_t, new_s)):
            solved[n] = out[k] + back[k] * solved[n]
            out[k] = solved[n]
        if k == half:
            leave(half)
    leave(0)
    for copy in copies:
        copy.wait()


def call(body, outs, args, scratch=(), aliases=None, limit=8, flops=2_000_000):
    vmem = pl.BlockSpec(memory_space=pltpu.VMEM)
    outs = [x if hasattr(x, "dtype") else jax.ShapeDtypeStruct(x, F32) for x in outs]
    where = pltpu.HBM if body is pack else pltpu.VMEM
    vmem = pl.BlockSpec(memory_space=pltpu.HBM) if body is finish else vmem
    return pl.pallas_call(
        body,
        out_shape=tuple(outs),
        in_specs=[pl.BlockSpec(memory_space=where)] * len(args),
        out_specs=tuple(vmem for _ in outs),
        scratch_shapes=[x if not isinstance(x, tuple) else pltpu.VMEM(x, F32) for x in scratch],
        input_output_aliases=aliases or {},
        compiler_params=pltpu.CompilerParams(vmem_limit_bytes=limit * 2**20),
        cost_estimate=pl.CostEstimate(flops=flops, bytes_accessed=2_000_000, transcendentals=0),
    )(*args)


def local(n_lon, n_lat, *args):
    levels, rows, lanes = args[0].shape
    wide = rows + 8

    def number(i, j):
        return (i % n_lon) * n_lat + j

    grid = [(i, j) for i in range(n_lon) for j in range(n_lat)]

    def beside(i):
        return i - 1 if i % 2 == 0 else i + 1

    cores = [(number(i, j), number(i ^ 1, j)) for i, j in grid]
    chips = [(number(i, j), number(beside(i), j)) for i, j in grid]
    lats = [(number(i, j), number(i, n_lat - 1 - j)) for i, j in grid]
    folds = [(number(i, j), number(n_lon - 1 - i, j)) for i, j in grid]
    ends = [(number(i, j), number(i, n_lat - 1 - j)) for i, j in grid if i in (0, n_lon - 1)]
    inner = [(number(i, j), number(beside(i), j)) for i, j in grid if 0 < i < n_lon - 1] + ends

    def send(x, pairs):
        return lax.ppermute(x, AXES, pairs)

    chip1, bound, top, own, *held = call(
        pack,
        [(16, lanes)] + [(2, rows, lanes)] * 2 + [(6, 2, rows, lanes)]
        + [jax.ShapeDtypeStruct(x.shape, x.dtype) for x in args],
        [pltpu.with_memory_space_constraint(x, pltpu.HBM) for x in args],
        [pltpu.SemaphoreType.DMA((len(args),))],
    )
    chip1_in = send(chip1, inner)
    core, chip = call(
        pack_columns,
        [(levels + 1, rows, lanes), (levels, rows, lanes)],
        (*held[:5], *held[6:], bound, top),
    )
    core_in = send(core, cores)
    chip_in = send(chip, chips)
    cell = (levels + 2, 40, lanes)
    inverse, onward, back, *cells = call(
        prepare, [(levels, rows, lanes)] * 3 + [cell] * 6, (*held, core_in)
    )
    fold, lat = call(repack, [(2 * wide + 8, lanes), (2 * wide, lanes)], (top, bound, core_in, chip1_in), limit=2)
    fold_in = send(fold, folds)
    lat_in = send(lat, lats)
    adv_t, adv_s, chip_side, *_ = call(
        main,
        [(levels, rows, lanes)] * 2 + [(2, rows, lanes)] + [cell] * 6,
        (*cells, chip_in),
        [cell] * 18,
        aliases={n: 3 + n for n in range(6)},
        limit=20,
        flops=20_000_000,
    )
    strip = (2, 40, lanes)
    south_in, *both = call(
        south,
        [(2, 2, rows, lanes)] + [strip] * 6,
        (adv_t, own, core_in, chip_side, lat_in),
        [(2, wide, lanes), (2, rows, lanes)] + [strip] * 24,
    )
    return call(
        finish,
        [(levels, rows, lanes)] * 2,
        (adv_t, adv_s, inverse, onward, back, top, lat_in, fold_in, south_in, *both),
        [(4, wide, lanes), (2, wide, lanes), (2, 2, rows, lanes)] + [(levels, rows, lanes)] * 2
        + [pltpu.SemaphoreType.DMA((4,))] + [strip] * 24,
    )


def solution(mesh):
    n_lon, n_lat = mesh.shape["lon"], mesh.shape["lat"]
    cube = P(None, "lon", "lat")
    plane = P("lon", "lat")
    return jax.shard_map(
        lambda *args: tuple(local(n_lon, n_lat, *args)),
        mesh=mesh,
        in_specs=(cube,) * 6 + (plane,) * 2,
        out_specs=(cube, cube),
        check_vma=False,
    )
```
